256 devices in a mesh: line: 16 (over z, x_lo), bus: 8 (over y, core), tm: 2 (over x_hi).
Axes of the slice: x: 4 (x_hi: 2, x_lo: 2; x = x_hi * 2 + x_lo), y: 4, z: 8, core: 2. Of those that a mesh axis runs over, the one named last changes fastest.
Arguments:
- ptdf_matrix: float32 [15360, 12288], P('line', 'bus'), may hold values from -0.0546875 to 0.0546875
- bus_load: float32 [12288, 256], P('bus', 'tm'), may hold values from 0 to 1
- unit_bus: int32 [4096], P(('line', 'bus')), may hold values from 0 to 12287, as said below
- unit_type: int32 [4096], P(('line', 'bus')), may hold values from 0 to 3
- unit_limit: int32 [4096], P(('line', 'bus')), may hold values from 50 to 499
- unit_cost: float32 [4096], P(('line', 'bus')), may hold values from 0.1 to 1
- line_rating: int32 [15360], P('line'), may hold values from 20 to 299
Outputs:
- generation: float32 [4096, 256], P(('line', 'bus'), 'tm')
- line_dual: float32 [15360, 256], P('line', 'tm')
The draws below stay inside these ranges and needn't reach their ends.
Inputs may be any that keep to these rules, and one draw needn't show every extreme that they name: `unit_bus`: let G be the number of devices of line and bus together, U = 4096 / G and S = 12288 / G. Unit u lies in group q = u // U; it sits at a bus of the S consecutive buses that begin at (q mod the size of bus) * 12288 / (size of bus) + (q // size of bus) * S.
All inputs are finite; a program needn't handle non-finite values.
Results may differ from the reference program's by a relative error of at most 0.0003.
Values sent between devices are 32-bit elements; how exact they have to be, the bound alone decides.
No kernel may reach another device: no remote copies, remote signals or barrier semaphores. Data moves between devices by JAX's collectives and lax.ppermute only.
A program may use at most 64 MiB of HBM per device.

```python
import math
import jax
import jax.numpy as jnp
from jax import lax

BUSES = 12288
LINES = 15360
UNITS = 4096
HOUR_DEV = 128
ITERS = 4
N_LINE = 16
N_BUS = 8
N_TM = 2


def draw_unit_bus(key, part):
    groups = N_LINE * N_BUS
    per_group = UNITS // groups
    sub_rows = BUSES // groups
    block_rows = BUSES // N_BUS
    owner = jnp.arange(UNITS, dtype=jnp.int32) // per_group
    line_place = owner // N_BUS
    bus_place = owner % N_BUS
    offset = jax.random.randint(key, (UNITS,), 0, sub_rows, dtype=jnp.int32)
    return (bus_place * block_rows + line_place * sub_rows + offset).astype(jnp.int32)


def draw_bus_load(key, part):
    key_profile = jax.random.fold_in(key, 11)
    key_local = jax.random.fold_in(key, 12)
    profile = jax.random.uniform(key_profile, (1, BUSES * 0 + HOUR_DEV * N_TM), jnp.float32, 0.1, 1.0)
    local = jax.random.uniform(key_local, (BUSES, HOUR_DEV * N_TM), jnp.float32, 0.3, 1.0)
    return (local * profile).astype(jnp.float32)


def place_ends(result, key, low, top_value):
    spot = [jax.random.randint(jax.random.fold_in(key, axis), (), 0, length) for axis, length in enumerate(result.shape)]
    main_axis = result.shape.index(max(result.shape))
    next_to = spot[:main_axis] + [(spot[main_axis] + 1) % result.shape[main_axis]] + spot[main_axis + 1:]
    return result.at[tuple(spot)].set(low).at[tuple(next_to)].set(top_value)


def steps_of(own_key, extent, pieces, low, largest):
    loudness, own = 1.0, jax.random.fold_in(own_key, 6)
    for position, blocks in pieces:
        steps = jnp.exp(jax.random.uniform(jax.random.fold_in(own, position), (blocks,), jnp.float32, low / len(pieces), largest / len(pieces)))
        loudness = loudness * jnp.repeat(steps, extent[position] // blocks).reshape([-1 if axis == position else 1 for axis in range(len(extent))])
    return loudness


def scatter_about(key, dims, deviation, most, shards=(), kind=jnp.bfloat16):
    level = steps_of(key, dims, shards, -0.22, 0.18) if shards else 1.0
    entries = jax.random.normal(key, dims, jnp.float32) * deviation * level
    return jnp.minimum(jnp.maximum(entries, -most), most).astype(kind)


def setup_inputs(seed: int = 0) -> dict:
    key_of = jax.random.split(jax.random.key(seed), 8)
    return {
        "ptdf_matrix": scatter_about(key_of[0], (LINES, BUSES), BUSES ** -0.5, 0.0546875, ((0, 16), (1, 8)), jnp.float32),
        "bus_load": draw_bus_load(jax.random.fold_in(key_of[7], 71), 0),
        "unit_bus": draw_unit_bus(jax.random.fold_in(key_of[7], 71), 0),
        "unit_type": place_ends(jax.random.randint(key_of[3], (UNITS,), 0, 4), jax.random.fold_in(key_of[3], 1), 0, 3).astype(jnp.int32),
        "unit_limit": place_ends(jax.random.randint(key_of[4], (UNITS,), 50, 500), jax.random.fold_in(key_of[4], 1), 50, 499).astype(jnp.int32),
        "unit_cost": jnp.clip(jnp.exp(math.log(1.0) - 2.3025851 * jax.random.uniform(key_of[5], (UNITS,), jnp.float32) ** steps_of(key_of[5], (UNITS,), ((0, 128),), -0.2, 0.2)), 0.1, 1.0),
        "line_rating": place_ends(jax.random.randint(key_of[6], (LINES,), 20, 300), jax.random.fold_in(key_of[6], 1), 20, 299).astype(jnp.int32),
    }


RAMP_RATES = (0.1, 0.2, 0.4, 0.5)
COST_FACTORS = (1.0, 1.5, 3.0, 0.05)
PRIMAL_STEP = 0.5
DUAL_STEP = 0.5


def unit_tables(unit_type, unit_limit, unit_cost):
    capacity = unit_limit.astype(jnp.float32) / 100.0
    kinds = (unit_type[:, None] == jnp.arange(4, dtype=jnp.int32)[None, :]).astype(jnp.float32)
    rates = jnp.sum(kinds * jnp.array(RAMP_RATES, jnp.float32)[None, :], axis=1)
    factors = jnp.sum(kinds * jnp.array(COST_FACTORS, jnp.float32)[None, :], axis=1)
    storage = kinds[:, 3]
    return unit_cost * factors, -capacity * storage, capacity, rates * capacity, storage, 2.0 * capacity


def reference(ptdf_matrix, bus_load, unit_bus, unit_type, unit_limit, unit_cost, line_rating):
    cost, lower_limit, upper_limit, ramp, storage, energy = unit_tables(unit_type, unit_limit, unit_cost)
    rating = (line_rating.astype(jnp.float32) / 100.0)[:, None]
    hour_count = bus_load.shape[1]
    hour_mask = (jnp.arange(hour_count) >= 1).astype(jnp.float32)[None, :]
    demand = jnp.sum(bus_load, axis=0)
    generation = jnp.zeros((UNITS, hour_count), jnp.float32)
    ramp_dual = jnp.zeros((UNITS, hour_count), jnp.float32)
    store_dual = jnp.zeros((UNITS, hour_count), jnp.float32)
    line_dual = jnp.zeros((LINES, hour_count), jnp.float32)
    balance_dual = jnp.zeros((hour_count,), jnp.float32)
    zero_column = jnp.zeros((UNITS, 1), jnp.float32)
    for iteration in range(ITERS):
        prices = jnp.dot(ptdf_matrix.T, line_dual, precision=lax.Precision.HIGHEST, preferred_element_type=jnp.float32)
        ramp_next = jnp.concatenate([ramp_dual[:, 1:], zero_column], axis=1)
        suffix = jnp.flip(jnp.cumsum(jnp.flip(store_dual, 1), axis=1), 1)
        gradient = cost[:, None] + balance_dual[None, :] + prices[unit_bus] + ramp_dual - ramp_next + storage[:, None] * suffix
        updated = jnp.clip(generation - PRIMAL_STEP * gradient, lower_limit[:, None], upper_limit[:, None])
        extrap = 2.0 * updated - generation
        injection = jax.ops.segment_sum(extrap, unit_bus, num_segments=BUSES) - bus_load
        flow = jnp.dot(ptdf_matrix, injection, precision=lax.Precision.HIGHEST, preferred_element_type=jnp.float32)
        moved = line_dual + DUAL_STEP * flow
        line_dual = moved - jnp.clip(moved, -DUAL_STEP * rating, DUAL_STEP * rating)
        balance_dual = balance_dual + (jnp.sum(extrap, axis=0) - demand) / UNITS
        previous = jnp.concatenate([zero_column, extrap[:, :-1]], axis=1)
        moved = ramp_dual + DUAL_STEP * (extrap - previous) * hour_mask
        ramp_dual = moved - jnp.clip(moved, -DUAL_STEP * ramp[:, None], DUAL_STEP * ramp[:, None])
        moved = store_dual + DUAL_STEP * storage[:, None] * jnp.cumsum(extrap, axis=1)
        store_dual = moved - jnp.clip(moved, -DUAL_STEP * energy[:, None], DUAL_STEP * energy[:, None])
        generation = updated
    return generation, line_dual
```

```python
import functools

import jax
import jax.numpy as jnp
from jax import lax
from jax.experimental import pallas as pl
from jax.experimental.pallas import tpu as pltpu
from jax.sharding import Mesh
from jax.sharding import PartitionSpec as P

UNITS = 4096
ITERS = 4
LINE = ("z", "xl")
BUS = ("y", "c")
LINE_BUS = ("z", "xl", "y", "c")
LINE_TM = ("z", "xl", "t")

RAMP_RATES = (0.1, 0.2, 0.4, 0.5)
COST_FACTORS = (1.0, 1.5, 3.0, 0.05)
PRIMAL_STEP = 0.5
DUAL_STEP = 0.5

LINES_DEV = 960
ROWS = 1024
HALF = 496
BLOCK = 256
BF16 = jnp.bfloat16
F32 = jnp.float32
VMEM = pl.BlockSpec(memory_space=pltpu.VMEM)
SMEM = pl.BlockSpec(memory_space=pltpu.SMEM)


def params(mib):
    return pltpu.CompilerParams(vmem_limit_bytes=mib << 20)


def cost_of(flops, size):
    return pl.CostEstimate(flops=flops, bytes_accessed=size, transcendentals=0)


def halves(value):
    high = value.astype(BF16)
    return high, (value - high.astype(F32)).astype(BF16)


def dot(left, right, dims=((1,), (0,))):
    return lax.dot_general(left, right, (dims, ((), ())), preferred_element_type=F32)


def row_index(shape, first):
    return first + lax.broadcasted_iota(jnp.int32, shape, 0)


def picked(kinds, values):
    total = 0.0
    for kind, value in enumerate(values):
        total = total + jnp.where(kinds == kind, value, 0.0)
    return total


def column(row):
    count = row.shape[1]
    same = lax.broadcasted_iota(jnp.int32, (count, count), 0) == lax.broadcasted_iota(
        jnp.int32, (count, count), 1
    )
    return jnp.sum(jnp.where(same, row, jnp.zeros_like(row)), axis=1, keepdims=True)


def table_kernel(place_ref, bus_ref, type_ref, limit_ref, cost_ref, table_ref, first_ref, copies_ref):
    kinds = column(type_ref[...])
    capacity = column(limit_ref[...]).astype(F32) / 100.0
    cost = column(cost_ref[...]) * picked(kinds, COST_FACTORS)
    storage = jnp.where(kinds == 3, 1.0, 0.0)
    lower = -capacity * storage
    lane = lax.broadcasted_iota(jnp.int32, table_ref.shape, 1)
    table = jnp.zeros(table_ref.shape, F32)
    parts = (cost, lower, capacity, picked(kinds, RAMP_RATES) * capacity, storage, 2.0 * capacity)
    for spot, part in enumerate(parts):
        table = jnp.where(lane == spot, part, table)
    table_ref[...] = table
    first = jnp.clip(-PRIMAL_STEP * cost, lower, capacity)
    first_ref[...] = jnp.broadcast_to(first, first_ref.shape)
    bus = column(bus_ref[...] - place_ref[0]).astype(F32)
    sent = jnp.where(lane < 64, 2.0 * first, bus)
    copies_ref[...] = jnp.broadcast_to(sent[None], copies_ref.shape)


def unit_tables(place, unit_bus, unit_type, unit_limit, unit_cost, line_count):
    units = unit_bus.shape[0]
    rows = [x.reshape(1, units) for x in (unit_bus, unit_type, unit_limit, unit_cost)]
    one = jax.ShapeDtypeStruct((units, 128), F32)
    return pl.pallas_call(
        table_kernel,
        in_specs=[SMEM] + [VMEM] * 4,
        out_specs=[VMEM] * 3,
        out_shape=[one, one, jax.ShapeDtypeStruct((line_count, units, 128), F32)],
        compiler_params=params(16),
        name="unit_tables",
    )(place, *rows)


def load_kernel(ptdf_ref, load_ref, out_ref, pair_ref):
    step = pl.program_id(0)

    @pl.when(step == 0)
    def _():
        high, low = halves(load_ref[...])
        pair_ref[:, :128] = high
        pair_ref[:, 128:] = low

    rows = row_index(ptdf_ref.shape, step * BLOCK)
    ptdf = jnp.where(rows < LINES_DEV, ptdf_ref[...], jnp.where(rows == LINES_DEV, 1.0, 0.0))
    high, low = halves(ptdf)
    both = dot(high, pair_ref[...])
    out_ref[...] = -(both[:, :128] + both[:, 128:] + dot(low, pair_ref[:, :128]))


def load_flows(ptdf, load):
    buses = ptdf.shape[1]
    return pl.pallas_call(
        load_kernel,
        grid=(ROWS // BLOCK,),
        in_specs=[
            pl.BlockSpec((BLOCK, buses), lambda i: (i, 0)),
            pl.BlockSpec((buses, 128), lambda i: (0, 0)),
        ],
        out_specs=pl.BlockSpec((BLOCK, 128), lambda i: (i, 0)),
        out_shape=jax.ShapeDtypeStruct((ROWS, 128), F32),
        scratch_shapes=[pltpu.VMEM((buses, 256), BF16)],
        compiler_params=params(48),
        cost_estimate=cost_of(3 * 2 * ROWS * buses * 128, 4 * ROWS * buses),
        name="load_flows",
    )(ptdf, load)


def columns_kernel(ptdf_ref, unit_ref, high_ref, low_ref, pick_ref):
    step = pl.program_id(0)
    span = ptdf_ref.shape[1] // 2
    units = unit_ref.shape[0] // 2

    @pl.when(step == 0)
    def _():
        for group in range(2):
            spots = unit_ref[group * units : (group + 1) * units, 64:65].astype(jnp.int32)
            index = lax.broadcasted_iota(jnp.int32, (units, span), 1) + group * span
            pick_ref[group] = jnp.where(index == spots, 1.0, 0.0).astype(BF16)

    rows = row_index((BLOCK, units), step * BLOCK)
    inside = row_index((BLOCK, span), step * BLOCK) < LINES_DEV
    for group in range(2):
        ptdf = jnp.where(inside, ptdf_ref[:, group * span : (group + 1) * span], 0.0)
        high, low = halves(ptdf)
        pick = pick_ref[group]
        high = dot(high, pick, ((1,), (1,)))
        low = dot(low, pick, ((1,), (1,)))
        where = slice(group * units, (group + 1) * units)
        high_ref[:, where] = jnp.where(rows == LINES_DEV, 1.0, high).astype(BF16)
        low_ref[:, where] = low.astype(BF16)


def unit_columns(ptdf, unit_rows):
    buses = ptdf.shape[1]
    units = unit_rows.shape[0]
    by_row = pl.BlockSpec((BLOCK, units), lambda i: (i, 0))
    return pl.pallas_call(
        columns_kernel,
        grid=(ROWS // BLOCK,),
        in_specs=[
            pl.BlockSpec((BLOCK, buses), lambda i: (i, 0)),
            pl.BlockSpec((units, 128), lambda i: (0, 0)),
        ],
        out_specs=[by_row, by_row],
        out_shape=[jax.ShapeDtypeStruct((ROWS, units), BF16)] * 2,
        scratch_shapes=[pltpu.VMEM((2, units // 2, buses // 2), BF16)],
        compiler_params=params(48),
        cost_estimate=cost_of(2 * 2 * ROWS * buses * units // 2, 4 * ROWS * buses),
        name="unit_columns",
    )(ptdf, unit_rows)


def flow_kernel(first, core_ref, high_ref, low_ref, extrap_ref, *refs):
    core = core_ref[0]
    mine_ref, other_ref = refs[-2:]
    extrap = extrap_ref[...]
    if first:
        extrap = jnp.broadcast_to(extrap[:, :1], extrap.shape)
    high, low = halves(extrap)
    pair = jnp.concatenate([high, low], axis=1)
    for ref, place in ((other_ref, 1 - core), (mine_ref, core)):
        rows = pl.ds(pl.multiple_of(place * HALF, 16), HALF)
        both = dot(high_ref[rows, :], pair)
        flow = both[:, :128] + both[:, 128:] + dot(low_ref[rows, :], high)
        ref[...] = flow + refs[0][rows, :] if first else flow


def unit_flows(core, high, low, extrap, *load):
    half = jax.ShapeDtypeStruct((HALF, 128), F32)
    return pl.pallas_call(
        functools.partial(flow_kernel, bool(load)),
        in_specs=[SMEM] + [VMEM] * (3 + len(load)),
        out_specs=[VMEM, VMEM],
        out_shape=[half, half],
        compiler_params=params(8),
        cost_estimate=cost_of(3 * 2 * ROWS * 512 * 128, 4 * ROWS * 512),
        name="unit_flows",
    )(core, high, low, extrap, *load)


def dual_kernel(left_ref, right_ref, flow_ref, dual_ref, step_ref, limit_ref, flow_out, dual_out):
    flow = flow_ref[...] + (left_ref[...] + right_ref[...])
    flow_out[...] = flow
    moved = dual_ref[...] + step_ref[...] * flow
    limit = limit_ref[...]
    dual_out[...] = moved - jnp.clip(moved, -limit, limit)


def dual_step(left, right, flow, dual, steps, limits):
    half = jax.ShapeDtypeStruct((HALF, 128), F32)
    return pl.pallas_call(
        dual_kernel,
        in_specs=[VMEM] * 6,
        out_specs=[VMEM, VMEM],
        out_shape=[half, half],
        compiler_params=params(8),
        name="dual_step",
    )(left, right, flow, dual, steps, limits)


def price_kernel(core_ref, mine_ref, other_ref, high_ref, low_ref, price_ref, dual_ref):
    core = core_ref[0]
    for ref, place in ((mine_ref, core), (other_ref, 1 - core)):
        dual_ref[pl.ds(pl.multiple_of(place * HALF, 8), HALF), :] = ref[...]
    dual_ref[2 * HALF :, :] = jnp.zeros((ROWS - 2 * HALF, 128), F32)
    high, low = halves(dual_ref[...].T)
    both = dot(jnp.concatenate([high, low], axis=0), high_ref[...])
    price = both[:128] + both[128:] + dot(high, low_ref[...])
    price_ref[...] = price.T


def unit_prices(core, mine, other, high, low):
    units = high.shape[1]
    return pl.pallas_call(
        price_kernel,
        in_specs=[SMEM] + [VMEM] * 4,
        out_specs=VMEM,
        out_shape=jax.ShapeDtypeStruct((units, 128), F32),
        scratch_shapes=[pltpu.VMEM((ROWS, 128), F32)],
        compiler_params=params(8),
        cost_estimate=cost_of(3 * 2 * ROWS * 512 * 128, 4 * ROWS * 512),
        name="unit_prices",
    )(core, mine, other, high, low)


def joined_kernel(core_ref, mine_ref, other_ref, dual_ref):
    first = core_ref[0] == 0
    mine, other = mine_ref[...], other_ref[...]
    dual_ref[:HALF, :] = jnp.where(first, mine, other)
    rest = LINES_DEV - HALF
    dual_ref[HALF:, :] = jnp.where(first, other[:rest], mine[:rest])


def joined(core, mine, other):
    return pl.pallas_call(
        joined_kernel,
        in_specs=[SMEM, VMEM, VMEM],
        out_specs=VMEM,
        out_shape=jax.ShapeDtypeStruct((LINES_DEV, 128), F32),
        compiler_params=params(8),
        name="joined",
    )(core, mine, other)


def unit_kernel(price_ref, gen_ref, old_ref, state_ref, table_ref, gen_out, extrap_ref, copies_ref):
    cost = table_ref[:, 0:1]
    lower = table_ref[:, 1:2]
    upper = table_ref[:, 2:3]
    gen = gen_ref[...]
    peers = price_ref.shape[0]
    prices = []
    for hours in range(2):
        total = price_ref[hours]
        for peer in range(hours + 2, peers, 2):
            total = total + price_ref[peer]
        prices.append(total)
    gradient = cost + jnp.concatenate(prices, axis=1) + state_ref[...]
    updated = jnp.clip(gen - PRIMAL_STEP * gradient, lower, upper)
    extrap = 2.0 * updated - gen
    gen_out[...] = updated
    extrap_ref[...] = extrap
    change = extrap - old_ref[...]
    for peer in range(peers):
        hours = peer % 2
        copies_ref[peer] = change[:, 128 * hours : 128 * (hours + 1)]


def unit_step(prices, gen, old, state, table):
    wide = jax.ShapeDtypeStruct(gen.shape, F32)
    return pl.pallas_call(
        unit_kernel,
        in_specs=[VMEM] * 5,
        out_specs=[VMEM] * 3,
        out_shape=[wide, wide, jax.ShapeDtypeStruct(prices.shape, F32)],
        compiler_params=params(8),
        name="unit_step",
    )(prices, gen, old, state, table)


def state_kernel(extrap_ref, ramp_ref, store_ref, table_ref, ramp_out, store_out, state_ref):
    ramp_limit = DUAL_STEP * table_ref[:, 3:4]
    storage = table_ref[:, 4:5]
    store_limit = DUAL_STEP * table_ref[:, 5:6]
    extrap = extrap_ref[...]
    hour = lax.broadcasted_iota(jnp.int32, extrap.shape, 1)
    hours = extrap.shape[1]
    previous = pltpu.roll(extrap, 1, 1)
    moved = ramp_ref[...] + jnp.where(hour >= 1, DUAL_STEP * (extrap - previous), 0.0)
    ramp = moved - jnp.clip(moved, -ramp_limit, ramp_limit)
    ramp_out[...] = ramp
    early = lax.broadcasted_iota(jnp.int32, (hours, hours), 0)
    late = lax.broadcasted_iota(jnp.int32, (hours, hours), 1)
    forward = jnp.where(early <= late, 1.0, 0.0)
    backward = jnp.where(early >= late, 1.0, 0.0)
    running = jnp.dot(extrap, forward, precision=lax.Precision.HIGHEST, preferred_element_type=F32)
    moved = store_ref[...] + DUAL_STEP * storage * running
    store = moved - jnp.clip(moved, -store_limit, store_limit)
    store_out[...] = store
    suffix = jnp.dot(store, backward, precision=lax.Precision.HIGHEST, preferred_element_type=F32)
    after = jnp.where(hour < hours - 1, pltpu.roll(ramp, hours - 1, 1), 0.0)
    state_ref[...] = ramp - after + storage * suffix


def state_step(extrap, ramp, store, table):
    wide = jax.ShapeDtypeStruct(ramp.shape, F32)
    return pl.pallas_call(
        state_kernel,
        in_specs=[VMEM] * 4,
        out_specs=[VMEM] * 3,
        out_shape=[wide] * 3,
        compiler_params=params(8),
        cost_estimate=cost_of(12 * 2 * 16 * 256 * 256, 1 << 17),
        name="state_step",
    )(extrap, ramp, store, table)


SWAP = ((0, 1), (1, 0))
NEAR = ((0, 1), (1, 0), (2, 3), (3, 2))
FAR = ((1, 2), (2, 1), (3, 0), (0, 3))


def along_y(value, by_core):
    pairs = [(2 * i + core, 2 * j + core) for core in range(2) for i, j in by_core[core]]
    return lax.ppermute(value, BUS, pairs)


def summed_over_bus(mine, other):
    total = mine + lax.ppermute(other, "c", SWAP)
    total = total + along_y(total, (NEAR, FAR))
    return total, along_y(total, (FAR, NEAR))


def on_device(ptdf, bus_load, unit_bus, unit_type, unit_limit, unit_cost, line_rating):
    line_count = lax.axis_size(LINE)
    hour_dev = bus_load.shape[1]
    local = unit_bus.shape[0]
    core = lax.axis_index("c").astype(jnp.int32)
    half_units = local // 2
    block = (lax.axis_index(BUS) * ptdf.shape[1]).astype(jnp.int32)
    table, first, copies = unit_tables(
        block[None], unit_bus, unit_type, unit_limit, unit_cost, line_count
    )
    unit_rows = lax.all_to_all(copies, LINE, 0, 0, tiled=True)
    unit_rows = unit_rows.reshape(line_count * local, hour_dev)
    load = load_flows(ptdf, bus_load)
    high, low = unit_columns(ptdf, unit_rows)

    own = lax.axis_index("t") * half_units
    table = lax.dynamic_slice_in_dim(table, own, half_units, 0)
    own_first = lax.dynamic_slice_in_dim(first, own, half_units, 0)
    gen = jnp.concatenate([own_first, own_first], axis=1)
    extrap = 2.0 * gen

    pad = jnp.zeros((2 * HALF - LINES_DEV,), F32)
    limits = jnp.concatenate([DUAL_STEP * (line_rating.astype(F32) / 100.0), pad])
    index = core * HALF + jnp.arange(HALF, dtype=jnp.int32)
    weight = 1.0 / (UNITS * 16)
    steps = jnp.where(index < LINES_DEV, DUAL_STEP, jnp.where(index == LINES_DEV, weight, 0.0))
    steps = steps.astype(F32)[:, None]
    limits = lax.dynamic_slice_in_dim(limits, core * HALF, HALF, 0)[:, None]
    core = core[None]
    flow = dual = jnp.zeros((HALF, hour_dev), F32)
    ramp = store = jnp.zeros((half_units, 2 * hour_dev), F32)
    mine, other = unit_flows(core, high, low, unit_rows, load)
    for iteration in range(ITERS):
        last = iteration == ITERS - 1
        if not last:
            ramp, store, state = state_step(extrap, ramp, store, table)
        left, right = summed_over_bus(mine, other)
        if not last:
            right, state, ramp, store = lax.optimization_barrier((right, state, ramp, store))
        flow, dual = dual_step(left, right, flow, dual, steps, limits)
        far = lax.ppermute(dual, "c", SWAP)
        if last:
            break
        prices = unit_prices(core, dual, far, high, low)
        prices = prices.reshape(2 * line_count, half_units, hour_dev)
        prices = lax.all_to_all(prices, LINE_TM, 0, 0, tiled=True)
        gen, extrap, copies = unit_step(prices, gen, extrap, state, table)
        changes = lax.all_to_all(copies, LINE_TM, 0, 0, tiled=True)
        mine, other = unit_flows(core, high, low, changes.reshape(-1, hour_dev))
    first_hours = lax.axis_index("t") == 0
    sent = jnp.where(first_hours, gen[:, hour_dev:], gen[:, :hour_dev])
    kept = jnp.where(first_hours, gen[:, :hour_dev], gen[:, hour_dev:])
    got = lax.ppermute(sent, "t", SWAP)
    upper_half = jnp.where(first_hours, kept, got)
    lower_half = jnp.where(first_hours, got, kept)
    return jnp.concatenate([upper_half, lower_half], axis=0), joined(core, dual, far)


def solution(mesh):
    finer = Mesh(
        mesh.devices.reshape(8, 2, 4, 2, mesh.shape["tm"]),
        ("z", "xl", "y", "c", "t"),
    )
    return jax.shard_map(
        on_device,
        mesh=finer,
        in_specs=(
            P(LINE, BUS),
            P(BUS, "t"),
            P(LINE_BUS),
            P(LINE_BUS),
            P(LINE_BUS),
            P(LINE_BUS),
            P(LINE),
        ),
        out_specs=(P(LINE_BUS, "t"), P(LINE, "t")),
        check_vma=False,
    )
```

```python
import functools

import jax
import jax.numpy as jnp
from jax import lax
from jax.experimental import pallas as pl
from jax.experimental.pallas import tpu as pltpu
from jax.sharding import Mesh
from jax.sharding import PartitionSpec as P

UNITS = 4096
ITERS = 4
LINE = ("z", "xl")
BUS = ("y", "c")
LINE_BUS = ("z", "xl", "y", "c")

RAMP_RATES = (0.1, 0.2, 0.4, 0.5)
COST_FACTORS = (1.0, 1.5, 3.0, 0.05)
PRIMAL_STEP = 0.5
DUAL_STEP = 0.5

LINES_DEV = 960
ROWS = 1024
HALF = 496
BLOCK = 256
PART = 248
BF16 = jnp.bfloat16
F32 = jnp.float32
VMEM = pl.BlockSpec(memory_space=pltpu.VMEM)
SMEM = pl.BlockSpec(memory_space=pltpu.SMEM)


def params(mib):
    return pltpu.CompilerParams(vmem_limit_bytes=mib << 20)


def cost_of(flops, size):
    return pl.CostEstimate(flops=flops, bytes_accessed=size, transcendentals=0)


def halves(value):
    high = value.astype(BF16)
    return high, (value - high.astype(F32)).astype(BF16)


def dot(left, right, dims=((1,), (0,))):
    return lax.dot_general(left, right, (dims, ((), ())), preferred_element_type=F32)


def row_index(shape, first):
    return first + lax.broadcasted_iota(jnp.int32, shape, 0)


def picked(kinds, values):
    total = 0.0
    for kind, value in enumerate(values):
        total = total + jnp.where(kinds == kind, value, 0.0)
    return total


def column(row):
    count = row.shape[1]
    same = lax.broadcasted_iota(jnp.int32, (count, count), 0) == lax.broadcasted_iota(
        jnp.int32, (count, count), 1
    )
    return jnp.sum(jnp.where(same, row, jnp.zeros_like(row)), axis=1, keepdims=True)


def table_kernel(
    place_ref, bus_in, type_in, limit_in, cost_in, load_in, table_ref, first_ref, copies_ref, load_ref,
    bus_ref, type_ref, limit_ref, cost_ref, arrived
):
    pairs = (
        (bus_in, bus_ref.at[0]),
        (type_in, type_ref.at[0]),
        (limit_in, limit_ref.at[0]),
        (cost_in, cost_ref.at[0]),
        (load_in, load_ref),
    )
    copies = [pltpu.make_async_copy(*pair, arrived.at[spot]) for spot, pair in enumerate(pairs)]
    for copy in copies:
        copy.start()
    for copy in copies[:-1]:
        copy.wait()
    kinds = column(type_ref[...])
    capacity = column(limit_ref[...]).astype(F32) / 100.0
    cost = column(cost_ref[...]) * picked(kinds, COST_FACTORS)
    storage = jnp.where(kinds == 3, 1.0, 0.0)
    lower = -capacity * storage
    lane = lax.broadcasted_iota(jnp.int32, table_ref.shape, 1)
    table = jnp.zeros(table_ref.shape, F32)
    parts = (cost, lower, capacity, picked(kinds, RAMP_RATES) * capacity, storage, 2.0 * capacity)
    for spot, part in enumerate(parts):
        table = jnp.where(lane == spot, part, table)
    table_ref[...] = table
    first = jnp.clip(-PRIMAL_STEP * cost, lower, capacity)
    first_ref[...] = jnp.broadcast_to(first, first_ref.shape)
    bus = column(bus_ref[...] - place_ref[0]).astype(F32)
    same = lane == lax.broadcasted_iota(jnp.int32, table_ref.shape, 0)
    bus = jnp.sum(jnp.where(same, bus, 0.0), axis=0, keepdims=True)
    extrap = jnp.sum(jnp.where(same, 2.0 * first, 0.0), axis=0, keepdims=True)
    sent = jnp.where(lax.broadcasted_iota(jnp.int32, (8, 128), 0) == 0, bus, extrap)
    copies_ref[...] = jnp.broadcast_to(sent[None], copies_ref.shape)
    copies[-1].wait()


def unit_tables(place, unit_bus, unit_type, unit_limit, unit_cost, load, line_count):
    units = unit_bus.shape[0]
    rows = (unit_bus, unit_type, unit_limit, unit_cost)
    one = jax.ShapeDtypeStruct((units, 128), F32)
    return pl.pallas_call(
        table_kernel,
        in_specs=[SMEM] + [pl.BlockSpec(memory_space=pltpu.HBM)] * 5,
        out_specs=[VMEM] * 4,
        out_shape=[
            one,
            one,
            jax.ShapeDtypeStruct((line_count, 8, 128), F32),
            jax.ShapeDtypeStruct(load.shape, F32),
        ],
        scratch_shapes=[pltpu.VMEM((1, units), row.dtype) for row in rows]
        + [pltpu.SemaphoreType.DMA((5,))],
        compiler_params=params(16),
        name="unit_tables",
    )(place, *(pltpu.with_memory_space_constraint(x, pltpu.HBM) for x in (*rows, load)))


def first_kernel(core_ref, ptdf_ref, unit_ref, load_ref, mine_ref, other_ref, pair_ref):
    step = pl.program_id(0)

    @pl.when(step == 0)
    def _():
        peers = unit_ref.shape[0]
        span = load_ref.shape[0] // peers
        units = 32
        lane = lax.broadcasted_iota(jnp.int32, (span, 128), 1)
        for peer in range(peers):
            spots = unit_ref[peer][0:1, :].astype(jnp.int32)
            bus = row_index((span, 128), peer * span)
            held = jnp.where((bus == spots) & (lane < units), unit_ref[peer][1:2, :], 0.0)
            rows = slice(peer * span, (peer + 1) * span)
            injection = jnp.sum(held, axis=1, keepdims=True) - load_ref[rows, :]
            high, low = halves(injection)
            pair_ref[rows, :128] = high
            pair_ref[rows, 128:] = low

    rows = row_index(ptdf_ref.shape, step * PART)
    ptdf = jnp.where(rows < LINES_DEV, ptdf_ref[...], jnp.where(rows == LINES_DEV, 1.0, 0.0))
    high, low = halves(ptdf)
    both = dot(high, pair_ref[...])
    flow = both[:, :128] + both[:, 128:] + dot(low, pair_ref[:, :128])
    rows = pl.ds(pl.multiple_of((step % 2) * PART, 8), PART)
    mine = step // 2 == core_ref[0]

    @pl.when(mine)
    def _():
        mine_ref[rows, :] = flow

    @pl.when(jnp.logical_not(mine))
    def _():
        other_ref[rows, :] = flow


def first_flows(core, ptdf, unit_rows, load):
    buses = ptdf.shape[1]
    half = jax.ShapeDtypeStruct((HALF, 128), F32)
    whole = pl.BlockSpec((HALF, 128), lambda i: (0, 0))
    return pl.pallas_call(
        first_kernel,
        grid=(2 * HALF // PART,),
        in_specs=[
            SMEM,
            pl.BlockSpec((PART, buses), lambda i: (i, 0)),
            pl.BlockSpec(unit_rows.shape, lambda i: (0, 0, 0)),
            pl.BlockSpec((buses, 128), lambda i: (0, 0)),
        ],
        out_specs=[whole, whole],
        out_shape=[half, half],
        scratch_shapes=[pltpu.VMEM((buses, 256), BF16)],
        compiler_params=params(48),
        cost_estimate=cost_of(3 * 2 * ROWS * buses * 128, 4 * ROWS * buses),
        name="first_flows",
    )(core, ptdf, unit_rows, load)


def columns_kernel(ptdf_ref, unit_ref, high_ref, low_ref, pick_ref):
    step = pl.program_id(0)
    peers = unit_ref.shape[0]
    span = ptdf_ref.shape[1] // 2
    units = high_ref.shape[1] // 2
    local = units * 2 // peers

    @pl.when(step == 0)
    def _():
        for peer in range(peers):
            group, place = divmod(peer, peers // 2)
            spots = column(unit_ref[peer][0:1, :local]).astype(jnp.int32)
            index = lax.broadcasted_iota(jnp.int32, (local, span), 1) + group * span
            pick = jnp.where(index == spots, 1.0, 0.0).astype(BF16)
            pick_ref[group, place * local : (place + 1) * local, :] = pick

    rows = row_index((BLOCK, units), step * BLOCK)
    inside = row_index((BLOCK, span), step * BLOCK) < LINES_DEV
    for group in range(2):
        ptdf = jnp.where(inside, ptdf_ref[:, group * span : (group + 1) * span], 0.0)
        high, low = halves(ptdf)
        pick = pick_ref[group]
        high = dot(high, pick, ((1,), (1,)))
        low = dot(low, pick, ((1,), (1,)))
        where = slice(group * units, (group + 1) * units)
        high_ref[:, where] = jnp.where(rows == LINES_DEV, 1.0, high).astype(BF16)
        low_ref[:, where] = low.astype(BF16)


def unit_columns(ptdf, unit_rows, units):
    buses = ptdf.shape[1]
    by_row = pl.BlockSpec((BLOCK, units), lambda i: (i, 0))
    return pl.pallas_call(
        columns_kernel,
        grid=(ROWS // BLOCK,),
        in_specs=[
            pl.BlockSpec((BLOCK, buses), lambda i: (i, 0)),
            pl.BlockSpec(unit_rows.shape, lambda i: (0, 0, 0)),
        ],
        out_specs=[by_row, by_row],
        out_shape=[jax.ShapeDtypeStruct((ROWS, units), BF16)] * 2,
        scratch_shapes=[pltpu.VMEM((2, units // 2, buses // 2), BF16)],
        compiler_params=params(48),
        cost_estimate=cost_of(2 * 2 * ROWS * buses * units // 2, 4 * ROWS * buses),
        name="unit_columns",
    )(ptdf, unit_rows)


def flow_kernel(core_ref, high_ref, low_ref, extrap_ref, mine_ref, other_ref):
    core = core_ref[0]
    high, low = halves(extrap_ref[...])
    pair = jnp.concatenate([high, low], axis=1)
    for ref, place in ((other_ref, 1 - core), (mine_ref, core)):
        rows = pl.ds(pl.multiple_of(place * HALF, 16), HALF)
        both = dot(high_ref[rows, :], pair)
        ref[...] = both[:, :128] + both[:, 128:] + dot(low_ref[rows, :], high)


def unit_flows(core, high, low, extrap):
    half = jax.ShapeDtypeStruct((HALF, 128), F32)
    return pl.pallas_call(
        flow_kernel,
        in_specs=[SMEM] + [VMEM] * 3,
        out_specs=[VMEM, VMEM],
        out_shape=[half, half],
        compiler_params=params(8),
        cost_estimate=cost_of(3 * 2 * ROWS * 512 * 128, 4 * ROWS * 512),
        name="unit_flows",
    )(core, high, low, extrap)


def dual_kernel(left_ref, right_ref, flow_ref, dual_ref, step_ref, limit_ref, dual_out, *flow_out):
    flow = flow_ref[...] + (left_ref[...] + right_ref[...])
    for ref in flow_out:
        ref[...] = flow
    moved = dual_ref[...] + step_ref[...] * flow
    limit = limit_ref[...]
    dual_out[...] = moved - jnp.clip(moved, -limit, limit)


def dual_step(left, right, flow, dual, steps, limits, outputs):
    half = jax.ShapeDtypeStruct((HALF, 128), F32)
    return pl.pallas_call(
        dual_kernel,
        in_specs=[VMEM] * 6,
        out_specs=[VMEM] * outputs,
        out_shape=[half] * outputs,
        compiler_params=params(8),
        name="dual_step",
    )(left, right, flow, dual, steps, limits)


def price_kernel(core_ref, mine_ref, other_ref, high_ref, low_ref, price_ref, dual_ref):
    core = core_ref[0]
    for ref, place in ((mine_ref, core), (other_ref, 1 - core)):
        dual_ref[pl.ds(pl.multiple_of(place * HALF, 8), HALF), :] = ref[...]
    dual_ref[2 * HALF :, :] = jnp.zeros((ROWS - 2 * HALF, 128), F32)
    high, low = halves(dual_ref[...].T)
    both = dot(jnp.concatenate([high, low], axis=0), high_ref[...])
    price = both[:128] + both[128:] + dot(high, low_ref[...])
    price_ref[...] = price.T


def unit_prices(core, mine, other, high, low):
    units = high.shape[1]
    return pl.pallas_call(
        price_kernel,
        in_specs=[SMEM] + [VMEM] * 4,
        out_specs=VMEM,
        out_shape=jax.ShapeDtypeStruct((units, 128), F32),
        scratch_shapes=[pltpu.VMEM((ROWS, 128), F32)],
        compiler_params=params(8),
        cost_estimate=cost_of(3 * 2 * ROWS * 512 * 128, 4 * ROWS * 512),
        name="unit_prices",
    )(core, mine, other, high, low)


def joined_kernel(core_ref, mine_ref, other_ref, dual_ref):
    first = core_ref[0] == 0
    mine, other = mine_ref[...], other_ref[...]
    dual_ref[:HALF, :] = jnp.where(first, mine, other)
    rest = LINES_DEV - HALF
    dual_ref[HALF:, :] = jnp.where(first, other[:rest], mine[:rest])


def joined(core, mine, other):
    return pl.pallas_call(
        joined_kernel,
        in_specs=[SMEM, VMEM, VMEM],
        out_specs=VMEM,
        out_shape=jax.ShapeDtypeStruct((LINES_DEV, 128), F32),
        compiler_params=params(8),
        name="joined",
    )(core, mine, other)


def unit_kernel(price_ref, gen_ref, old_ref, state_ref, table_ref, gen_out, extrap_ref, copies_ref):
    cost = table_ref[:, 0:1]
    lower = table_ref[:, 1:2]
    upper = table_ref[:, 2:3]
    gen = gen_ref[...]
    gradient = cost + jnp.sum(price_ref[...], axis=0) + state_ref[...]
    updated = jnp.clip(gen - PRIMAL_STEP * gradient, lower, upper)
    extrap = 2.0 * updated - gen
    gen_out[...] = updated
    extrap_ref[...] = extrap
    copies_ref[...] = jnp.broadcast_to((extrap - old_ref[...])[None], copies_ref.shape)


def unit_step(prices, gen, old, state, table):
    one = jax.ShapeDtypeStruct(gen.shape, F32)
    return pl.pallas_call(
        unit_kernel,
        in_specs=[VMEM] * 5,
        out_specs=[VMEM] * 3,
        out_shape=[one, one, jax.ShapeDtypeStruct(prices.shape, F32)],
        compiler_params=params(8),
        name="unit_step",
    )(prices, gen, old, state, table)


def state_kernel(place_ref, own_ref, far_ref, ramp_ref, store_ref, table_ref, ramp_out, store_out, state_ref):
    ramp_limit = DUAL_STEP * table_ref[:, 3:4]
    storage = table_ref[:, 4:5]
    store_limit = DUAL_STEP * table_ref[:, 5:6]
    first = place_ref[0] == 0
    own, far = own_ref[...], far_ref[...]
    extrap = jnp.concatenate([jnp.where(first, own, far), jnp.where(first, far, own)], axis=1)
    hour = lax.broadcasted_iota(jnp.int32, extrap.shape, 1)
    hours = extrap.shape[1]
    previous = pltpu.roll(extrap, 1, 1)
    moved = ramp_ref[...] + jnp.where(hour >= 1, DUAL_STEP * (extrap - previous), 0.0)
    ramp = moved - jnp.clip(moved, -ramp_limit, ramp_limit)
    ramp_out[...] = ramp
    early = lax.broadcasted_iota(jnp.int32, (hours, hours), 0)
    late = lax.broadcasted_iota(jnp.int32, (hours, hours), 1)
    forward = jnp.where(early <= late, 1.0, 0.0)
    backward = jnp.where(early >= late, 1.0, 0.0)
    running = jnp.dot(extrap, forward, precision=lax.Precision.HIGHEST, preferred_element_type=F32)
    moved = store_ref[...] + DUAL_STEP * storage * running
    store = moved - jnp.clip(moved, -store_limit, store_limit)
    store_out[...] = store
    suffix = jnp.dot(store, backward, precision=lax.Precision.HIGHEST, preferred_element_type=F32)
    after = jnp.where(hour < hours - 1, pltpu.roll(ramp, hours - 1, 1), 0.0)
    state = ramp - after + storage * suffix
    state_ref[...] = jnp.where(first, state[:, :128], state[:, 128:])


def state_step(place, own, far, ramp, store, table):
    wide = jax.ShapeDtypeStruct(ramp.shape, F32)
    return pl.pallas_call(
        state_kernel,
        in_specs=[SMEM] + [VMEM] * 5,
        out_specs=[VMEM] * 3,
        out_shape=[wide, wide, jax.ShapeDtypeStruct(own.shape, F32)],
        compiler_params=params(8),
        cost_estimate=cost_of(12 * 2 * 32 * 256 * 256, 1 << 18),
        name="state_step",
    )(place, own, far, ramp, store, table)


SWAP = ((0, 1), (1, 0))
NEAR = ((0, 1), (1, 0), (2, 3), (3, 2))
FAR = ((1, 2), (2, 1), (3, 0), (0, 3))


def along_y(value, by_core):
    pairs = [(2 * i + core, 2 * j + core) for core in range(2) for i, j in by_core[core]]
    return lax.ppermute(value, BUS, pairs)


def on_device(ptdf, bus_load, unit_bus, unit_type, unit_limit, unit_cost, line_rating):
    line_count = lax.axis_size(LINE)
    hour_dev = bus_load.shape[1]
    local = unit_bus.shape[0]
    core = lax.axis_index("c").astype(jnp.int32)
    place = lax.axis_index("t").astype(jnp.int32)[None]
    block = (lax.axis_index(BUS) * ptdf.shape[1]).astype(jnp.int32)
    table, gen, copies, load = unit_tables(
        block[None], unit_bus, unit_type, unit_limit, unit_cost, bus_load, line_count
    )
    unit_rows = lax.all_to_all(copies, LINE, 0, 0, tiled=True)
    mine, other = first_flows(core[None], ptdf, unit_rows, load)
    extrap = far = 2.0 * gen

    pad = jnp.zeros((2 * HALF - LINES_DEV,), F32)
    limits = jnp.concatenate([DUAL_STEP * (line_rating.astype(F32) / 100.0), pad])
    index = core * HALF + jnp.arange(HALF, dtype=jnp.int32)
    weight = 1.0 / (UNITS * 16)
    steps = jnp.where(index < LINES_DEV, DUAL_STEP, jnp.where(index == LINES_DEV, weight, 0.0))
    steps = steps.astype(F32)[:, None]
    limits = lax.dynamic_slice_in_dim(limits, core * HALF, HALF, 0)[:, None]
    core = core[None]
    flow = dual = jnp.zeros((HALF, hour_dev), F32)
    ramp = store = jnp.zeros((local, 2 * hour_dev), F32)
    high = low = None
    for iteration in range(ITERS):
        last = iteration == ITERS - 1
        total = mine + lax.ppermute(other, "c", SWAP)
        if iteration == 0:
            total, tied, rows = lax.optimization_barrier((total, ptdf, unit_rows))
            high, low = unit_columns(tied, rows, line_count * local)
        elif not last:
            total, tied = lax.optimization_barrier((total, extrap))
            far = lax.ppermute(tied, "t", SWAP)
        total = total + along_y(total, (NEAR, FAR))
        if not last:
            ramp, store, state = state_step(place, extrap, far, ramp, store, table)
        right = along_y(total, (FAR, NEAR))
        if iteration == 0:
            right, high, low = lax.optimization_barrier((right, high, low))
        if last:
            (dual,) = dual_step(total, right, flow, dual, steps, limits, 1)
            return gen, joined(core, dual, lax.ppermute(dual, "c", SWAP))
        right, state, ramp, store = lax.optimization_barrier((right, state, ramp, store))
        dual, flow = dual_step(total, right, flow, dual, steps, limits, 2)
        prices = unit_prices(core, dual, lax.ppermute(dual, "c", SWAP), high, low)
        prices = prices.reshape(line_count, local, hour_dev)
        prices = lax.all_to_all(prices, LINE, 0, 0, tiled=True)
        gen, extrap, copies = unit_step(prices, gen, extrap, state, table)
        changes = lax.all_to_all(copies, LINE, 0, 0, tiled=True)
        mine, other = unit_flows(core, high, low, changes.reshape(-1, hour_dev))


def solution(mesh):
    finer = Mesh(
        mesh.devices.reshape(8, 2, 4, 2, mesh.shape["tm"]),
        ("z", "xl", "y", "c", "t"),
    )
    return jax.shard_map(
        on_device,
        mesh=finer,
        in_specs=(
            P(LINE, BUS),
            P(BUS, "t"),
            P(LINE_BUS),
            P(LINE_BUS),
            P(LINE_BUS),
            P(LINE_BUS),
            P(LINE),
        ),
        out_specs=(P(LINE_BUS, "t"), P(LINE, "t")),
        check_vma=False,
    )
```

```python
import jax
import jax.numpy as jnp
from jax import lax
from jax.experimental import pallas as pl
from jax.experimental.pallas import tpu as pltpu
from jax.sharding import Mesh
from jax.sharding import PartitionSpec as P

UNITS = 4096
ITERS = 4
LINE = ("z", "xl")
BUS = ("y", "c")
LINE_BUS = ("z", "xl", "y", "c")

RAMP_RATES = (0.1, 0.2, 0.4, 0.5)
COST_FACTORS = (1.0, 1.5, 3.0, 0.05)
PRIMAL_STEP = 0.5
DUAL_STEP = 0.5

LINES_DEV = 960
ROWS = 1024
HALF = 496
BLOCK = 256
PART = 248
CHUNKS = ((0, 240), (240, HALF))
BF16 = jnp.bfloat16
F32 = jnp.float32
VMEM = pl.BlockSpec(memory_space=pltpu.VMEM)
SMEM = pl.BlockSpec(memory_space=pltpu.SMEM)


def params(mib):
    return pltpu.CompilerParams(vmem_limit_bytes=mib << 20)


def cost_of(flops, size):
    return pl.CostEstimate(flops=flops, bytes_accessed=size, transcendentals=0)


def halves(value):
    high = value.astype(BF16)
    return high, (value - high.astype(F32)).astype(BF16)


def dot(left, right, dims=((1,), (0,))):
    return lax.dot_general(left, right, (dims, ((), ())), preferred_element_type=F32)


def row_index(shape, first):
    return first + lax.broadcasted_iota(jnp.int32, shape, 0)


def picked(kinds, values):
    total = 0.0
    for kind, value in enumerate(values):
        total = total + jnp.where(kinds == kind, value, 0.0)
    return total


def column(row):
    count = row.shape[1]
    same = lax.broadcasted_iota(jnp.int32, (count, count), 0) == lax.broadcasted_iota(
        jnp.int32, (count, count), 1
    )
    return jnp.sum(jnp.where(same, row, jnp.zeros_like(row)), axis=1, keepdims=True)


def table_kernel(
    place_ref, bus_in, type_in, limit_in, cost_in, load_in, table_ref, first_ref, copies_ref, load_ref,
    bus_ref, type_ref, limit_ref, cost_ref, arrived
):
    pairs = (
        (bus_in, bus_ref.at[0]),
        (type_in, type_ref.at[0]),
        (limit_in, limit_ref.at[0]),
        (cost_in, cost_ref.at[0]),
        (load_in, load_ref),
    )
    copies = [pltpu.make_async_copy(*pair, arrived.at[spot]) for spot, pair in enumerate(pairs)]
    for copy in copies:
        copy.start()
    for copy in copies[:-1]:
        copy.wait()
    kinds = column(type_ref[...])
    capacity = column(limit_ref[...]).astype(F32) / 100.0
    cost = column(cost_ref[...]) * picked(kinds, COST_FACTORS)
    storage = jnp.where(kinds == 3, 1.0, 0.0)
    lower = -capacity * storage
    lane = lax.broadcasted_iota(jnp.int32, table_ref.shape, 1)
    table = jnp.zeros(table_ref.shape, F32)
    parts = (cost, lower, capacity, picked(kinds, RAMP_RATES) * capacity, storage, 2.0 * capacity)
    for spot, part in enumerate(parts):
        table = jnp.where(lane == spot, part, table)
    table_ref[...] = table
    first = jnp.clip(-PRIMAL_STEP * cost, lower, capacity)
    first_ref[...] = jnp.broadcast_to(first, first_ref.shape)
    bus = column(bus_ref[...] - place_ref[0]).astype(F32)
    same = lane == lax.broadcasted_iota(jnp.int32, table_ref.shape, 0)
    bus = jnp.sum(jnp.where(same, bus, 0.0), axis=0, keepdims=True)
    extrap = jnp.sum(jnp.where(same, 2.0 * first, 0.0), axis=0, keepdims=True)
    sent = jnp.where(lax.broadcasted_iota(jnp.int32, (8, 128), 0) == 0, bus, extrap)
    copies_ref[...] = jnp.broadcast_to(sent[None], copies_ref.shape)
    copies[-1].wait()


def unit_tables(place, unit_bus, unit_type, unit_limit, unit_cost, load, line_count):
    units = unit_bus.shape[0]
    rows = (unit_bus, unit_type, unit_limit, unit_cost)
    one = jax.ShapeDtypeStruct((units, 128), F32)
    return pl.pallas_call(
        table_kernel,
        in_specs=[SMEM] + [pl.BlockSpec(memory_space=pltpu.HBM)] * 5,
        out_specs=[VMEM] * 4,
        out_shape=[
            one,
            one,
            jax.ShapeDtypeStruct((line_count, 8, 128), F32),
            jax.ShapeDtypeStruct(load.shape, F32),
        ],
        scratch_shapes=[pltpu.VMEM((1, units), row.dtype) for row in rows]
        + [pltpu.SemaphoreType.DMA((5,))],
        compiler_params=params(16),
        name="unit_tables",
    )(place, *(pltpu.with_memory_space_constraint(x, pltpu.HBM) for x in (*rows, load)))


def first_kernel(core_ref, ptdf_ref, unit_ref, load_ref, mine_ref, other_ref, pair_ref):
    step = pl.program_id(0)

    @pl.when(step == 0)
    def _():
        peers = unit_ref.shape[0]
        span = load_ref.shape[0] // peers
        units = 32
        lane = lax.broadcasted_iota(jnp.int32, (span, 128), 1)
        for peer in range(peers):
            spots = unit_ref[peer][0:1, :].astype(jnp.int32)
            bus = row_index((span, 128), peer * span)
            held = jnp.where((bus == spots) & (lane < units), unit_ref[peer][1:2, :], 0.0)
            rows = slice(peer * span, (peer + 1) * span)
            injection = jnp.sum(held, axis=1, keepdims=True) - load_ref[rows, :]
            high, low = halves(injection)
            pair_ref[rows, :128] = high
            pair_ref[rows, 128:] = low

    rows = row_index(ptdf_ref.shape, step * PART)
    ptdf = jnp.where(rows < LINES_DEV, ptdf_ref[...], jnp.where(rows == LINES_DEV, 1.0, 0.0))
    high, low = halves(ptdf)
    both = dot(high, pair_ref[...])
    flow = both[:, :128] + both[:, 128:] + dot(low, pair_ref[:, :128])
    rows = pl.ds(pl.multiple_of((step % 2) * PART, 8), PART)
    mine = step // 2 == core_ref[0]

    @pl.when(mine)
    def _():
        mine_ref[rows, :] = flow

    @pl.when(jnp.logical_not(mine))
    def _():
        other_ref[rows, :] = flow


def first_flows(core, ptdf, unit_rows, load):
    buses = ptdf.shape[1]
    half = jax.ShapeDtypeStruct((HALF, 128), F32)
    whole = pl.BlockSpec((HALF, 128), lambda i: (0, 0))
    return pl.pallas_call(
        first_kernel,
        grid=(2 * HALF // PART,),
        in_specs=[
            SMEM,
            pl.BlockSpec((PART, buses), lambda i: (i, 0)),
            pl.BlockSpec(unit_rows.shape, lambda i: (0, 0, 0)),
            pl.BlockSpec((buses, 128), lambda i: (0, 0)),
        ],
        out_specs=[whole, whole],
        out_shape=[half, half],
        scratch_shapes=[pltpu.VMEM((buses, 256), BF16)],
        compiler_params=params(48),
        cost_estimate=cost_of(3 * 2 * ROWS * buses * 128, 4 * ROWS * buses),
        name="first_flows",
    )(core, ptdf, unit_rows, load)


def columns_kernel(ptdf_ref, unit_ref, high_ref, low_ref, pick_ref):
    step = pl.program_id(0)
    peers = unit_ref.shape[0]
    span = ptdf_ref.shape[1] // 2
    units = high_ref.shape[1] // 2
    local = units * 2 // peers

    @pl.when(step == 0)
    def _():
        for peer in range(peers):
            group, place = divmod(peer, peers // 2)
            spots = column(unit_ref[peer][0:1, :local]).astype(jnp.int32)
            index = lax.broadcasted_iota(jnp.int32, (local, span), 1) + group * span
            pick = jnp.where(index == spots, 1.0, 0.0).astype(BF16)
            pick_ref[group, place * local : (place + 1) * local, :] = pick

    rows = row_index((BLOCK, units), step * BLOCK)
    inside = row_index((BLOCK, span), step * BLOCK) < LINES_DEV
    for group in range(2):
        ptdf = jnp.where(inside, ptdf_ref[:, group * span : (group + 1) * span], 0.0)
        high, low = halves(ptdf)
        pick = pick_ref[group]
        high = dot(high, pick, ((1,), (1,)))
        low = dot(low, pick, ((1,), (1,)))
        where = slice(group * units, (group + 1) * units)
        high_ref[:, where] = jnp.where(rows == LINES_DEV, 1.0, high).astype(BF16)
        low_ref[:, where] = low.astype(BF16)


def unit_columns(ptdf, unit_rows, units):
    buses = ptdf.shape[1]
    by_row = pl.BlockSpec((BLOCK, units), lambda i: (i, 0))
    return pl.pallas_call(
        columns_kernel,
        grid=(ROWS // BLOCK,),
        in_specs=[
            pl.BlockSpec((BLOCK, buses), lambda i: (i, 0)),
            pl.BlockSpec(unit_rows.shape, lambda i: (0, 0, 0)),
        ],
        out_specs=[by_row, by_row],
        out_shape=[jax.ShapeDtypeStruct((ROWS, units), BF16)] * 2,
        scratch_shapes=[pltpu.VMEM((2, units // 2, buses // 2), BF16)],
        compiler_params=params(48),
        cost_estimate=cost_of(2 * 2 * ROWS * buses * units // 2, 4 * ROWS * buses),
        name="unit_columns",
    )(ptdf, unit_rows)


def flow_kernel(place_ref, high_ref, low_ref, extrap_ref, flow_ref):
    high, low = halves(extrap_ref[...])
    pair = jnp.concatenate([high, low], axis=1)
    rows = pl.ds(pl.multiple_of(place_ref[0] * HALF, 16), HALF)
    both = dot(high_ref[rows, :], pair)
    flow_ref[...] = both[:, :128] + both[:, 128:] + dot(low_ref[rows, :], high)


def unit_flows(place, high, low, extrap):
    return pl.pallas_call(
        flow_kernel,
        in_specs=[SMEM] + [VMEM] * 3,
        out_specs=VMEM,
        out_shape=jax.ShapeDtypeStruct((HALF, 128), F32),
        compiler_params=params(8),
        cost_estimate=cost_of(3 * 2 * HALF * 512 * 128, 4 * HALF * 512),
        name="unit_flows",
    )(place, high, low, extrap)


def dual_kernel(*refs):
    count = len(CHUNKS)
    lefts, rights = refs[:count], refs[count : 2 * count]
    flow_ref, dual_ref, step_ref, limit_ref, dual_out, *flow_out = refs[2 * count :]
    for chunk, ends in enumerate(CHUNKS):
        rows = slice(*ends)
        flow = flow_ref[rows, :] + (lefts[chunk][...] + rights[chunk][...])
        for ref in flow_out:
            ref[rows, :] = flow
        moved = dual_ref[rows, :] + step_ref[rows, :] * flow
        limit = limit_ref[rows, :]
        dual_out[rows, :] = moved - jnp.clip(moved, -limit, limit)


def dual_step(lefts, rights, flow, dual, steps, limits, outputs):
    half = jax.ShapeDtypeStruct((HALF, 128), F32)
    return pl.pallas_call(
        dual_kernel,
        in_specs=[VMEM] * (4 + 2 * len(lefts)),
        out_specs=[VMEM] * outputs,
        out_shape=[half] * outputs,
        compiler_params=params(8),
        name="dual_step",
    )(*lefts, *rights, flow, dual, steps, limits)


def price_kernel(place_ref, dual_ref, high_ref, low_ref, *refs):
    rows = pl.ds(pl.multiple_of(place_ref[0] * HALF, 16), HALF)
    high, low = halves(dual_ref[...].T)
    both = dot(jnp.concatenate([high, low], axis=0), high_ref[rows, :])
    price = both[:128] + both[128:] + dot(high, low_ref[rows, :])
    if len(refs) == 2:
        refs[1][...] = (refs[0][...] + price).T
    else:
        refs[0][...] = price


def unit_prices(place, dual, high, low, *part):
    units = high.shape[1]
    return pl.pallas_call(
        price_kernel,
        in_specs=[SMEM] + [VMEM] * (3 + len(part)),
        out_specs=VMEM,
        out_shape=jax.ShapeDtypeStruct((units, 128) if part else (128, units), F32),
        compiler_params=params(8),
        cost_estimate=cost_of(3 * 2 * HALF * 512 * 128, 4 * HALF * 512),
        name="unit_prices",
    )(place, dual, high, low, *part)


def joined_kernel(core_ref, mine_ref, other_ref, dual_ref):
    first = core_ref[0] == 0
    mine, other = mine_ref[...], other_ref[...]
    dual_ref[:HALF, :] = jnp.where(first, mine, other)
    rest = LINES_DEV - HALF
    dual_ref[HALF:, :] = jnp.where(first, other[:rest], mine[:rest])


def joined(core, mine, other):
    return pl.pallas_call(
        joined_kernel,
        in_specs=[SMEM, VMEM, VMEM],
        out_specs=VMEM,
        out_shape=jax.ShapeDtypeStruct((LINES_DEV, 128), F32),
        compiler_params=params(8),
        name="joined",
    )(core, mine, other)


def unit_kernel(price_ref, gen_ref, old_ref, state_ref, table_ref, gen_out, extrap_ref, copies_ref):
    cost = table_ref[:, 0:1]
    lower = table_ref[:, 1:2]
    upper = table_ref[:, 2:3]
    gen = gen_ref[...]
    gradient = cost + jnp.sum(price_ref[...], axis=0) + state_ref[...]
    updated = jnp.clip(gen - PRIMAL_STEP * gradient, lower, upper)
    extrap = 2.0 * updated - gen
    gen_out[...] = updated
    extrap_ref[...] = extrap
    copies_ref[...] = jnp.broadcast_to((extrap - old_ref[...])[None], copies_ref.shape)


def unit_step(prices, gen, old, state, table):
    one = jax.ShapeDtypeStruct(gen.shape, F32)
    return pl.pallas_call(
        unit_kernel,
        in_specs=[VMEM] * 5,
        out_specs=[VMEM] * 3,
        out_shape=[one, one, jax.ShapeDtypeStruct(prices.shape, F32)],
        compiler_params=params(8),
        name="unit_step",
    )(prices, gen, old, state, table)


def state_kernel(place_ref, own_ref, far_ref, ramp_ref, store_ref, table_ref, ramp_out, store_out, state_ref):
    ramp_limit = DUAL_STEP * table_ref[:, 3:4]
    storage = table_ref[:, 4:5]
    store_limit = DUAL_STEP * table_ref[:, 5:6]
    first = place_ref[0] == 0
    own, far = own_ref[...], far_ref[...]
    extrap = jnp.concatenate([jnp.where(first, own, far), jnp.where(first, far, own)], axis=1)
    hour = lax.broadcasted_iota(jnp.int32, extrap.shape, 1)
    hours = extrap.shape[1]
    previous = pltpu.roll(extrap, 1, 1)
    moved = ramp_ref[...] + jnp.where(hour >= 1, DUAL_STEP * (extrap - previous), 0.0)
    ramp = moved - jnp.clip(moved, -ramp_limit, ramp_limit)
    ramp_out[...] = ramp
    early = lax.broadcasted_iota(jnp.int32, (hours, hours), 0)
    late = lax.broadcasted_iota(jnp.int32, (hours, hours), 1)
    forward = jnp.where(early <= late, 1.0, 0.0)
    backward = jnp.where(early >= late, 1.0, 0.0)
    running = jnp.dot(extrap, forward, precision=lax.Precision.HIGHEST, preferred_element_type=F32)
    moved = store_ref[...] + DUAL_STEP * storage * running
    store = moved - jnp.clip(moved, -store_limit, store_limit)
    store_out[...] = store
    suffix = jnp.dot(store, backward, precision=lax.Precision.HIGHEST, preferred_element_type=F32)
    after = jnp.where(hour < hours - 1, pltpu.roll(ramp, hours - 1, 1), 0.0)
    state = ramp - after + storage * suffix
    state_ref[...] = jnp.where(first, state[:, :128], state[:, 128:])


def state_step(place, own, far, ramp, store, table):
    wide = jax.ShapeDtypeStruct(ramp.shape, F32)
    return pl.pallas_call(
        state_kernel,
        in_specs=[SMEM] + [VMEM] * 5,
        out_specs=[VMEM] * 3,
        out_shape=[wide, wide, jax.ShapeDtypeStruct(own.shape, F32)],
        compiler_params=params(8),
        cost_estimate=cost_of(12 * 2 * 32 * 256 * 256, 1 << 18),
        name="state_step",
    )(place, own, far, ramp, store, table)


SWAP = ((0, 1), (1, 0))
NEAR = ((0, 1), (1, 0), (2, 3), (3, 2))
FAR = ((1, 2), (2, 1), (3, 0), (0, 3))


def along_y(value, by_core):
    pairs = [(2 * i + core, 2 * j + core) for core in range(2) for i, j in by_core[core]]
    return lax.ppermute(value, BUS, pairs)


def on_device(ptdf, bus_load, unit_bus, unit_type, unit_limit, unit_cost, line_rating):
    line_count = lax.axis_size(LINE)
    hour_dev = bus_load.shape[1]
    local = unit_bus.shape[0]
    core = lax.axis_index("c").astype(jnp.int32)
    place = lax.axis_index("t").astype(jnp.int32)[None]
    block = (lax.axis_index(BUS) * ptdf.shape[1]).astype(jnp.int32)
    table, gen, copies, load = unit_tables(
        block[None], unit_bus, unit_type, unit_limit, unit_cost, bus_load, line_count
    )
    unit_rows = lax.all_to_all(copies, LINE, 0, 0, tiled=True)
    mine, other = first_flows(core[None], ptdf, unit_rows, load)
    extrap = far = 2.0 * gen

    pad = jnp.zeros((2 * HALF - LINES_DEV,), F32)
    limits = jnp.concatenate([DUAL_STEP * (line_rating.astype(F32) / 100.0), pad])
    index = core * HALF + jnp.arange(HALF, dtype=jnp.int32)
    weight = 1.0 / (UNITS * 16)
    steps = jnp.where(index < LINES_DEV, DUAL_STEP, jnp.where(index == LINES_DEV, weight, 0.0))
    steps = steps.astype(F32)[:, None]
    limits = lax.dynamic_slice_in_dim(limits, core * HALF, HALF, 0)[:, None]
    core, partner = core[None], 1 - core[None]
    flow = dual = jnp.zeros((HALF, hour_dev), F32)
    ramp = store = jnp.zeros((local, 2 * hour_dev), F32)
    high = low = None
    for iteration in range(ITERS):
        last = iteration == ITERS - 1
        total = mine + lax.ppermute(other, "c", SWAP)
        if iteration == 0:
            total, tied, rows = lax.optimization_barrier((total, ptdf, unit_rows))
            high, low = unit_columns(tied, rows, line_count * local)
        elif not last:
            total, tied = lax.optimization_barrier((total, extrap))
            far = lax.ppermute(tied, "t", SWAP)
        lefts = [total[start:stop] for start, stop in CHUNKS]
        lefts = [left + along_y(left, (NEAR, FAR)) for left in lefts]
        if 0 < iteration < ITERS - 1:
            lefts[0], far = lax.optimization_barrier((lefts[0], far))
        if not last:
            ramp, store, state = state_step(place, extrap, far, ramp, store, table)
        rights = [along_y(left, (FAR, NEAR)) for left in lefts]
        if iteration == 0:
            rights[-1], high, low = lax.optimization_barrier((rights[-1], high, low))
        if last:
            (dual,) = dual_step(lefts, rights, flow, dual, steps, limits, 1)
            return gen, joined(core, dual, lax.ppermute(dual, "c", SWAP))
        rights[-1], state, ramp, store = lax.optimization_barrier((rights[-1], state, ramp, store))
        dual, flow = dual_step(lefts, rights, flow, dual, steps, limits, 2)
        prices = unit_prices(core, dual, high, low)
        prices = unit_prices(partner, lax.ppermute(dual, "c", SWAP), high, low, prices)
        prices = prices.reshape(line_count, local, hour_dev)
        prices = lax.all_to_all(prices, LINE, 0, 0, tiled=True)
        gen, extrap, copies = unit_step(prices, gen, extrap, state, table)
        changes = lax.all_to_all(copies, LINE, 0, 0, tiled=True).reshape(-1, hour_dev)
        other = unit_flows(partner, high, low, changes)
        mine = unit_flows(core, high, low, changes)


def solution(mesh):
    finer = Mesh(
        mesh.devices.reshape(8, 2, 4, 2, mesh.shape["tm"]),
        ("z", "xl", "y", "c", "t"),
    )
    return jax.shard_map(
        on_device,
        mesh=finer,
        in_specs=(
            P(LINE, BUS),
            P(BUS, "t"),
            P(LINE_BUS),
            P(LINE_BUS),
            P(LINE_BUS),
            P(LINE_BUS),
            P(LINE),
        ),
        out_specs=(P(LINE_BUS, "t"), P(LINE, "t")),
        check_vma=False,
    )
```

```python
import functools

import jax
import jax.numpy as jnp
from jax import lax
from jax.experimental import pallas as pl
from jax.experimental.pallas import tpu as pltpu
from jax.sharding import Mesh
from jax.sharding import PartitionSpec as P

UNITS = 4096
ITERS = 4
LINE = ("z", "xl")
BUS = ("y", "c")
LINE_BUS = ("z", "xl", "y", "c")

RAMP_RATES = (0.1, 0.2, 0.4, 0.5)
COST_FACTORS = (1.0, 1.5, 3.0, 0.05)
PRIMAL_STEP = 0.5
DUAL_STEP = 0.5

LINES_DEV = 960
ROWS = 1024
HALF = 496
BLOCK = 256
PART = 248
KEPT = 400
CHUNKS = ((0, 240), (240, HALF))
BF16 = jnp.bfloat16
F32 = jnp.float32
VMEM = pl.BlockSpec(memory_space=pltpu.VMEM)
SMEM = pl.BlockSpec(memory_space=pltpu.SMEM)


def params(mib):
    return pltpu.CompilerParams(vmem_limit_bytes=mib << 20)


def cost_of(flops, size):
    return pl.CostEstimate(flops=flops, bytes_accessed=size, transcendentals=0)


def halves(value):
    high = value.astype(BF16)
    return high, (value - high.astype(F32)).astype(BF16)


def dot(left, right, dims=((1,), (0,))):
    return lax.dot_general(left, right, (dims, ((), ())), preferred_element_type=F32)


def row_index(shape, first):
    return first + lax.broadcasted_iota(jnp.int32, shape, 0)


def picked(kinds, values):
    total = 0.0
    for kind, value in enumerate(values):
        total = total + jnp.where(kinds == kind, value, 0.0)
    return total


def column(row):
    count = row.shape[1]
    same = lax.broadcasted_iota(jnp.int32, (count, count), 0) == lax.broadcasted_iota(
        jnp.int32, (count, count), 1
    )
    return jnp.sum(jnp.where(same, row, jnp.zeros_like(row)), axis=1, keepdims=True)


def table_kernel(
    place_ref, bus_in, type_in, limit_in, cost_in, table_ref, first_ref, copies_ref,
    bus_ref, type_ref, limit_ref, cost_ref, arrived
):
    pairs = (
        (bus_in, bus_ref.at[0]),
        (type_in, type_ref.at[0]),
        (limit_in, limit_ref.at[0]),
        (cost_in, cost_ref.at[0]),
    )
    copies = [pltpu.make_async_copy(*pair, arrived.at[spot]) for spot, pair in enumerate(pairs)]
    for copy in copies:
        copy.start()
    for copy in copies:
        copy.wait()
    kinds = column(type_ref[...])
    capacity = column(limit_ref[...]).astype(F32) / 100.0
    cost = column(cost_ref[...]) * picked(kinds, COST_FACTORS)
    storage = jnp.where(kinds == 3, 1.0, 0.0)
    lower = -capacity * storage
    lane = lax.broadcasted_iota(jnp.int32, table_ref.shape, 1)
    table = jnp.zeros(table_ref.shape, F32)
    parts = (cost, lower, capacity, picked(kinds, RAMP_RATES) * capacity, storage, 2.0 * capacity)
    for spot, part in enumerate(parts):
        table = jnp.where(lane == spot, part, table)
    table_ref[...] = table
    first = jnp.clip(-PRIMAL_STEP * cost, lower, capacity)
    first_ref[...] = jnp.broadcast_to(first, first_ref.shape)
    bus = column(bus_ref[...] - place_ref[0]).astype(F32)
    same = lane == lax.broadcasted_iota(jnp.int32, table_ref.shape, 0)
    bus = jnp.sum(jnp.where(same, bus, 0.0), axis=0, keepdims=True)
    extrap = jnp.sum(jnp.where(same, 2.0 * first, 0.0), axis=0, keepdims=True)
    sent = jnp.where(lax.broadcasted_iota(jnp.int32, (8, 128), 0) == 0, bus, extrap)
    copies_ref[...] = jnp.broadcast_to(sent[None], copies_ref.shape)


def unit_tables(place, unit_bus, unit_type, unit_limit, unit_cost, line_count):
    units = unit_bus.shape[0]
    rows = (unit_bus, unit_type, unit_limit, unit_cost)
    one = jax.ShapeDtypeStruct((units, 128), F32)
    return pl.pallas_call(
        table_kernel,
        in_specs=[SMEM] + [pl.BlockSpec(memory_space=pltpu.HBM)] * 4,
        out_specs=[VMEM] * 3,
        out_shape=[
            one,
            one,
            jax.ShapeDtypeStruct((line_count, 8, 128), F32),
        ],
        scratch_shapes=[pltpu.VMEM((1, units), row.dtype) for row in rows]
        + [pltpu.SemaphoreType.DMA((4,))],
        compiler_params=params(16),
        name="unit_tables",
    )(place, *(pltpu.with_memory_space_constraint(x, pltpu.HBM) for x in rows))


def load_kernel(ptdf_ref, load_ref, flow_ref, kept_ref, pair_ref):
    step = pl.program_id(0)

    @pl.when(step == 0)
    def _():
        high, low = halves(load_ref[...])
        pair_ref[:, :128] = high
        pair_ref[:, 128:] = low

    for start in range(0, KEPT, PART):
        count = min(PART, KEPT - start)

        @pl.when(step == start // PART)
        def _(start=start, count=count):
            kept_ref[start : start + count, :] = ptdf_ref[:count, :]

    rows = row_index(ptdf_ref.shape, step * PART)
    ptdf = jnp.where(rows < LINES_DEV, ptdf_ref[...], jnp.where(rows == LINES_DEV, 1.0, 0.0))
    high, low = halves(ptdf)
    both = dot(high, pair_ref[...])
    flow_ref[...] = both[:, :128] + both[:, 128:] + dot(low, pair_ref[:, :128])


def load_flows(ptdf, load):
    buses = ptdf.shape[1]
    return pl.pallas_call(
        load_kernel,
        grid=(2 * HALF // PART,),
        in_specs=[
            pl.BlockSpec((PART, buses), lambda i: (i, 0)),
            pl.BlockSpec((buses, 128), lambda i: (0, 0)),
        ],
        out_specs=[
            pl.BlockSpec((PART, 128), lambda i: (i, 0)),
            pl.BlockSpec((KEPT, buses), lambda i: (0, 0)),
        ],
        out_shape=[
            jax.ShapeDtypeStruct((2 * HALF, 128), F32),
            jax.ShapeDtypeStruct((KEPT, buses), F32),
        ],
        scratch_shapes=[pltpu.VMEM((buses, 256), BF16)],
        compiler_params=params(40),
        cost_estimate=cost_of(3 * 2 * ROWS * buses * 128, 4 * ROWS * buses),
        name="load_flows",
    )(*(pltpu.with_memory_space_constraint(x, pltpu.HBM) for x in (ptdf, load)))


def first_kernel(
    core_ref, ptdf_in, load_in, kept_ref, unit_ref, mine_ref, other_ref, rest_ref, load_ref, flow_ref, arrived
):
    load = pltpu.make_async_copy(load_in, load_ref, arrived.at[0])
    load.start()
    rest_rows = ptdf_in.at[pl.ds(KEPT, LINES_DEV - KEPT), :]
    copy = pltpu.make_async_copy(rest_rows, rest_ref, arrived.at[1])
    copy.start()
    peers, buses = unit_ref.shape[0], ptdf_in.shape[1]
    span, units = buses // peers, 32
    lane = lax.broadcasted_iota(jnp.int32, (units, 128), 1)
    tiles = [jnp.zeros((units, 128), F32)] * (buses // 128)
    for peer in range(peers):
        spots = column(unit_ref[peer][0:1, :units]).astype(jnp.int32)
        extrap = column(unit_ref[peer][1:2, :units])
        for tile in range(peer * span // 128, ((peer + 1) * span - 1) // 128 + 1):
            tiles[tile] += jnp.where(lane + tile * 128 == spots, extrap, 0.0)
    injection = jnp.concatenate(
        [jnp.sum(tile, axis=0, keepdims=True) for tile in tiles], axis=1
    )
    load.wait()
    flow_ref[:KEPT, :] = jnp.sum(kept_ref[...] * injection, axis=1, keepdims=True) - load_ref[:KEPT, :]
    total = jnp.sum(injection, axis=1, keepdims=True)
    end = row_index((2 * HALF - LINES_DEV, 128), LINES_DEV)
    flow_ref[LINES_DEV:, :] = jnp.where(end == LINES_DEV, total, 0.0) - load_ref[LINES_DEV:, :]
    copy.wait()
    rest = jnp.sum(rest_ref[...] * injection, axis=1, keepdims=True)
    flow_ref[KEPT:LINES_DEV, :] = rest - load_ref[KEPT:LINES_DEV, :]
    core = core_ref[0]
    for ref, place in ((other_ref, 1 - core), (mine_ref, core)):
        ref[...] = flow_ref[pl.ds(pl.multiple_of(place * HALF, 8), HALF), :]


def first_flows(core, ptdf, kept, unit_rows, load):
    half = jax.ShapeDtypeStruct((HALF, 128), F32)
    return pl.pallas_call(
        first_kernel,
        in_specs=[SMEM] + [pl.BlockSpec(memory_space=pltpu.HBM)] * 2 + [VMEM, VMEM],
        out_specs=[VMEM, VMEM],
        out_shape=[half, half],
        scratch_shapes=[
            pltpu.VMEM((LINES_DEV - KEPT, ptdf.shape[1]), F32),
            pltpu.VMEM((2 * HALF, 128), F32),
            pltpu.VMEM((2 * HALF, 128), F32),
            pltpu.SemaphoreType.DMA((2,)),
        ],
        compiler_params=params(24),
        cost_estimate=cost_of(2 * ROWS * ptdf.shape[1], 4 * ROWS * ptdf.shape[1]),
        name="first_flows",
    )(
        core,
        pltpu.with_memory_space_constraint(ptdf, pltpu.HBM),
        pltpu.with_memory_space_constraint(load, pltpu.HBM),
        kept,
        unit_rows,
    )


def columns_kernel(part, ptdf_ref, unit_ref, out_ref, pick_ref):
    step = pl.program_id(0)
    peers = unit_ref.shape[0]
    span = ptdf_ref.shape[1] // 2
    units = out_ref.shape[1] // 2
    local = units * 2 // peers

    @pl.when(step == 0)
    def _():
        for peer in range(peers):
            group, place = divmod(peer, peers // 2)
            spots = column(unit_ref[peer][0:1, :local]).astype(jnp.int32)
            index = lax.broadcasted_iota(jnp.int32, (local, span), 1) + group * span
            pick = jnp.where(index == spots, 1.0, 0.0).astype(BF16)
            pick_ref[group, place * local : (place + 1) * local, :] = pick

    rows = row_index((BLOCK, units), step * BLOCK)
    inside = row_index((BLOCK, span), step * BLOCK) < LINES_DEV
    for group in range(2):
        ptdf = jnp.where(inside, ptdf_ref[:, group * span : (group + 1) * span], 0.0)
        value = dot(halves(ptdf)[part], pick_ref[group], ((1,), (1,)))
        if part == 0:
            value = jnp.where(rows == LINES_DEV, 1.0, value)
        out_ref[:, group * units : (group + 1) * units] = value.astype(BF16)


def unit_columns(part, ptdf, unit_rows, units):
    buses = ptdf.shape[1]
    return pl.pallas_call(
        functools.partial(columns_kernel, part),
        grid=(ROWS // BLOCK,),
        in_specs=[
            pl.BlockSpec((BLOCK, buses), lambda i: (i, 0)),
            pl.BlockSpec(unit_rows.shape, lambda i: (0, 0, 0)),
        ],
        out_specs=pl.BlockSpec((BLOCK, units), lambda i: (i, 0)),
        out_shape=jax.ShapeDtypeStruct((ROWS, units), BF16),
        scratch_shapes=[pltpu.VMEM((2, units // 2, buses // 2), BF16)],
        compiler_params=params(48),
        cost_estimate=cost_of(2 * ROWS * buses * units // 2, 4 * ROWS * buses),
        name="unit_columns",
    )(ptdf, unit_rows)


def flow_kernel(place_ref, high_ref, low_ref, extrap_ref, flow_ref):
    high, low = halves(extrap_ref[...])
    pair = jnp.concatenate([high, low], axis=1)
    rows = pl.ds(pl.multiple_of(place_ref[0] * HALF, 16), HALF)
    both = dot(high_ref[rows, :], pair)
    flow_ref[...] = both[:, :128] + both[:, 128:] + dot(low_ref[rows, :], high)


def unit_flows(place, high, low, extrap):
    return pl.pallas_call(
        flow_kernel,
        in_specs=[SMEM] + [VMEM] * 3,
        out_specs=VMEM,
        out_shape=jax.ShapeDtypeStruct((HALF, 128), F32),
        compiler_params=params(8),
        cost_estimate=cost_of(3 * 2 * HALF * 512 * 128, 4 * HALF * 512),
        name="unit_flows",
    )(place, high, low, extrap)


def dual_kernel(*refs):
    count = len(CHUNKS)
    lefts, rights = refs[:count], refs[count : 2 * count]
    flow_ref, dual_ref, step_ref, limit_ref, dual_out, *flow_out = refs[2 * count :]
    for chunk, ends in enumerate(CHUNKS):
        rows = slice(*ends)
        flow = flow_ref[rows, :] + (lefts[chunk][...] + rights[chunk][...])
        for ref in flow_out:
            ref[rows, :] = flow
        moved = dual_ref[rows, :] + step_ref[rows, :] * flow
        limit = limit_ref[rows, :]
        dual_out[rows, :] = moved - jnp.clip(moved, -limit, limit)


def dual_step(lefts, rights, flow, dual, steps, limits, outputs):
    half = jax.ShapeDtypeStruct((HALF, 128), F32)
    return pl.pallas_call(
        dual_kernel,
        in_specs=[VMEM] * (4 + 2 * len(lefts)),
        out_specs=[VMEM] * outputs,
        out_shape=[half] * outputs,
        compiler_params=params(8),
        name="dual_step",
    )(*lefts, *rights, flow, dual, steps, limits)


def price_kernel(place_ref, dual_ref, high_ref, low_ref, *refs):
    rows = pl.ds(pl.multiple_of(place_ref[0] * HALF, 16), HALF)
    high, low = halves(dual_ref[...].T)
    both = dot(jnp.concatenate([high, low], axis=0), high_ref[rows, :])
    price = both[:128] + both[128:] + dot(high, low_ref[rows, :])
    if len(refs) == 2:
        refs[1][...] = (refs[0][...] + price).T
    else:
        refs[0][...] = price


def unit_prices(place, dual, high, low, *part):
    units = high.shape[1]
    return pl.pallas_call(
        price_kernel,
        in_specs=[SMEM] + [VMEM] * (3 + len(part)),
        out_specs=VMEM,
        out_shape=jax.ShapeDtypeStruct((units, 128) if part else (128, units), F32),
        compiler_params=params(8),
        cost_estimate=cost_of(3 * 2 * HALF * 512 * 128, 4 * HALF * 512),
        name="unit_prices",
    )(place, dual, high, low, *part)


def joined_kernel(core_ref, mine_ref, other_ref, dual_ref):
    first = core_ref[0] == 0
    mine, other = mine_ref[...], other_ref[...]
    dual_ref[:HALF, :] = jnp.where(first, mine, other)
    rest = LINES_DEV - HALF
    dual_ref[HALF:, :] = jnp.where(first, other[:rest], mine[:rest])


def joined(core, mine, other):
    return pl.pallas_call(
        joined_kernel,
        in_specs=[SMEM, VMEM, VMEM],
        out_specs=VMEM,
        out_shape=jax.ShapeDtypeStruct((LINES_DEV, 128), F32),
        compiler_params=params(8),
        name="joined",
    )(core, mine, other)


def unit_kernel(price_ref, gen_ref, old_ref, state_ref, table_ref, gen_out, extrap_ref, copies_ref):
    cost = table_ref[:, 0:1]
    lower = table_ref[:, 1:2]
    upper = table_ref[:, 2:3]
    gen = gen_ref[...]
    gradient = cost + jnp.sum(price_ref[...], axis=0) + state_ref[...]
    updated = jnp.clip(gen - PRIMAL_STEP * gradient, lower, upper)
    extrap = 2.0 * updated - gen
    gen_out[...] = updated
    extrap_ref[...] = extrap
    copies_ref[...] = jnp.broadcast_to((extrap - old_ref[...])[None], copies_ref.shape)


def unit_step(prices, gen, old, state, table):
    one = jax.ShapeDtypeStruct(gen.shape, F32)
    return pl.pallas_call(
        unit_kernel,
        in_specs=[VMEM] * 5,
        out_specs=[VMEM] * 3,
        out_shape=[one, one, jax.ShapeDtypeStruct(prices.shape, F32)],
        compiler_params=params(8),
        name="unit_step",
    )(prices, gen, old, state, table)


def state_kernel(place_ref, own_ref, far_ref, ramp_ref, store_ref, table_ref, ramp_out, store_out, state_ref):
    ramp_limit = DUAL_STEP * table_ref[:, 3:4]
    storage = table_ref[:, 4:5]
    store_limit = DUAL_STEP * table_ref[:, 5:6]
    first = place_ref[0] == 0
    own, far = own_ref[...], far_ref[...]
    extrap = jnp.concatenate([jnp.where(first, own, far), jnp.where(first, far, own)], axis=1)
    hour = lax.broadcasted_iota(jnp.int32, extrap.shape, 1)
    hours = extrap.shape[1]
    previous = pltpu.roll(extrap, 1, 1)
    moved = ramp_ref[...] + jnp.where(hour >= 1, DUAL_STEP * (extrap - previous), 0.0)
    ramp = moved - jnp.clip(moved, -ramp_limit, ramp_limit)
    ramp_out[...] = ramp
    early = lax.broadcasted_iota(jnp.int32, (hours, hours), 0)
    late = lax.broadcasted_iota(jnp.int32, (hours, hours), 1)
    forward = jnp.where(early <= late, 1.0, 0.0)
    backward = jnp.where(early >= late, 1.0, 0.0)
    running = jnp.dot(extrap, forward, precision=lax.Precision.HIGHEST, preferred_element_type=F32)
    moved = store_ref[...] + DUAL_STEP * storage * running
    store = moved - jnp.clip(moved, -store_limit, store_limit)
    store_out[...] = store
    suffix = jnp.dot(store, backward, precision=lax.Precision.HIGHEST, preferred_element_type=F32)
    after = jnp.where(hour < hours - 1, pltpu.roll(ramp, hours - 1, 1), 0.0)
    state = ramp - after + storage * suffix
    state_ref[...] = jnp.where(first, state[:, :128], state[:, 128:])


def state_step(place, own, far, ramp, store, table):
    wide = jax.ShapeDtypeStruct(ramp.shape, F32)
    return pl.pallas_call(
        state_kernel,
        in_specs=[SMEM] + [VMEM] * 5,
        out_specs=[VMEM] * 3,
        out_shape=[wide, wide, jax.ShapeDtypeStruct(own.shape, F32)],
        compiler_params=params(8),
        cost_estimate=cost_of(12 * 2 * 32 * 256 * 256, 1 << 18),
        name="state_step",
    )(place, own, far, ramp, store, table)


SWAP = ((0, 1), (1, 0))
NEAR = ((0, 1), (1, 0), (2, 3), (3, 2))
FAR = ((1, 2), (2, 1), (3, 0), (0, 3))


def along_y(value, by_core):
    pairs = [(2 * i + core, 2 * j + core) for core in range(2) for i, j in by_core[core]]
    return lax.ppermute(value, BUS, pairs)


def on_device(ptdf, bus_load, unit_bus, unit_type, unit_limit, unit_cost, line_rating):
    line_count = lax.axis_size(LINE)
    hour_dev = bus_load.shape[1]
    local = unit_bus.shape[0]
    core = lax.axis_index("c").astype(jnp.int32)
    place = lax.axis_index("t").astype(jnp.int32)[None]
    block = (lax.axis_index(BUS) * ptdf.shape[1]).astype(jnp.int32)
    table, gen, copies = unit_tables(
        block[None], unit_bus, unit_type, unit_limit, unit_cost, line_count
    )
    unit_rows = lax.all_to_all(copies, LINE, 0, 0, tiled=True)
    load, kept = load_flows(ptdf, bus_load)
    mine, other = first_flows(core[None], ptdf, kept, unit_rows, load)
    extrap = far = 2.0 * gen

    pad = jnp.zeros((2 * HALF - LINES_DEV,), F32)
    limits = jnp.concatenate([DUAL_STEP * (line_rating.astype(F32) / 100.0), pad])
    index = core * HALF + jnp.arange(HALF, dtype=jnp.int32)
    weight = 1.0 / (UNITS * 16)
    steps = jnp.where(index < LINES_DEV, DUAL_STEP, jnp.where(index == LINES_DEV, weight, 0.0))
    steps = steps.astype(F32)[:, None]
    limits = lax.dynamic_slice_in_dim(limits, core * HALF, HALF, 0)[:, None]
    core, partner = core[None], 1 - core[None]
    flow = dual = jnp.zeros((HALF, hour_dev), F32)
    ramp = store = jnp.zeros((local, 2 * hour_dev), F32)
    high = low = None
    for iteration in range(ITERS):
        last = iteration == ITERS - 1
        total = mine + lax.ppermute(other, "c", SWAP)
        if iteration == 0:
            total, tied, rows = lax.optimization_barrier((total, ptdf, unit_rows))
            high = unit_columns(0, tied, rows, line_count * local)
        elif not last:
            total, tied = lax.optimization_barrier((total, extrap))
            far = lax.ppermute(tied, "t", SWAP)
        lefts = [total[start:stop] for start, stop in CHUNKS]
        lefts = [left + along_y(left, (NEAR, FAR)) for left in lefts]
        if iteration == 0:
            lefts[1], high = lax.optimization_barrier((lefts[1], high))
            lefts[0], tied, rows = lax.optimization_barrier((lefts[0], tied, rows))
            low = unit_columns(1, tied, rows, line_count * local)
        elif not last:
            lefts[0], far = lax.optimization_barrier((lefts[0], far))
        if not last:
            ramp, store, state = state_step(place, extrap, far, ramp, store, table)
        rights = [along_y(left, (FAR, NEAR)) for left in lefts]
        if iteration == 0:
            rights[-1], low = lax.optimization_barrier((rights[-1], low))
        if last:
            (dual,) = dual_step(lefts, rights, flow, dual, steps, limits, 1)
            return gen, joined(core, dual, lax.ppermute(dual, "c", SWAP))
        rights[-1], state, ramp, store = lax.optimization_barrier((rights[-1], state, ramp, store))
        dual, flow = dual_step(lefts, rights, flow, dual, steps, limits, 2)
        prices = unit_prices(core, dual, high, low)
        prices = unit_prices(partner, lax.ppermute(dual, "c", SWAP), high, low, prices)
        prices = prices.reshape(line_count, local, hour_dev)
        prices = lax.all_to_all(prices, LINE, 0, 0, tiled=True)
        gen, extrap, copies = unit_step(prices, gen, extrap, state, table)
        changes = lax.all_to_all(copies, LINE, 0, 0, tiled=True).reshape(-1, hour_dev)
        other = unit_flows(partner, high, low, changes)
        mine = unit_flows(core, high, low, changes)


def solution(mesh):
    finer = Mesh(
        mesh.devices.reshape(8, 2, 4, 2, mesh.shape["tm"]),
        ("z", "xl", "y", "c", "t"),
    )
    return jax.shard_map(
        on_device,
        mesh=finer,
        in_specs=(
            P(LINE, BUS),
            P(BUS, "t"),
            P(LINE_BUS),
            P(LINE_BUS),
            P(LINE_BUS),
            P(LINE_BUS),
            P(LINE),
        ),
        out_specs=(P(LINE_BUS, "t"), P(LINE, "t")),
        check_vma=False,
    )
```

```python
import functools

import jax
import jax.numpy as jnp
from jax import lax
from jax.experimental import pallas as pl
from jax.experimental.pallas import tpu as pltpu
from jax.sharding import Mesh
from jax.sharding import PartitionSpec as P

UNITS = 4096
ITERS = 4
LINE = ("z", "xl")
BUS = ("y", "c")
LINE_BUS = ("z", "xl", "y", "c")

RAMP_RATES = (0.1, 0.2, 0.4, 0.5)
COST_FACTORS = (1.0, 1.5, 3.0, 0.05)
PRIMAL_STEP = 0.5
DUAL_STEP = 0.5

LINES_DEV = 960
ROWS = 1024
HALF = 496
BLOCK = 128
KEPT = 320
CHUNKS = ((0, 240), (240, HALF))
BF16 = jnp.bfloat16
F32 = jnp.float32
VMEM = pl.BlockSpec(memory_space=pltpu.VMEM)
SMEM = pl.BlockSpec(memory_space=pltpu.SMEM)


def params(mib):
    return pltpu.CompilerParams(vmem_limit_bytes=mib << 20)


def cost_of(flops, size):
    return pl.CostEstimate(flops=flops, bytes_accessed=size, transcendentals=0)


def halves(value):
    high = value.astype(BF16)
    return high, (value - high.astype(F32)).astype(BF16)


def dot(left, right, dims=((1,), (0,))):
    return lax.dot_general(left, right, (dims, ((), ())), preferred_element_type=F32)


def row_index(shape, first):
    return first + lax.broadcasted_iota(jnp.int32, shape, 0)


def picked(kinds, values):
    total = 0.0
    for kind, value in enumerate(values):
        total = total + jnp.where(kinds == kind, value, 0.0)
    return total


def column(row):
    count = row.shape[1]
    same = lax.broadcasted_iota(jnp.int32, (count, count), 0) == lax.broadcasted_iota(
        jnp.int32, (count, count), 1
    )
    return jnp.sum(jnp.where(same, row, jnp.zeros_like(row)), axis=1, keepdims=True)


def table_kernel(
    place_ref, bus_in, type_in, limit_in, cost_in, table_ref, first_ref, copies_ref,
    bus_ref, type_ref, limit_ref, cost_ref, arrived
):
    pairs = (
        (bus_in, bus_ref.at[0]),
        (type_in, type_ref.at[0]),
        (limit_in, limit_ref.at[0]),
        (cost_in, cost_ref.at[0]),
    )
    copies = [pltpu.make_async_copy(*pair, arrived.at[spot]) for spot, pair in enumerate(pairs)]
    for copy in copies:
        copy.start()
    for copy in copies:
        copy.wait()
    kinds = column(type_ref[...])
    capacity = column(limit_ref[...]).astype(F32) / 100.0
    cost = column(cost_ref[...]) * picked(kinds, COST_FACTORS)
    storage = jnp.where(kinds == 3, 1.0, 0.0)
    lower = -capacity * storage
    lane = lax.broadcasted_iota(jnp.int32, table_ref.shape, 1)
    table = jnp.zeros(table_ref.shape, F32)
    parts = (cost, lower, capacity, picked(kinds, RAMP_RATES) * capacity, storage, 2.0 * capacity)
    for spot, part in enumerate(parts):
        table = jnp.where(lane == spot, part, table)
    table_ref[...] = table
    first = jnp.clip(-PRIMAL_STEP * cost, lower, capacity)
    first_ref[...] = jnp.broadcast_to(first, first_ref.shape)
    bus = column(bus_ref[...] - place_ref[0]).astype(F32)
    same = lane == lax.broadcasted_iota(jnp.int32, table_ref.shape, 0)
    bus = jnp.sum(jnp.where(same, bus, 0.0), axis=0, keepdims=True)
    extrap = jnp.sum(jnp.where(same, 2.0 * first, 0.0), axis=0, keepdims=True)
    sent = jnp.where(lax.broadcasted_iota(jnp.int32, (8, 128), 0) == 0, bus, extrap)
    copies_ref[...] = jnp.broadcast_to(sent[None], copies_ref.shape)


def unit_tables(place, unit_bus, unit_type, unit_limit, unit_cost, line_count):
    units = unit_bus.shape[0]
    rows = (unit_bus, unit_type, unit_limit, unit_cost)
    one = jax.ShapeDtypeStruct((units, 128), F32)
    return pl.pallas_call(
        table_kernel,
        in_specs=[SMEM] + [pl.BlockSpec(memory_space=pltpu.HBM)] * 4,
        out_specs=[VMEM] * 3,
        out_shape=[
            one,
            one,
            jax.ShapeDtypeStruct((line_count, 8, 128), F32),
        ],
        scratch_shapes=[pltpu.VMEM((1, units), row.dtype) for row in rows]
        + [pltpu.SemaphoreType.DMA((4,))],
        compiler_params=params(16),
        name="unit_tables",
    )(place, *(pltpu.with_memory_space_constraint(x, pltpu.HBM) for x in rows))


def load_kernel(ptdf_ref, load_ref, flow_ref, kept_ref, pair_ref):
    step = pl.program_id(0)

    @pl.when(step == 0)
    def _():
        high, low = halves(load_ref[...])
        pair_ref[:, :128] = high
        pair_ref[:, 128:] = low

    for start in range(0, KEPT, BLOCK):
        count = min(BLOCK, KEPT - start)

        @pl.when(step == start // BLOCK)
        def _(start=start, count=count):
            kept_ref[start : start + count, :] = ptdf_ref[:count, :]

    rows = row_index(ptdf_ref.shape, step * BLOCK)
    ptdf = jnp.where(rows < LINES_DEV, ptdf_ref[...], jnp.where(rows == LINES_DEV, 1.0, 0.0))
    high, low = halves(ptdf)
    both = dot(high, pair_ref[...])
    flow_ref[...] = both[:, :128] + both[:, 128:] + dot(low, pair_ref[:, :128])


def load_flows(ptdf, load):
    buses = ptdf.shape[1]
    return pl.pallas_call(
        load_kernel,
        grid=(ROWS // BLOCK,),
        in_specs=[
            pl.BlockSpec((BLOCK, buses), lambda i: (i, 0)),
            pl.BlockSpec((buses, 128), lambda i: (0, 0)),
        ],
        out_specs=[
            pl.BlockSpec((BLOCK, 128), lambda i: (i, 0)),
            pl.BlockSpec((KEPT, buses), lambda i: (0, 0)),
        ],
        out_shape=[
            jax.ShapeDtypeStruct((ROWS, 128), F32),
            jax.ShapeDtypeStruct((KEPT, buses), F32),
        ],
        scratch_shapes=[pltpu.VMEM((buses, 256), BF16)],
        compiler_params=params(40),
        cost_estimate=cost_of(3 * 2 * ROWS * buses * 128, 4 * ROWS * buses),
        name="load_flows",
    )(*(pltpu.with_memory_space_constraint(x, pltpu.HBM) for x in (ptdf, load)))


def first_kernel(
    core_ref, ptdf_in, load_ref, kept_ref, unit_ref, mine_ref, other_ref, rest_ref, flow_ref, arrived
):
    rest_rows = ptdf_in.at[pl.ds(KEPT, LINES_DEV - KEPT), :]
    copy = pltpu.make_async_copy(rest_rows, rest_ref, arrived)
    copy.start()
    peers, buses = unit_ref.shape[0], ptdf_in.shape[1]
    span, units = buses // peers, 32
    lane = lax.broadcasted_iota(jnp.int32, (units, 128), 1)
    tiles = [jnp.zeros((units, 128), F32)] * (buses // 128)
    for peer in range(peers):
        spots = column(unit_ref[peer][0:1, :units]).astype(jnp.int32)
        extrap = column(unit_ref[peer][1:2, :units])
        for tile in range(peer * span // 128, ((peer + 1) * span - 1) // 128 + 1):
            tiles[tile] += jnp.where(lane + tile * 128 == spots, extrap, 0.0)
    injection = jnp.concatenate(
        [jnp.sum(tile, axis=0, keepdims=True) for tile in tiles], axis=1
    )
    flow_ref[:KEPT, :] = jnp.sum(kept_ref[...] * injection, axis=1, keepdims=True) - load_ref[:KEPT, :]
    total = jnp.sum(injection, axis=1, keepdims=True)
    end = row_index((2 * HALF - LINES_DEV, 128), LINES_DEV)
    flow_ref[LINES_DEV:, :] = jnp.where(end == LINES_DEV, total, 0.0) - load_ref[LINES_DEV : 2 * HALF, :]
    copy.wait()
    rest = jnp.sum(rest_ref[...] * injection, axis=1, keepdims=True)
    flow_ref[KEPT:LINES_DEV, :] = rest - load_ref[KEPT:LINES_DEV, :]
    core = core_ref[0]
    for ref, place in ((other_ref, 1 - core), (mine_ref, core)):
        ref[...] = flow_ref[pl.ds(pl.multiple_of(place * HALF, 8), HALF), :]


def first_flows(core, ptdf, kept, unit_rows, load):
    half = jax.ShapeDtypeStruct((HALF, 128), F32)
    return pl.pallas_call(
        first_kernel,
        in_specs=[SMEM, pl.BlockSpec(memory_space=pltpu.HBM)] + [VMEM] * 3,
        out_specs=[VMEM, VMEM],
        out_shape=[half, half],
        scratch_shapes=[
            pltpu.VMEM((LINES_DEV - KEPT, ptdf.shape[1]), F32),
            pltpu.VMEM((2 * HALF, 128), F32),
            pltpu.SemaphoreType.DMA(()),
        ],
        compiler_params=params(24),
        cost_estimate=cost_of(2 * ROWS * ptdf.shape[1], 4 * ROWS * ptdf.shape[1]),
        name="first_flows",
    )(
        core,
        pltpu.with_memory_space_constraint(ptdf, pltpu.HBM),
        load,
        kept,
        unit_rows,
    )


def columns_kernel(first, ptdf_ref, unit_ref, *refs):
    high_ref, low_ref, pick_ref = refs[-3:]
    step = pl.program_id(0)
    peers = unit_ref.shape[0]
    span = ptdf_ref.shape[1] // 2
    units = high_ref.shape[1] // 2
    local = units * 2 // peers

    @pl.when(step == 0)
    def _():
        for peer in range(peers):
            group, place = divmod(peer, peers // 2)
            spots = column(unit_ref[peer][0:1, :local]).astype(jnp.int32)
            index = lax.broadcasted_iota(jnp.int32, (local, span), 1) + group * span
            pick = jnp.where(index == spots, 1.0, 0.0).astype(BF16)
            pick_ref[group, place * local : (place + 1) * local, :] = pick

    rows = row_index((BLOCK, units), (first + step) * BLOCK)
    inside = row_index((BLOCK, span), (first + step) * BLOCK) < LINES_DEV
    for group in range(2):
        ptdf = jnp.where(inside, ptdf_ref[:, group * span : (group + 1) * span], 0.0)
        high, low = halves(ptdf)
        pick = pick_ref[group]
        high = dot(high, pick, ((1,), (1,)))
        low = dot(low, pick, ((1,), (1,)))
        where = slice(group * units, (group + 1) * units)
        high_ref[:, where] = jnp.where(rows == LINES_DEV, 1.0, high).astype(BF16)
        low_ref[:, where] = low.astype(BF16)


def unit_columns(ptdf, unit_rows, units, *begun):
    buses = ptdf.shape[1]
    count = ROWS // BLOCK // 2
    first = count if begun else 0
    by_row = pl.BlockSpec((BLOCK, units), lambda i: (first + i, 0))
    return pl.pallas_call(
        functools.partial(columns_kernel, first),
        grid=(count,),
        in_specs=[
            pl.BlockSpec((BLOCK, buses), lambda i: (first + i, 0)),
            pl.BlockSpec(unit_rows.shape, lambda i: (0, 0, 0)),
        ]
        + [pl.BlockSpec(memory_space=pl.ANY)] * len(begun),
        out_specs=[by_row, by_row],
        out_shape=[jax.ShapeDtypeStruct((ROWS, units), BF16)] * 2,
        scratch_shapes=[pltpu.VMEM((2, units // 2, buses // 2), BF16)],
        input_output_aliases={2: 0, 3: 1} if begun else {},
        compiler_params=params(48),
        cost_estimate=cost_of(2 * ROWS * buses * units // 2, 2 * ROWS * buses),
        name="unit_columns",
    )(pltpu.with_memory_space_constraint(ptdf, pltpu.HBM), unit_rows, *begun)


def flow_kernel(place_ref, high_ref, low_ref, extrap_ref, flow_ref):
    high, low = halves(extrap_ref[...])
    pair = jnp.concatenate([high, low], axis=1)
    rows = pl.ds(pl.multiple_of(place_ref[0] * HALF, 16), HALF)
    both = dot(high_ref[rows, :], pair)
    flow_ref[...] = both[:, :128] + both[:, 128:] + dot(low_ref[rows, :], high)


def unit_flows(place, high, low, extrap):
    return pl.pallas_call(
        flow_kernel,
        in_specs=[SMEM] + [VMEM] * 3,
        out_specs=VMEM,
        out_shape=jax.ShapeDtypeStruct((HALF, 128), F32),
        compiler_params=params(8),
        cost_estimate=cost_of(3 * 2 * HALF * 512 * 128, 4 * HALF * 512),
        name="unit_flows",
    )(place, high, low, extrap)


def dual_kernel(*refs):
    count = len(CHUNKS)
    lefts, rights = refs[:count], refs[count : 2 * count]
    flow_ref, dual_ref, step_ref, limit_ref, dual_out, *flow_out = refs[2 * count :]
    for chunk, ends in enumerate(CHUNKS):
        rows = slice(*ends)
        flow = flow_ref[rows, :] + (lefts[chunk][...] + rights[chunk][...])
        for ref in flow_out:
            ref[rows, :] = flow
        moved = dual_ref[rows, :] + step_ref[rows, :] * flow
        limit = limit_ref[rows, :]
        dual_out[rows, :] = moved - jnp.clip(moved, -limit, limit)


def dual_step(lefts, rights, flow, dual, steps, limits, outputs):
    half = jax.ShapeDtypeStruct((HALF, 128), F32)
    return pl.pallas_call(
        dual_kernel,
        in_specs=[VMEM] * (4 + 2 * len(lefts)),
        out_specs=[VMEM] * outputs,
        out_shape=[half] * outputs,
        compiler_params=params(8),
        name="dual_step",
    )(*lefts, *rights, flow, dual, steps, limits)


def price_kernel(place_ref, dual_ref, high_ref, low_ref, *refs):
    rows = pl.ds(pl.multiple_of(place_ref[0] * HALF, 16), HALF)
    high, low = halves(dual_ref[...].T)
    both = dot(jnp.concatenate([high, low], axis=0), high_ref[rows, :])
    price = both[:128] + both[128:] + dot(high, low_ref[rows, :])
    if len(refs) == 2:
        refs[1][...] = (refs[0][...] + price).T
    else:
        refs[0][...] = price


def unit_prices(place, dual, high, low, *part):
    units = high.shape[1]
    return pl.pallas_call(
        price_kernel,
        in_specs=[SMEM] + [VMEM] * (3 + len(part)),
        out_specs=VMEM,
        out_shape=jax.ShapeDtypeStruct((units, 128) if part else (128, units), F32),
        compiler_params=params(8),
        cost_estimate=cost_of(3 * 2 * HALF * 512 * 128, 4 * HALF * 512),
        name="unit_prices",
    )(place, dual, high, low, *part)


def joined_kernel(core_ref, mine_ref, other_ref, dual_ref):
    first = core_ref[0] == 0
    mine, other = mine_ref[...], other_ref[...]
    dual_ref[:HALF, :] = jnp.where(first, mine, other)
    rest = LINES_DEV - HALF
    dual_ref[HALF:, :] = jnp.where(first, other[:rest], mine[:rest])


def joined(core, mine, other):
    return pl.pallas_call(
        joined_kernel,
        in_specs=[SMEM, VMEM, VMEM],
        out_specs=VMEM,
        out_shape=jax.ShapeDtypeStruct((LINES_DEV, 128), F32),
        compiler_params=params(8),
        name="joined",
    )(core, mine, other)


def unit_kernel(price_ref, gen_ref, old_ref, state_ref, table_ref, gen_out, extrap_ref, copies_ref):
    cost = table_ref[:, 0:1]
    lower = table_ref[:, 1:2]
    upper = table_ref[:, 2:3]
    gen = gen_ref[...]
    gradient = cost + jnp.sum(price_ref[...], axis=0) + state_ref[...]
    updated = jnp.clip(gen - PRIMAL_STEP * gradient, lower, upper)
    extrap = 2.0 * updated - gen
    gen_out[...] = updated
    extrap_ref[...] = extrap
    copies_ref[...] = jnp.broadcast_to((extrap - old_ref[...])[None], copies_ref.shape)


def unit_step(prices, gen, old, state, table):
    one = jax.ShapeDtypeStruct(gen.shape, F32)
    return pl.pallas_call(
        unit_kernel,
        in_specs=[VMEM] * 5,
        out_specs=[VMEM] * 3,
        out_shape=[one, one, jax.ShapeDtypeStruct(prices.shape, F32)],
        compiler_params=params(8),
        name="unit_step",
    )(prices, gen, old, state, table)


def state_kernel(place_ref, own_ref, far_ref, ramp_ref, store_ref, table_ref, ramp_out, store_out, state_ref):
    ramp_limit = DUAL_STEP * table_ref[:, 3:4]
    storage = table_ref[:, 4:5]
    store_limit = DUAL_STEP * table_ref[:, 5:6]
    first = place_ref[0] == 0
    own, far = own_ref[...], far_ref[...]
    extrap = jnp.concatenate([jnp.where(first, own, far), jnp.where(first, far, own)], axis=1)
    hour = lax.broadcasted_iota(jnp.int32, extrap.shape, 1)
    hours = extrap.shape[1]
    previous = pltpu.roll(extrap, 1, 1)
    moved = ramp_ref[...] + jnp.where(hour >= 1, DUAL_STEP * (extrap - previous), 0.0)
    ramp = moved - jnp.clip(moved, -ramp_limit, ramp_limit)
    ramp_out[...] = ramp
    early = lax.broadcasted_iota(jnp.int32, (hours, hours), 0)
    late = lax.broadcasted_iota(jnp.int32, (hours, hours), 1)
    forward = jnp.where(early <= late, 1.0, 0.0)
    backward = jnp.where(early >= late, 1.0, 0.0)
    running = jnp.dot(extrap, forward, precision=lax.Precision.HIGHEST, preferred_element_type=F32)
    moved = store_ref[...] + DUAL_STEP * storage * running
    store = moved - jnp.clip(moved, -store_limit, store_limit)
    store_out[...] = store
    suffix = jnp.dot(store, backward, precision=lax.Precision.HIGHEST, preferred_element_type=F32)
    after = jnp.where(hour < hours - 1, pltpu.roll(ramp, hours - 1, 1), 0.0)
    state = ramp - after + storage * suffix
    state_ref[...] = jnp.where(first, state[:, :128], state[:, 128:])


def state_step(place, own, far, ramp, store, table):
    wide = jax.ShapeDtypeStruct(ramp.shape, F32)
    return pl.pallas_call(
        state_kernel,
        in_specs=[SMEM] + [VMEM] * 5,
        out_specs=[VMEM] * 3,
        out_shape=[wide, wide, jax.ShapeDtypeStruct(own.shape, F32)],
        compiler_params=params(8),
        cost_estimate=cost_of(12 * 2 * 32 * 256 * 256, 1 << 18),
        name="state_step",
    )(place, own, far, ramp, store, table)


SWAP = ((0, 1), (1, 0))
NEAR = ((0, 1), (1, 0), (2, 3), (3, 2))
FAR = ((1, 2), (2, 1), (3, 0), (0, 3))


def along_y(value, by_core):
    pairs = [(2 * i + core, 2 * j + core) for core in range(2) for i, j in by_core[core]]
    return lax.ppermute(value, BUS, pairs)


def on_device(ptdf, bus_load, unit_bus, unit_type, unit_limit, unit_cost, line_rating):
    line_count = lax.axis_size(LINE)
    hour_dev = bus_load.shape[1]
    local = unit_bus.shape[0]
    core = lax.axis_index("c").astype(jnp.int32)
    place = lax.axis_index("t").astype(jnp.int32)[None]
    block = (lax.axis_index(BUS) * ptdf.shape[1]).astype(jnp.int32)
    table, gen, copies = unit_tables(
        block[None], unit_bus, unit_type, unit_limit, unit_cost, line_count
    )
    unit_rows = lax.all_to_all(copies, LINE, 0, 0, tiled=True)
    load, kept = load_flows(ptdf, bus_load)
    mine, other = first_flows(core[None], ptdf, kept, unit_rows, load)
    extrap = far = 2.0 * gen

    pad = jnp.zeros((2 * HALF - LINES_DEV,), F32)
    limits = jnp.concatenate([DUAL_STEP * (line_rating.astype(F32) / 100.0), pad])
    index = core * HALF + jnp.arange(HALF, dtype=jnp.int32)
    weight = 1.0 / (UNITS * 16)
    steps = jnp.where(index < LINES_DEV, DUAL_STEP, jnp.where(index == LINES_DEV, weight, 0.0))
    steps = steps.astype(F32)[:, None]
    limits = lax.dynamic_slice_in_dim(limits, core * HALF, HALF, 0)[:, None]
    core, partner = core[None], 1 - core[None]
    flow = dual = jnp.zeros((HALF, hour_dev), F32)
    ramp = store = jnp.zeros((local, 2 * hour_dev), F32)
    high = low = None
    for iteration in range(ITERS):
        last = iteration == ITERS - 1
        total = mine + lax.ppermute(other, "c", SWAP)
        if iteration == 0:
            ramp, store, state = state_step(place, extrap, far, ramp, store, table)
            total, tied, rows, state = lax.optimization_barrier((total, ptdf, unit_rows, state))
            high, low = unit_columns(tied, rows, line_count * local)
        elif not last:
            total, tied = lax.optimization_barrier((total, extrap))
            far = lax.ppermute(tied, "t", SWAP)
        lefts = [total[start:stop] for start, stop in CHUNKS]
        lefts = [left + along_y(left, (NEAR, FAR)) for left in lefts]
        if iteration == 0:
            lefts[0], high, low = lax.optimization_barrier((lefts[0], high, low))
            high, low = unit_columns(tied, rows, line_count * local, high, low)
        elif not last:
            lefts[0], far = lax.optimization_barrier((lefts[0], far))
        if 0 < iteration < ITERS - 1:
            ramp, store, state = state_step(place, extrap, far, ramp, store, table)
        rights = [along_y(left, (FAR, NEAR)) for left in lefts]
        if iteration == 0:
            rights[-1], high, low = lax.optimization_barrier((rights[-1], high, low))
        if last:
            (dual,) = dual_step(lefts, rights, flow, dual, steps, limits, 1)
            return gen, joined(core, dual, lax.ppermute(dual, "c", SWAP))
        rights[-1], state, ramp, store = lax.optimization_barrier((rights[-1], state, ramp, store))
        dual, flow = dual_step(lefts, rights, flow, dual, steps, limits, 2)
        prices = unit_prices(core, dual, high, low)
        prices = unit_prices(partner, lax.ppermute(dual, "c", SWAP), high, low, prices)
        prices = prices.reshape(line_count, local, hour_dev)
        prices = lax.all_to_all(prices, LINE, 0, 0, tiled=True)
        gen, extrap, copies = unit_step(prices, gen, extrap, state, table)
        changes = lax.all_to_all(copies, LINE, 0, 0, tiled=True).reshape(-1, hour_dev)
        other = unit_flows(partner, high, low, changes)
        mine = unit_flows(core, high, low, changes)


def solution(mesh):
    finer = Mesh(
        mesh.devices.reshape(8, 2, 4, 2, mesh.shape["tm"]),
        ("z", "xl", "y", "c", "t"),
    )
    return jax.shard_map(
        on_device,
        mesh=finer,
        in_specs=(
            P(LINE, BUS),
            P(BUS, "t"),
            P(LINE_BUS),
            P(LINE_BUS),
            P(LINE_BUS),
            P(LINE_BUS),
            P(LINE),
        ),
        out_specs=(P(LINE_BUS, "t"), P(LINE, "t")),
        check_vma=False,
    )
```

```python
import functools

import jax
import jax.numpy as jnp
from jax import lax
from jax.experimental import pallas as pl
from jax.experimental.pallas import tpu as pltpu
from jax.sharding import Mesh
from jax.sharding import PartitionSpec as P

UNITS = 4096
ITERS = 4
LINE = ("z", "xl")
BUS = ("y", "c")
LINE_BUS = ("z", "xl", "y", "c")

RAMP_RATES = (0.1, 0.2, 0.4, 0.5)
COST_FACTORS = (1.0, 1.5, 3.0, 0.05)
PRIMAL_STEP = 0.5
DUAL_STEP = 0.5

LINES_DEV = 960
ROWS = 1024
HALF = 496
BLOCK = 512
KEPT = 320
CHUNKS = ((0, 240), (240, HALF))
BF16 = jnp.bfloat16
F32 = jnp.float32
VMEM = pl.BlockSpec(memory_space=pltpu.VMEM)
SMEM = pl.BlockSpec(memory_space=pltpu.SMEM)


def params(mib):
    return pltpu.CompilerParams(vmem_limit_bytes=mib << 20)


def cost_of(flops, size):
    return pl.CostEstimate(flops=flops, bytes_accessed=size, transcendentals=0)


def halves(value):
    high = value.astype(BF16)
    return high, (value - high.astype(F32)).astype(BF16)


def dot(left, right, dims=((1,), (0,))):
    return lax.dot_general(left, right, (dims, ((), ())), preferred_element_type=F32)


def row_index(shape, first):
    return first + lax.broadcasted_iota(jnp.int32, shape, 0)


def picked(kinds, values):
    total = 0.0
    for kind, value in enumerate(values):
        total = total + jnp.where(kinds == kind, value, 0.0)
    return total


def column(row):
    count = row.shape[1]
    same = lax.broadcasted_iota(jnp.int32, (count, count), 0) == lax.broadcasted_iota(
        jnp.int32, (count, count), 1
    )
    return jnp.sum(jnp.where(same, row, jnp.zeros_like(row)), axis=1, keepdims=True)


def table_kernel(
    place_ref, bus_in, type_in, limit_in, cost_in, table_ref, first_ref, copies_ref,
    bus_ref, type_ref, limit_ref, cost_ref, arrived
):
    pairs = (
        (bus_in, bus_ref.at[0]),
        (type_in, type_ref.at[0]),
        (limit_in, limit_ref.at[0]),
        (cost_in, cost_ref.at[0]),
    )
    copies = [pltpu.make_async_copy(*pair, arrived.at[spot]) for spot, pair in enumerate(pairs)]
    for copy in copies:
        copy.start()
    for copy in copies:
        copy.wait()
    kinds = column(type_ref[...])
    capacity = column(limit_ref[...]).astype(F32) / 100.0
    cost = column(cost_ref[...]) * picked(kinds, COST_FACTORS)
    storage = jnp.where(kinds == 3, 1.0, 0.0)
    lower = -capacity * storage
    lane = lax.broadcasted_iota(jnp.int32, table_ref.shape, 1)
    table = jnp.zeros(table_ref.shape, F32)
    parts = (cost, lower, capacity, picked(kinds, RAMP_RATES) * capacity, storage, 2.0 * capacity)
    for spot, part in enumerate(parts):
        table = jnp.where(lane == spot, part, table)
    table_ref[...] = table
    first = jnp.clip(-PRIMAL_STEP * cost, lower, capacity)
    first_ref[...] = jnp.broadcast_to(first, first_ref.shape)
    bus = column(bus_ref[...] - place_ref[0]).astype(F32)
    same = lane == lax.broadcasted_iota(jnp.int32, table_ref.shape, 0)
    bus = jnp.sum(jnp.where(same, bus, 0.0), axis=0, keepdims=True)
    extrap = jnp.sum(jnp.where(same, 2.0 * first, 0.0), axis=0, keepdims=True)
    sent = jnp.where(lax.broadcasted_iota(jnp.int32, (8, 128), 0) == 0, bus, extrap)
    copies_ref[...] = jnp.broadcast_to(sent[None], copies_ref.shape)


def unit_tables(place, unit_bus, unit_type, unit_limit, unit_cost, line_count):
    units = unit_bus.shape[0]
    rows = (unit_bus, unit_type, unit_limit, unit_cost)
    one = jax.ShapeDtypeStruct((units, 128), F32)
    return pl.pallas_call(
        table_kernel,
        in_specs=[SMEM] + [pl.BlockSpec(memory_space=pltpu.HBM)] * 4,
        out_specs=[VMEM] * 3,
        out_shape=[
            one,
            one,
            jax.ShapeDtypeStruct((line_count, 8, 128), F32),
        ],
        scratch_shapes=[pltpu.VMEM((1, units), row.dtype) for row in rows]
        + [pltpu.SemaphoreType.DMA((4,))],
        compiler_params=params(16),
        name="unit_tables",
    )(place, *(pltpu.with_memory_space_constraint(x, pltpu.HBM) for x in rows))


def load_kernel(ptdf_ref, load_ref, flow_ref, kept_ref):
    step = pl.program_id(0)
    ptdf, load = ptdf_ref[...], load_ref[...]
    kept_ref[...] = ptdf[:KEPT]
    high, low = halves(load)
    ptdf_high, ptdf_low = halves(ptdf)
    both = dot(ptdf_high, jnp.concatenate([high, low], axis=1))
    flow = both[:, :128] + both[:, 128:] + dot(ptdf_low, high)
    total = jnp.sum(load, axis=0, keepdims=True)
    end = row_index((2 * HALF - LINES_DEV, 128), LINES_DEV) == LINES_DEV
    total = jnp.where(end, total, 0.0)

    @pl.when(step == 0)
    def _():
        flow_ref[:LINES_DEV, :] = flow
        flow_ref[LINES_DEV:, :] = total

    @pl.when(step > 0)
    def _():
        flow_ref[:LINES_DEV, :] += flow
        flow_ref[LINES_DEV:, :] += total


def load_flows(ptdf, load):
    lines, buses = ptdf.shape
    return pl.pallas_call(
        load_kernel,
        grid=(buses // BLOCK,),
        in_specs=[
            pl.BlockSpec((lines, BLOCK), lambda i: (0, i)),
            pl.BlockSpec((BLOCK, 128), lambda i: (i, 0)),
        ],
        out_specs=[
            pl.BlockSpec((2 * HALF, 128), lambda i: (0, 0)),
            pl.BlockSpec((KEPT, BLOCK), lambda i: (0, i)),
        ],
        out_shape=[
            jax.ShapeDtypeStruct((2 * HALF, 128), F32),
            jax.ShapeDtypeStruct((KEPT, buses), F32),
        ],
        compiler_params=params(40),
        cost_estimate=cost_of(3 * 2 * ROWS * buses * 128, 4 * ROWS * buses),
        name="load_flows",
    )(*(pltpu.with_memory_space_constraint(x, pltpu.HBM) for x in (ptdf, load)))


def first_kernel(
    core_ref, ptdf_in, load_ref, kept_ref, unit_ref, mine_ref, other_ref, rest_ref, flow_ref, arrived
):
    rest_rows = ptdf_in.at[pl.ds(KEPT, LINES_DEV - KEPT), :]
    copy = pltpu.make_async_copy(rest_rows, rest_ref, arrived)
    copy.start()
    peers, buses = unit_ref.shape[0], ptdf_in.shape[1]
    span, units = buses // peers, 32
    lane = lax.broadcasted_iota(jnp.int32, (units, 128), 1)
    tiles = [jnp.zeros((units, 128), F32)] * (buses // 128)
    for peer in range(peers):
        spots = column(unit_ref[peer][0:1, :units]).astype(jnp.int32)
        extrap = column(unit_ref[peer][1:2, :units])
        for tile in range(peer * span // 128, ((peer + 1) * span - 1) // 128 + 1):
            tiles[tile] += jnp.where(lane + tile * 128 == spots, extrap, 0.0)
    injection = jnp.concatenate(
        [jnp.sum(tile, axis=0, keepdims=True) for tile in tiles], axis=1
    )
    flow_ref[:KEPT, :] = jnp.sum(kept_ref[...] * injection, axis=1, keepdims=True) - load_ref[:KEPT, :]
    total = jnp.sum(injection, axis=1, keepdims=True)
    end = row_index((2 * HALF - LINES_DEV, 128), LINES_DEV)
    flow_ref[LINES_DEV:, :] = jnp.where(end == LINES_DEV, total, 0.0) - load_ref[LINES_DEV:, :]
    copy.wait()
    rest = jnp.sum(rest_ref[...] * injection, axis=1, keepdims=True)
    flow_ref[KEPT:LINES_DEV, :] = rest - load_ref[KEPT:LINES_DEV, :]
    core = core_ref[0]
    for ref, place in ((other_ref, 1 - core), (mine_ref, core)):
        ref[...] = flow_ref[pl.ds(pl.multiple_of(place * HALF, 8), HALF), :]


def first_flows(core, ptdf, kept, unit_rows, load):
    half = jax.ShapeDtypeStruct((HALF, 128), F32)
    return pl.pallas_call(
        first_kernel,
        in_specs=[SMEM, pl.BlockSpec(memory_space=pltpu.HBM)] + [VMEM] * 3,
        out_specs=[VMEM, VMEM],
        out_shape=[half, half],
        scratch_shapes=[
            pltpu.VMEM((LINES_DEV - KEPT, ptdf.shape[1]), F32),
            pltpu.VMEM((2 * HALF, 128), F32),
            pltpu.SemaphoreType.DMA(()),
        ],
        compiler_params=params(24),
        cost_estimate=cost_of(2 * ROWS * ptdf.shape[1], 4 * ROWS * ptdf.shape[1]),
        name="first_flows",
    )(
        core,
        pltpu.with_memory_space_constraint(ptdf, pltpu.HBM),
        load,
        kept,
        unit_rows,
    )


def columns_kernel(group, ptdf_ref, unit_ref, *refs):
    high_ref, low_ref, pick_ref = refs[-3:]
    step = pl.program_id(0)
    units, span = pick_ref.shape
    peers = unit_ref.shape[0] // 2
    local = units // peers

    @pl.when(step == 0)
    def _():
        for peer in range(peers):
            spots = column(unit_ref[group * peers + peer][0:1, :local]).astype(jnp.int32)
            index = lax.broadcasted_iota(jnp.int32, (local, span), 1) + group * span
            pick = jnp.where(index == spots, 1.0, 0.0).astype(BF16)
            pick_ref[peer * local : (peer + 1) * local, :] = pick

    inside = row_index((BLOCK, span), step * BLOCK) < LINES_DEV
    ptdf = jnp.where(inside, ptdf_ref[...], 0.0)
    both = dot(jnp.concatenate(halves(ptdf), axis=0), pick_ref[...], ((1,), (1,)))
    rows = row_index((BLOCK, units), step * BLOCK)
    high_ref[...] = jnp.where(rows == LINES_DEV, 1.0, both[:BLOCK]).astype(BF16)
    low_ref[...] = both[BLOCK:].astype(BF16)


def unit_columns(ptdf, unit_rows, units, *begun):
    span = ptdf.shape[1] // 2
    group = 1 if begun else 0
    by_row = pl.BlockSpec((BLOCK, units // 2), lambda i: (i, group))
    return pl.pallas_call(
        functools.partial(columns_kernel, group),
        grid=(ROWS // BLOCK,),
        in_specs=[
            pl.BlockSpec((BLOCK, span), lambda i: (i, group)),
            pl.BlockSpec(unit_rows.shape, lambda i: (0, 0, 0)),
        ]
        + [pl.BlockSpec(memory_space=pl.ANY)] * len(begun),
        out_specs=[by_row, by_row],
        out_shape=[jax.ShapeDtypeStruct((ROWS, units), BF16)] * 2,
        scratch_shapes=[pltpu.VMEM((units // 2, span), BF16)],
        input_output_aliases={2: 0, 3: 1} if begun else {},
        compiler_params=params(40),
        cost_estimate=cost_of(2 * ROWS * span * units, 4 * ROWS * span),
        name="unit_columns",
    )(pltpu.with_memory_space_constraint(ptdf, pltpu.HBM), unit_rows, *begun)


def flow_kernel(place_ref, high_ref, low_ref, extrap_ref, flow_ref):
    high, low = halves(extrap_ref[...])
    pair = jnp.concatenate([high, low], axis=1)
    rows = pl.ds(pl.multiple_of(place_ref[0] * HALF, 16), HALF)
    both = dot(high_ref[rows, :], pair)
    flow_ref[...] = both[:, :128] + both[:, 128:] + dot(low_ref[rows, :], high)


def unit_flows(place, high, low, extrap):
    return pl.pallas_call(
        flow_kernel,
        in_specs=[SMEM] + [VMEM] * 3,
        out_specs=VMEM,
        out_shape=jax.ShapeDtypeStruct((HALF, 128), F32),
        compiler_params=params(8),
        cost_estimate=cost_of(3 * 2 * HALF * 512 * 128, 4 * HALF * 512),
        name="unit_flows",
    )(place, high, low, extrap)


def dual_kernel(*refs):
    count = len(CHUNKS)
    lefts, rights = refs[:count], refs[count : 2 * count]
    flow_ref, dual_ref, step_ref, limit_ref, dual_out, *flow_out = refs[2 * count :]
    for chunk, ends in enumerate(CHUNKS):
        rows = slice(*ends)
        flow = flow_ref[rows, :] + (lefts[chunk][...] + rights[chunk][...])
        for ref in flow_out:
            ref[rows, :] = flow
        moved = dual_ref[rows, :] + step_ref[rows, :] * flow
        limit = limit_ref[rows, :]
        dual_out[rows, :] = moved - jnp.clip(moved, -limit, limit)


def dual_step(lefts, rights, flow, dual, steps, limits, outputs):
    half = jax.ShapeDtypeStruct((HALF, 128), F32)
    return pl.pallas_call(
        dual_kernel,
        in_specs=[VMEM] * (4 + 2 * len(lefts)),
        out_specs=[VMEM] * outputs,
        out_shape=[half] * outputs,
        compiler_params=params(8),
        name="dual_step",
    )(*lefts, *rights, flow, dual, steps, limits)


def price_kernel(place_ref, dual_ref, high_ref, low_ref, *refs):
    rows = pl.ds(pl.multiple_of(place_ref[0] * HALF, 16), HALF)
    high, low = halves(dual_ref[...].T)
    both = dot(jnp.concatenate([high, low], axis=0), high_ref[rows, :])
    price = both[:128] + both[128:] + dot(high, low_ref[rows, :])
    if len(refs) == 2:
        refs[1][...] = (refs[0][...] + price).T
    else:
        refs[0][...] = price


def unit_prices(place, dual, high, low, *part):
    units = high.shape[1]
    return pl.pallas_call(
        price_kernel,
        in_specs=[SMEM] + [VMEM] * (3 + len(part)),
        out_specs=VMEM,
        out_shape=jax.ShapeDtypeStruct((units, 128) if part else (128, units), F32),
        compiler_params=params(8),
        cost_estimate=cost_of(3 * 2 * HALF * 512 * 128, 4 * HALF * 512),
        name="unit_prices",
    )(place, dual, high, low, *part)


def joined_kernel(core_ref, mine_ref, other_ref, dual_ref):
    first = core_ref[0] == 0
    mine, other = mine_ref[...], other_ref[...]
    dual_ref[:HALF, :] = jnp.where(first, mine, other)
    rest = LINES_DEV - HALF
    dual_ref[HALF:, :] = jnp.where(first, other[:rest], mine[:rest])


def joined(core, mine, other):
    return pl.pallas_call(
        joined_kernel,
        in_specs=[SMEM, VMEM, VMEM],
        out_specs=VMEM,
        out_shape=jax.ShapeDtypeStruct((LINES_DEV, 128), F32),
        compiler_params=params(8),
        name="joined",
    )(core, mine, other)


def unit_kernel(price_ref, gen_ref, old_ref, state_ref, table_ref, gen_out, extrap_ref, copies_ref):
    cost = table_ref[:, 0:1]
    lower = table_ref[:, 1:2]
    upper = table_ref[:, 2:3]
    gen = gen_ref[...]
    gradient = cost + jnp.sum(price_ref[...], axis=0) + state_ref[...]
    updated = jnp.clip(gen - PRIMAL_STEP * gradient, lower, upper)
    extrap = 2.0 * updated - gen
    gen_out[...] = updated
    extrap_ref[...] = extrap
    copies_ref[...] = jnp.broadcast_to((extrap - old_ref[...])[None], copies_ref.shape)


def unit_step(prices, gen, old, state, table):
    one = jax.ShapeDtypeStruct(gen.shape, F32)
    return pl.pallas_call(
        unit_kernel,
        in_specs=[VMEM] * 5,
        out_specs=[VMEM] * 3,
        out_shape=[one, one, jax.ShapeDtypeStruct(prices.shape, F32)],
        compiler_params=params(8),
        name="unit_step",
    )(prices, gen, old, state, table)


def state_kernel(place_ref, own_ref, far_ref, ramp_ref, store_ref, table_ref, ramp_out, store_out, state_ref):
    ramp_limit = DUAL_STEP * table_ref[:, 3:4]
    storage = table_ref[:, 4:5]
    store_limit = DUAL_STEP * table_ref[:, 5:6]
    first = place_ref[0] == 0
    own, far = own_ref[...], far_ref[...]
    extrap = jnp.concatenate([jnp.where(first, own, far), jnp.where(first, far, own)], axis=1)
    hour = lax.broadcasted_iota(jnp.int32, extrap.shape, 1)
    hours = extrap.shape[1]
    previous = pltpu.roll(extrap, 1, 1)
    moved = ramp_ref[...] + jnp.where(hour >= 1, DUAL_STEP * (extrap - previous), 0.0)
    ramp = moved - jnp.clip(moved, -ramp_limit, ramp_limit)
    ramp_out[...] = ramp
    early = lax.broadcasted_iota(jnp.int32, (hours, hours), 0)
    late = lax.broadcasted_iota(jnp.int32, (hours, hours), 1)
    forward = jnp.where(early <= late, 1.0, 0.0)
    backward = jnp.where(early >= late, 1.0, 0.0)
    running = jnp.dot(extrap, forward, precision=lax.Precision.HIGHEST, preferred_element_type=F32)
    moved = store_ref[...] + DUAL_STEP * storage * running
    store = moved - jnp.clip(moved, -store_limit, store_limit)
    store_out[...] = store
    suffix = jnp.dot(store, backward, precision=lax.Precision.HIGHEST, preferred_element_type=F32)
    after = jnp.where(hour < hours - 1, pltpu.roll(ramp, hours - 1, 1), 0.0)
    state = ramp - after + storage * suffix
    state_ref[...] = jnp.where(first, state[:, :128], state[:, 128:])


def state_step(place, own, far, ramp, store, table):
    wide = jax.ShapeDtypeStruct(ramp.shape, F32)
    return pl.pallas_call(
        state_kernel,
        in_specs=[SMEM] + [VMEM] * 5,
        out_specs=[VMEM] * 3,
        out_shape=[wide, wide, jax.ShapeDtypeStruct(own.shape, F32)],
        compiler_params=params(8),
        cost_estimate=cost_of(12 * 2 * 32 * 256 * 256, 1 << 18),
        name="state_step",
    )(place, own, far, ramp, store, table)


SWAP = ((0, 1), (1, 0))
NEAR = ((0, 1), (1, 0), (2, 3), (3, 2))
FAR = ((1, 2), (2, 1), (3, 0), (0, 3))


def along_y(value, by_core):
    pairs = [(2 * i + core, 2 * j + core) for core in range(2) for i, j in by_core[core]]
    return lax.ppermute(value, BUS, pairs)


def on_device(ptdf, bus_load, unit_bus, unit_type, unit_limit, unit_cost, line_rating):
    line_count = lax.axis_size(LINE)
    hour_dev = bus_load.shape[1]
    local = unit_bus.shape[0]
    core = lax.axis_index("c").astype(jnp.int32)
    place = lax.axis_index("t").astype(jnp.int32)[None]
    block = (lax.axis_index(BUS) * ptdf.shape[1]).astype(jnp.int32)
    table, gen, copies = unit_tables(
        block[None], unit_bus, unit_type, unit_limit, unit_cost, line_count
    )
    unit_rows = lax.all_to_all(copies, LINE, 0, 0, tiled=True)
    load, kept = load_flows(ptdf, bus_load)
    mine, other = first_flows(core[None], ptdf, kept, unit_rows, load)
    extrap = far = 2.0 * gen

    pad = jnp.zeros((2 * HALF - LINES_DEV,), F32)
    limits = jnp.concatenate([DUAL_STEP * (line_rating.astype(F32) / 100.0), pad])
    index = core * HALF + jnp.arange(HALF, dtype=jnp.int32)
    weight = 1.0 / (UNITS * 16)
    steps = jnp.where(index < LINES_DEV, DUAL_STEP, jnp.where(index == LINES_DEV, weight, 0.0))
    steps = steps.astype(F32)[:, None]
    limits = lax.dynamic_slice_in_dim(limits, core * HALF, HALF, 0)[:, None]
    core, partner = core[None], 1 - core[None]
    flow = dual = jnp.zeros((HALF, hour_dev), F32)
    ramp = store = jnp.zeros((local, 2 * hour_dev), F32)
    high = low = None
    for iteration in range(ITERS):
        last = iteration == ITERS - 1
        total = mine + lax.ppermute(other, "c", SWAP)
        if iteration == 0:
            ramp, store, state = state_step(place, extrap, far, ramp, store, table)
            total, tied, rows, state = lax.optimization_barrier((total, ptdf, unit_rows, state))
            high, low = unit_columns(tied, rows, line_count * local)
        elif not last:
            total, tied = lax.optimization_barrier((total, extrap))
            far = lax.ppermute(tied, "t", SWAP)
        lefts = [total[start:stop] for start, stop in CHUNKS]
        lefts = [left + along_y(left, (NEAR, FAR)) for left in lefts]
        if iteration == 0:
            lefts[0], high, low = lax.optimization_barrier((lefts[0], high, low))
            high, low = unit_columns(tied, rows, line_count * local, high, low)
        elif not last:
            lefts[0], far = lax.optimization_barrier((lefts[0], far))
        if 0 < iteration < ITERS - 1:
            ramp, store, state = state_step(place, extrap, far, ramp, store, table)
        rights = [along_y(left, (FAR, NEAR)) for left in lefts]
        if iteration == 0:
            rights[-1], high, low = lax.optimization_barrier((rights[-1], high, low))
        if last:
            (dual,) = dual_step(lefts, rights, flow, dual, steps, limits, 1)
            return gen, joined(core, dual, lax.ppermute(dual, "c", SWAP))
        rights[-1], state, ramp, store = lax.optimization_barrier((rights[-1], state, ramp, store))
        dual, flow = dual_step(lefts, rights, flow, dual, steps, limits, 2)
        prices = unit_prices(core, dual, high, low)
        prices = unit_prices(partner, lax.ppermute(dual, "c", SWAP), high, low, prices)
        prices = prices.reshape(line_count, local, hour_dev)
        prices = lax.all_to_all(prices, LINE, 0, 0, tiled=True)
        gen, extrap, copies = unit_step(prices, gen, extrap, state, table)
        changes = lax.all_to_all(copies, LINE, 0, 0, tiled=True).reshape(-1, hour_dev)
        other = unit_flows(partner, high, low, changes)
        mine = unit_flows(core, high, low, changes)


def solution(mesh):
    finer = Mesh(
        mesh.devices.reshape(8, 2, 4, 2, mesh.shape["tm"]),
        ("z", "xl", "y", "c", "t"),
    )
    return jax.shard_map(
        on_device,
        mesh=finer,
        in_specs=(
            P(LINE, BUS),
            P(BUS, "t"),
            P(LINE_BUS),
            P(LINE_BUS),
            P(LINE_BUS),
            P(LINE_BUS),
            P(LINE),
        ),
        out_specs=(P(LINE_BUS, "t"), P(LINE, "t")),
        check_vma=False,
    )
```

```python
import functools

import jax
import jax.numpy as jnp
from jax import lax
from jax.experimental import pallas as pl
from jax.experimental.pallas import tpu as pltpu
from jax.sharding import Mesh
from jax.sharding import PartitionSpec as P

UNITS = 4096
ITERS = 4
LINE = ("z", "xl")
EXCHANGE = ("xl", "z")
BUS = ("y", "c")
LINE_BUS = ("z", "xl", "y", "c")

RAMP_RATES = (0.1, 0.2, 0.4, 0.5)
COST_FACTORS = (1.0, 1.5, 3.0, 0.05)
PRIMAL_STEP = 0.5
DUAL_STEP = 0.5

LINES_DEV = 960
ROWS = 1024
HALF = 496
BLOCK = 512
KEPT = 320
CHUNKS = ((0, 240), (240, HALF))
BF16 = jnp.bfloat16
F32 = jnp.float32
VMEM = pl.BlockSpec(memory_space=pltpu.VMEM)
SMEM = pl.BlockSpec(memory_space=pltpu.SMEM)


def params(mib):
    return pltpu.CompilerParams(vmem_limit_bytes=mib << 20)


def cost_of(flops, size):
    return pl.CostEstimate(flops=flops, bytes_accessed=size, transcendentals=0)


def halves(value):
    high = value.astype(BF16)
    return high, (value - high.astype(F32)).astype(BF16)


def dot(left, right, dims=((1,), (0,))):
    return lax.dot_general(left, right, (dims, ((), ())), preferred_element_type=F32)


def exchange_place(line):
    return line % 2 * 8 + line // 2


def row_index(shape, first):
    return first + lax.broadcasted_iota(jnp.int32, shape, 0)


def picked(kinds, values):
    total = 0.0
    for kind, value in enumerate(values):
        total = total + jnp.where(kinds == kind, value, 0.0)
    return total


def column(row):
    count = row.shape[1]
    same = lax.broadcasted_iota(jnp.int32, (count, count), 0) == lax.broadcasted_iota(
        jnp.int32, (count, count), 1
    )
    return jnp.sum(jnp.where(same, row, jnp.zeros_like(row)), axis=1, keepdims=True)


def table_kernel(
    place_ref, bus_in, type_in, limit_in, cost_in, table_ref, first_ref, copies_ref,
    bus_ref, type_ref, limit_ref, cost_ref, arrived
):
    pairs = (
        (bus_in, bus_ref.at[0]),
        (type_in, type_ref.at[0]),
        (limit_in, limit_ref.at[0]),
        (cost_in, cost_ref.at[0]),
    )
    copies = [pltpu.make_async_copy(*pair, arrived.at[spot]) for spot, pair in enumerate(pairs)]
    for copy in copies:
        copy.start()
    for copy in copies:
        copy.wait()
    kinds = column(type_ref[...])
    capacity = column(limit_ref[...]).astype(F32) / 100.0
    cost = column(cost_ref[...]) * picked(kinds, COST_FACTORS)
    storage = jnp.where(kinds == 3, 1.0, 0.0)
    lower = -capacity * storage
    lane = lax.broadcasted_iota(jnp.int32, table_ref.shape, 1)
    table = jnp.zeros(table_ref.shape, F32)
    parts = (cost, lower, capacity, picked(kinds, RAMP_RATES) * capacity, storage, 2.0 * capacity)
    for spot, part in enumerate(parts):
        table = jnp.where(lane == spot, part, table)
    table_ref[...] = table
    first = jnp.clip(-PRIMAL_STEP * cost, lower, capacity)
    first_ref[...] = jnp.broadcast_to(first, first_ref.shape)
    bus = column(bus_ref[...] - place_ref[0]).astype(F32)
    same = lane == lax.broadcasted_iota(jnp.int32, table_ref.shape, 0)
    bus = jnp.sum(jnp.where(same, bus, 0.0), axis=0, keepdims=True)
    extrap = jnp.sum(jnp.where(same, 2.0 * first, 0.0), axis=0, keepdims=True)
    sent = jnp.where(lax.broadcasted_iota(jnp.int32, (8, 128), 0) == 0, bus, extrap)
    copies_ref[...] = jnp.broadcast_to(sent[None], copies_ref.shape)


def unit_tables(place, unit_bus, unit_type, unit_limit, unit_cost, line_count):
    units = unit_bus.shape[0]
    rows = (unit_bus, unit_type, unit_limit, unit_cost)
    one = jax.ShapeDtypeStruct((units, 128), F32)
    return pl.pallas_call(
        table_kernel,
        in_specs=[SMEM] + [pl.BlockSpec(memory_space=pltpu.HBM)] * 4,
        out_specs=[VMEM] * 3,
        out_shape=[
            one,
            one,
            jax.ShapeDtypeStruct((line_count, 8, 128), F32),
        ],
        scratch_shapes=[pltpu.VMEM((1, units), row.dtype) for row in rows]
        + [pltpu.SemaphoreType.DMA((4,))],
        compiler_params=params(16),
        name="unit_tables",
    )(place, *(pltpu.with_memory_space_constraint(x, pltpu.HBM) for x in rows))


def load_kernel(ptdf_ref, load_ref, flow_ref, kept_ref):
    step = pl.program_id(0)
    ptdf, load = ptdf_ref[...], load_ref[...]
    kept_ref[...] = ptdf[:KEPT]
    high, low = halves(load)
    ptdf_high, ptdf_low = halves(ptdf)
    both = dot(ptdf_high, jnp.concatenate([high, low], axis=1))
    flow = both[:, :128] + both[:, 128:] + dot(ptdf_low, high)
    total = jnp.sum(load, axis=0, keepdims=True)
    end = row_index((2 * HALF - LINES_DEV, 128), LINES_DEV) == LINES_DEV
    total = jnp.where(end, total, 0.0)

    @pl.when(step == 0)
    def _():
        flow_ref[:LINES_DEV, :] = flow
        flow_ref[LINES_DEV:, :] = total

    @pl.when(step > 0)
    def _():
        flow_ref[:LINES_DEV, :] += flow
        flow_ref[LINES_DEV:, :] += total


def load_flows(ptdf, load):
    lines, buses = ptdf.shape
    return pl.pallas_call(
        load_kernel,
        grid=(buses // BLOCK,),
        in_specs=[
            pl.BlockSpec((lines, BLOCK), lambda i: (0, i)),
            pl.BlockSpec((BLOCK, 128), lambda i: (i, 0)),
        ],
        out_specs=[
            pl.BlockSpec((2 * HALF, 128), lambda i: (0, 0)),
            pl.BlockSpec((KEPT, BLOCK), lambda i: (0, i)),
        ],
        out_shape=[
            jax.ShapeDtypeStruct((2 * HALF, 128), F32),
            jax.ShapeDtypeStruct((KEPT, buses), F32),
        ],
        compiler_params=params(40),
        cost_estimate=cost_of(3 * 2 * ROWS * buses * 128, 4 * ROWS * buses),
        name="load_flows",
    )(*(pltpu.with_memory_space_constraint(x, pltpu.HBM) for x in (ptdf, load)))


def first_kernel(
    core_ref, ptdf_in, load_ref, kept_ref, unit_ref, mine_ref, other_ref, rest_ref, flow_ref, arrived
):
    rest_rows = ptdf_in.at[pl.ds(KEPT, LINES_DEV - KEPT), :]
    copy = pltpu.make_async_copy(rest_rows, rest_ref, arrived)
    copy.start()
    peers, buses = unit_ref.shape[0], ptdf_in.shape[1]
    span, units = buses // peers, 32
    lane = lax.broadcasted_iota(jnp.int32, (units, 128), 1)
    tiles = [jnp.zeros((units, 128), F32)] * (buses // 128)
    for peer in range(peers):
        spots = column(unit_ref[peer][0:1, :units]).astype(jnp.int32)
        extrap = column(unit_ref[peer][1:2, :units])
        for tile in range(peer * span // 128, ((peer + 1) * span - 1) // 128 + 1):
            tiles[tile] += jnp.where(lane + tile * 128 == spots, extrap, 0.0)
    injection = jnp.concatenate(
        [jnp.sum(tile, axis=0, keepdims=True) for tile in tiles], axis=1
    )
    flow_ref[:KEPT, :] = jnp.sum(kept_ref[...] * injection, axis=1, keepdims=True) - load_ref[:KEPT, :]
    total = jnp.sum(injection, axis=1, keepdims=True)
    end = row_index((2 * HALF - LINES_DEV, 128), LINES_DEV)
    flow_ref[LINES_DEV:, :] = jnp.where(end == LINES_DEV, total, 0.0) - load_ref[LINES_DEV:, :]
    copy.wait()
    rest = jnp.sum(rest_ref[...] * injection, axis=1, keepdims=True)
    flow_ref[KEPT:LINES_DEV, :] = rest - load_ref[KEPT:LINES_DEV, :]
    core = core_ref[0]
    for ref, place in ((other_ref, 1 - core), (mine_ref, core)):
        ref[...] = flow_ref[pl.ds(pl.multiple_of(place * HALF, 8), HALF), :]


def first_flows(core, ptdf, kept, unit_rows, load):
    half = jax.ShapeDtypeStruct((HALF, 128), F32)
    return pl.pallas_call(
        first_kernel,
        in_specs=[SMEM, pl.BlockSpec(memory_space=pltpu.HBM)] + [VMEM] * 3,
        out_specs=[VMEM, VMEM],
        out_shape=[half, half],
        scratch_shapes=[
            pltpu.VMEM((LINES_DEV - KEPT, ptdf.shape[1]), F32),
            pltpu.VMEM((2 * HALF, 128), F32),
            pltpu.SemaphoreType.DMA(()),
        ],
        compiler_params=params(24),
        cost_estimate=cost_of(2 * ROWS * ptdf.shape[1], 4 * ROWS * ptdf.shape[1]),
        name="first_flows",
    )(
        core,
        pltpu.with_memory_space_constraint(ptdf, pltpu.HBM),
        load,
        kept,
        unit_rows,
    )


def columns_kernel(group, ptdf_ref, unit_ref, *refs):
    high_ref, low_ref, pick_ref = refs[-3:]
    step = pl.program_id(0)
    units, span = pick_ref.shape
    peers = unit_ref.shape[0] // 2
    local = units // peers

    @pl.when(step == 0)
    def _():
        for peer in range(peers):
            spots = column(unit_ref[group * peers + peer][0:1, :local]).astype(jnp.int32)
            index = lax.broadcasted_iota(jnp.int32, (local, span), 1) + group * span
            pick = jnp.where(index == spots, 1.0, 0.0).astype(BF16)
            pick_ref[peer * local : (peer + 1) * local, :] = pick

    inside = row_index((BLOCK, span), step * BLOCK) < LINES_DEV
    ptdf = jnp.where(inside, ptdf_ref[...], 0.0)
    both = dot(jnp.concatenate(halves(ptdf), axis=0), pick_ref[...], ((1,), (1,)))
    rows = row_index((BLOCK, units), step * BLOCK)
    high_ref[...] = jnp.where(rows == LINES_DEV, 1.0, both[:BLOCK]).astype(BF16)
    low_ref[...] = both[BLOCK:].astype(BF16)


def unit_columns(ptdf, unit_rows, units, *begun):
    span = ptdf.shape[1] // 2
    group = 1 if begun else 0
    by_row = pl.BlockSpec((BLOCK, units // 2), lambda i: (i, group))
    return pl.pallas_call(
        functools.partial(columns_kernel, group),
        grid=(ROWS // BLOCK,),
        in_specs=[
            pl.BlockSpec((BLOCK, span), lambda i: (i, group)),
            pl.BlockSpec(unit_rows.shape, lambda i: (0, 0, 0)),
        ]
        + [pl.BlockSpec(memory_space=pl.ANY)] * len(begun),
        out_specs=[by_row, by_row],
        out_shape=[jax.ShapeDtypeStruct((ROWS, units), BF16)] * 2,
        scratch_shapes=[pltpu.VMEM((units // 2, span), BF16)],
        input_output_aliases={2: 0, 3: 1} if begun else {},
        compiler_params=params(40),
        cost_estimate=cost_of(2 * ROWS * span * units, 4 * ROWS * span),
        name="unit_columns",
    )(pltpu.with_memory_space_constraint(ptdf, pltpu.HBM), unit_rows, *begun)


def flow_kernel(place_ref, high_ref, low_ref, extrap_ref, flow_ref):
    blocks = [extrap_ref[exchange_place(line)] for line in range(extrap_ref.shape[0])]
    high, low = halves(jnp.concatenate(blocks, axis=0))
    pair = jnp.concatenate([high, low], axis=1)
    rows = pl.ds(pl.multiple_of(place_ref[0] * HALF, 16), HALF)
    both = dot(high_ref[rows, :], pair)
    flow_ref[...] = both[:, :128] + both[:, 128:] + dot(low_ref[rows, :], high)


def unit_flows(place, high, low, extrap):
    return pl.pallas_call(
        flow_kernel,
        in_specs=[SMEM] + [VMEM] * 3,
        out_specs=VMEM,
        out_shape=jax.ShapeDtypeStruct((HALF, 128), F32),
        compiler_params=params(8),
        cost_estimate=cost_of(3 * 2 * HALF * 512 * 128, 4 * HALF * 512),
        name="unit_flows",
    )(place, high, low, extrap)


def dual_kernel(*refs):
    count = len(CHUNKS)
    lefts, rights = refs[:count], refs[count : 2 * count]
    flow_ref, dual_ref, step_ref, limit_ref, dual_out, *flow_out = refs[2 * count :]
    for chunk, ends in enumerate(CHUNKS):
        rows = slice(*ends)
        flow = flow_ref[rows, :] + (lefts[chunk][...] + rights[chunk][...])
        for ref in flow_out:
            ref[rows, :] = flow
        moved = dual_ref[rows, :] + step_ref[rows, :] * flow
        limit = limit_ref[rows, :]
        dual_out[rows, :] = moved - jnp.clip(moved, -limit, limit)


def dual_step(lefts, rights, flow, dual, steps, limits, outputs):
    half = jax.ShapeDtypeStruct((HALF, 128), F32)
    return pl.pallas_call(
        dual_kernel,
        in_specs=[VMEM] * (4 + 2 * len(lefts)),
        out_specs=[VMEM] * outputs,
        out_shape=[half] * outputs,
        compiler_params=params(8),
        name="dual_step",
    )(*lefts, *rights, flow, dual, steps, limits)


def price_kernel(place_ref, dual_ref, high_ref, low_ref, *refs):
    rows = pl.ds(pl.multiple_of(place_ref[0] * HALF, 16), HALF)
    high, low = halves(dual_ref[...].T)
    both = dot(jnp.concatenate([high, low], axis=0), high_ref[rows, :])
    price = both[:128] + both[128:] + dot(high, low_ref[rows, :])
    if len(refs) == 2:
        price = (refs[0][...] + price).T
        count, local, _ = refs[1].shape
        for line in range(count):
            refs[1][exchange_place(line)] = price[line * local : (line + 1) * local]
    else:
        refs[0][...] = price


def unit_prices(place, dual, high, low, *part):
    units = high.shape[1]
    return pl.pallas_call(
        price_kernel,
        in_specs=[SMEM] + [VMEM] * (3 + len(part)),
        out_specs=VMEM,
        out_shape=jax.ShapeDtypeStruct((16, units // 16, 128) if part else (128, units), F32),
        compiler_params=params(8),
        cost_estimate=cost_of(3 * 2 * HALF * 512 * 128, 4 * HALF * 512),
        name="unit_prices",
    )(place, dual, high, low, *part)


def placed_kernel(place_ref, half_ref, *refs):
    out_ref, arrived = refs[-2:]
    for place, count in enumerate((HALF, LINES_DEV - HALF)):

        @pl.when(place_ref[0] == place)
        def _(place=place, count=count):
            rows = out_ref.at[pl.ds(place * HALF, count), :]
            copy = pltpu.make_async_copy(half_ref.at[pl.ds(0, count), :], rows, arrived)
            copy.start()
            copy.wait()


def placed(place, half, *begun):
    anywhere = pl.BlockSpec(memory_space=pl.ANY)
    return pl.pallas_call(
        placed_kernel,
        in_specs=[SMEM, VMEM] + [anywhere] * len(begun),
        out_specs=anywhere,
        out_shape=jax.ShapeDtypeStruct((LINES_DEV, 128), F32),
        scratch_shapes=[pltpu.SemaphoreType.DMA(())],
        input_output_aliases={2: 0} if begun else {},
        compiler_params=params(8),
        cost_estimate=cost_of(0, 8 * HALF * 128),
        name="placed",
    )(place, half, *begun)


def unit_kernel(price_ref, gen_ref, old_ref, state_ref, table_ref, extrap_ref, copies_ref, *gen_out):
    cost = table_ref[:, 0:1]
    lower = table_ref[:, 1:2]
    upper = table_ref[:, 2:3]
    gen = gen_ref[...]
    gradient = cost + jnp.sum(price_ref[...], axis=0) + state_ref[...]
    updated = jnp.clip(gen - PRIMAL_STEP * gradient, lower, upper)
    extrap = 2.0 * updated - gen
    for ref in gen_out:
        ref[...] = updated
    extrap_ref[...] = extrap
    copies_ref[...] = jnp.broadcast_to((extrap - old_ref[...])[None], copies_ref.shape)


def unit_step(prices, gen, old, state, table, last):
    one = jax.ShapeDtypeStruct(gen.shape, F32)
    shapes = [one, jax.ShapeDtypeStruct(prices.shape, F32)] + ([] if last else [one])
    return pl.pallas_call(
        unit_kernel,
        in_specs=[VMEM] * 5,
        out_specs=[VMEM] * len(shapes),
        out_shape=shapes,
        compiler_params=params(8),
        name="unit_step",
    )(prices, gen, old, state, table)


def state_kernel(place_ref, own_ref, far_ref, ramp_ref, store_ref, table_ref, state_ref, *kept):
    ramp_limit = DUAL_STEP * table_ref[:, 3:4]
    storage = table_ref[:, 4:5]
    store_limit = DUAL_STEP * table_ref[:, 5:6]
    first = place_ref[0] == 0
    own, far = own_ref[...], far_ref[...]
    extrap = jnp.concatenate([jnp.where(first, own, far), jnp.where(first, far, own)], axis=1)
    hour = lax.broadcasted_iota(jnp.int32, extrap.shape, 1)
    hours = extrap.shape[1]
    previous = pltpu.roll(extrap, 1, 1)
    moved = ramp_ref[...] + jnp.where(hour >= 1, DUAL_STEP * (extrap - previous), 0.0)
    ramp = moved - jnp.clip(moved, -ramp_limit, ramp_limit)
    early = lax.broadcasted_iota(jnp.int32, (hours, hours), 0)
    late = lax.broadcasted_iota(jnp.int32, (hours, hours), 1)
    forward = jnp.where(early <= late, 1.0, 0.0)
    backward = jnp.where(early >= late, 1.0, 0.0)
    running = jnp.dot(extrap, forward, precision=lax.Precision.HIGHEST, preferred_element_type=F32)
    moved = store_ref[...] + DUAL_STEP * storage * running
    store = moved - jnp.clip(moved, -store_limit, store_limit)
    for ref, value in zip(kept, (ramp, store)):
        ref[...] = value
    suffix = jnp.dot(store, backward, precision=lax.Precision.HIGHEST, preferred_element_type=F32)
    after = jnp.where(hour < hours - 1, pltpu.roll(ramp, hours - 1, 1), 0.0)
    state = ramp - after + storage * suffix
    state_ref[...] = jnp.where(first, state[:, :128], state[:, 128:])


def state_step(place, own, far, ramp, store, table, last):
    wide = jax.ShapeDtypeStruct(ramp.shape, F32)
    shapes = [jax.ShapeDtypeStruct(own.shape, F32)] + ([] if last else [wide, wide])
    return pl.pallas_call(
        state_kernel,
        in_specs=[SMEM] + [VMEM] * 5,
        out_specs=[VMEM] * len(shapes),
        out_shape=shapes,
        compiler_params=params(8),
        cost_estimate=cost_of(12 * 2 * 32 * 256 * 256, 1 << 18),
        name="state_step",
    )(place, own, far, ramp, store, table)


SWAP = ((0, 1), (1, 0))
NEAR = ((0, 1), (1, 0), (2, 3), (3, 2))
FAR = ((1, 2), (2, 1), (3, 0), (0, 3))


def along_y(value, by_core):
    pairs = [(2 * i + core, 2 * j + core) for core in range(2) for i, j in by_core[core]]
    return lax.ppermute(value, BUS, pairs)


def on_device(ptdf, bus_load, unit_bus, unit_type, unit_limit, unit_cost, line_rating):
    line_count = lax.axis_size(LINE)
    hour_dev = bus_load.shape[1]
    local = unit_bus.shape[0]
    core = lax.axis_index("c").astype(jnp.int32)
    place = lax.axis_index("t").astype(jnp.int32)[None]
    block = (lax.axis_index(BUS) * ptdf.shape[1]).astype(jnp.int32)
    table, gen, copies = unit_tables(
        block[None], unit_bus, unit_type, unit_limit, unit_cost, line_count
    )
    unit_rows = lax.all_to_all(copies, LINE, 0, 0, tiled=True)
    load, kept = load_flows(ptdf, bus_load)
    mine, other = first_flows(core[None], ptdf, kept, unit_rows, load)
    extrap = far = 2.0 * gen

    pad = jnp.zeros((2 * HALF - LINES_DEV,), F32)
    limits = jnp.concatenate([DUAL_STEP * (line_rating.astype(F32) / 100.0), pad])
    index = core * HALF + jnp.arange(HALF, dtype=jnp.int32)
    weight = 1.0 / (UNITS * 16)
    steps = jnp.where(index < LINES_DEV, DUAL_STEP, jnp.where(index == LINES_DEV, weight, 0.0))
    steps = steps.astype(F32)[:, None]
    limits = lax.dynamic_slice_in_dim(limits, core * HALF, HALF, 0)[:, None]
    core, partner = core[None], 1 - core[None]
    flow = dual = jnp.zeros((HALF, hour_dev), F32)
    ramp = store = jnp.zeros((local, 2 * hour_dev), F32)
    high = low = None
    for iteration in range(ITERS):
        last = iteration == ITERS - 1
        total = mine + lax.ppermute(other, "c", SWAP)
        if iteration == 0:
            state, ramp, store = state_step(place, extrap, far, ramp, store, table, False)
            total, tied, rows, state = lax.optimization_barrier((total, ptdf, unit_rows, state))
            high, low = unit_columns(tied, rows, line_count * local)
        elif not last:
            total, tied = lax.optimization_barrier((total, extrap))
            far = lax.ppermute(tied, "t", SWAP)
        lefts = [total[start:stop] for start, stop in CHUNKS]
        lefts = [left + along_y(left, (NEAR, FAR)) for left in lefts]
        if iteration == 0:
            lefts[0], high, low = lax.optimization_barrier((lefts[0], high, low))
            high, low = unit_columns(tied, rows, line_count * local, high, low)
        elif not last:
            lefts[0], far = lax.optimization_barrier((lefts[0], far))
        if 0 < iteration < ITERS - 1:
            state, *kept = state_step(place, extrap, far, ramp, store, table, iteration == ITERS - 2)
            ramp, store = kept if kept else (None, None)
        rights = [along_y(left, (FAR, NEAR)) for left in lefts]
        if iteration == 0:
            rights[-1], high, low = lax.optimization_barrier((rights[-1], high, low))
        if last:
            (dual,) = dual_step(lefts, rights, flow, dual, steps, limits, 1)
            result = placed(core, dual)
            return 0.5 * (extrap + before), placed(partner, lax.ppermute(dual, "c", SWAP), result)
        rights[-1], state, ramp, store = lax.optimization_barrier((rights[-1], state, ramp, store))
        dual, flow = dual_step(lefts, rights, flow, dual, steps, limits, 2)
        prices = unit_prices(core, dual, high, low)
        prices = unit_prices(partner, lax.ppermute(dual, "c", SWAP), high, low, prices)
        prices = lax.all_to_all(prices, EXCHANGE, 0, 0, tiled=True)
        before = gen
        extrap, copies, *updated = unit_step(
            prices, gen, extrap, state, table, iteration == ITERS - 2
        )
        gen = updated[0] if updated else None
        changes = lax.all_to_all(copies, EXCHANGE, 0, 0, tiled=True)
        other = unit_flows(partner, high, low, changes)
        mine = unit_flows(core, high, low, changes)


def solution(mesh):
    finer = Mesh(
        mesh.devices.reshape(8, 2, 4, 2, mesh.shape["tm"]),
        ("z", "xl", "y", "c", "t"),
    )
    return jax.shard_map(
        on_device,
        mesh=finer,
        in_specs=(
            P(LINE, BUS),
            P(BUS, "t"),
            P(LINE_BUS),
            P(LINE_BUS),
            P(LINE_BUS),
            P(LINE_BUS),
            P(LINE),
        ),
        out_specs=(P(LINE_BUS, "t"), P(LINE, "t")),
        check_vma=False,
    )
```

```python
import functools

import jax
import jax.numpy as jnp
from jax import lax
from jax.experimental import pallas as pl
from jax.experimental.pallas import tpu as pltpu
from jax.sharding import Mesh
from jax.sharding import PartitionSpec as P

UNITS = 4096
ITERS = 4
LINE = ("z", "xl")
EXCHANGE = ("xl", "z")
BUS = ("y", "c")
LINE_BUS = ("z", "xl", "y", "c")

RAMP_RATES = (0.1, 0.2, 0.4, 0.5)
COST_FACTORS = (1.0, 1.5, 3.0, 0.05)
PRIMAL_STEP = 0.5
DUAL_STEP = 0.5

LINES_DEV = 960
ROWS = 1024
HALF = 496
BLOCK = 512
KEPT = 320
CHUNKS = ((0, 240), (240, HALF))
BF16 = jnp.bfloat16
F32 = jnp.float32
VMEM = pl.BlockSpec(memory_space=pltpu.VMEM)
SMEM = pl.BlockSpec(memory_space=pltpu.SMEM)


def params(mib):
    return pltpu.CompilerParams(vmem_limit_bytes=mib << 20)


def cost_of(flops, size):
    return pl.CostEstimate(flops=flops, bytes_accessed=size, transcendentals=0)


def halves(value):
    high = value.astype(BF16)
    return high, (value - high.astype(F32)).astype(BF16)


def dot(left, right, dims=((1,), (0,))):
    return lax.dot_general(left, right, (dims, ((), ())), preferred_element_type=F32)


def exchange_place(line):
    return line % 2 * 8 + line // 2


def row_index(shape, first):
    return first + lax.broadcasted_iota(jnp.int32, shape, 0)


def picked(kinds, values):
    total = 0.0
    for kind, value in enumerate(values):
        total = total + jnp.where(kinds == kind, value, 0.0)
    return total


def column(row):
    count = row.shape[1]
    same = lax.broadcasted_iota(jnp.int32, (count, count), 0) == lax.broadcasted_iota(
        jnp.int32, (count, count), 1
    )
    return jnp.sum(jnp.where(same, row, jnp.zeros_like(row)), axis=1, keepdims=True)


def table_kernel(
    place_ref, bus_in, type_in, limit_in, cost_in, table_ref, first_ref, copies_ref,
    bus_ref, type_ref, limit_ref, cost_ref, arrived
):
    pairs = (
        (bus_in, bus_ref.at[0]),
        (type_in, type_ref.at[0]),
        (limit_in, limit_ref.at[0]),
        (cost_in, cost_ref.at[0]),
    )
    copies = [pltpu.make_async_copy(*pair, arrived.at[spot]) for spot, pair in enumerate(pairs)]
    for copy in copies:
        copy.start()
    for copy in copies:
        copy.wait()
    kinds = column(type_ref[...])
    capacity = column(limit_ref[...]).astype(F32) / 100.0
    cost = column(cost_ref[...]) * picked(kinds, COST_FACTORS)
    storage = jnp.where(kinds == 3, 1.0, 0.0)
    lower = -capacity * storage
    lane = lax.broadcasted_iota(jnp.int32, table_ref.shape, 1)
    table = jnp.zeros(table_ref.shape, F32)
    parts = (cost, lower, capacity, picked(kinds, RAMP_RATES) * capacity, storage, 2.0 * capacity)
    for spot, part in enumerate(parts):
        table = jnp.where(lane == spot, part, table)
    table_ref[...] = table
    first = jnp.clip(-PRIMAL_STEP * cost, lower, capacity)
    first_ref[...] = jnp.broadcast_to(first, first_ref.shape)
    bus = column(bus_ref[...] - place_ref[0]).astype(F32)
    same = lane == lax.broadcasted_iota(jnp.int32, table_ref.shape, 0)
    bus = jnp.sum(jnp.where(same, bus, 0.0), axis=0, keepdims=True)
    extrap = jnp.sum(jnp.where(same, 2.0 * first, 0.0), axis=0, keepdims=True)
    sent = jnp.where(lax.broadcasted_iota(jnp.int32, (8, 128), 0) == 0, bus, extrap)
    copies_ref[...] = jnp.broadcast_to(sent[None], copies_ref.shape)


def unit_tables(place, unit_bus, unit_type, unit_limit, unit_cost, line_count):
    units = unit_bus.shape[0]
    rows = (unit_bus, unit_type, unit_limit, unit_cost)
    one = jax.ShapeDtypeStruct((units, 128), F32)
    return pl.pallas_call(
        table_kernel,
        in_specs=[SMEM] + [pl.BlockSpec(memory_space=pltpu.HBM)] * 4,
        out_specs=[VMEM] * 3,
        out_shape=[
            one,
            one,
            jax.ShapeDtypeStruct((line_count, 8, 128), F32),
        ],
        scratch_shapes=[pltpu.VMEM((1, units), row.dtype) for row in rows]
        + [pltpu.SemaphoreType.DMA((4,))],
        compiler_params=params(16),
        name="unit_tables",
    )(place, *(pltpu.with_memory_space_constraint(x, pltpu.HBM) for x in rows))


def load_kernel(ptdf_ref, load_ref, flow_ref, kept_ref):
    step = pl.program_id(0)
    ptdf, load = ptdf_ref[...], load_ref[...]
    kept_ref[...] = ptdf[:KEPT]
    high, low = halves(load)
    ptdf_high, ptdf_low = halves(ptdf)
    both = dot(ptdf_high, jnp.concatenate([high, low], axis=1))
    flow = both[:, :128] + both[:, 128:] + dot(ptdf_low, high)
    total = jnp.sum(load, axis=0, keepdims=True)
    end = row_index((2 * HALF - LINES_DEV, 128), LINES_DEV) == LINES_DEV
    total = jnp.where(end, total, 0.0)

    @pl.when(step == 0)
    def _():
        flow_ref[:LINES_DEV, :] = flow
        flow_ref[LINES_DEV:, :] = total

    @pl.when(step > 0)
    def _():
        flow_ref[:LINES_DEV, :] += flow
        flow_ref[LINES_DEV:, :] += total


def load_flows(ptdf, load):
    lines, buses = ptdf.shape
    return pl.pallas_call(
        load_kernel,
        grid=(buses // BLOCK,),
        in_specs=[
            pl.BlockSpec((lines, BLOCK), lambda i: (0, i)),
            pl.BlockSpec((BLOCK, 128), lambda i: (i, 0)),
        ],
        out_specs=[
            pl.BlockSpec((2 * HALF, 128), lambda i: (0, 0)),
            pl.BlockSpec((KEPT, BLOCK), lambda i: (0, i)),
        ],
        out_shape=[
            jax.ShapeDtypeStruct((2 * HALF, 128), F32),
            jax.ShapeDtypeStruct((KEPT, buses), F32),
        ],
        compiler_params=params(40),
        cost_estimate=cost_of(3 * 2 * ROWS * buses * 128, 4 * ROWS * buses),
        name="load_flows",
    )(*(pltpu.with_memory_space_constraint(x, pltpu.HBM) for x in (ptdf, load)))


def first_kernel(
    core_ref, ptdf_in, load_ref, kept_ref, unit_ref, mine_ref, other_ref, rest_ref, flow_ref, arrived
):
    rest_rows = ptdf_in.at[pl.ds(KEPT, LINES_DEV - KEPT), :]
    copy = pltpu.make_async_copy(rest_rows, rest_ref, arrived)
    copy.start()
    peers, buses = unit_ref.shape[0], ptdf_in.shape[1]
    span, units = buses // peers, 32
    lane = lax.broadcasted_iota(jnp.int32, (units, 128), 1)
    tiles = [jnp.zeros((units, 128), F32)] * (buses // 128)
    for peer in range(peers):
        spots = column(unit_ref[exchange_place(peer)][0:1, :units]).astype(jnp.int32)
        extrap = column(unit_ref[exchange_place(peer)][1:2, :units])
        for tile in range(peer * span // 128, ((peer + 1) * span - 1) // 128 + 1):
            tiles[tile] += jnp.where(lane + tile * 128 == spots, extrap, 0.0)
    injection = jnp.concatenate(
        [jnp.sum(tile, axis=0, keepdims=True) for tile in tiles], axis=1
    )
    flow_ref[:KEPT, :] = jnp.sum(kept_ref[...] * injection, axis=1, keepdims=True) - load_ref[:KEPT, :]
    total = jnp.sum(injection, axis=1, keepdims=True)
    end = row_index((2 * HALF - LINES_DEV, 128), LINES_DEV)
    flow_ref[LINES_DEV:, :] = jnp.where(end == LINES_DEV, total, 0.0) - load_ref[LINES_DEV:, :]
    copy.wait()
    rest = jnp.sum(rest_ref[...] * injection, axis=1, keepdims=True)
    flow_ref[KEPT:LINES_DEV, :] = rest - load_ref[KEPT:LINES_DEV, :]
    core = core_ref[0]
    for ref, place in ((other_ref, 1 - core), (mine_ref, core)):
        ref[...] = flow_ref[pl.ds(pl.multiple_of(place * HALF, 8), HALF), :]


def first_flows(core, ptdf, kept, unit_rows, load):
    half = jax.ShapeDtypeStruct((HALF, 128), F32)
    return pl.pallas_call(
        first_kernel,
        in_specs=[SMEM, pl.BlockSpec(memory_space=pltpu.HBM)] + [VMEM] * 3,
        out_specs=[VMEM, VMEM],
        out_shape=[half, half],
        scratch_shapes=[
            pltpu.VMEM((LINES_DEV - KEPT, ptdf.shape[1]), F32),
            pltpu.VMEM((2 * HALF, 128), F32),
            pltpu.SemaphoreType.DMA(()),
        ],
        compiler_params=params(24),
        cost_estimate=cost_of(2 * ROWS * ptdf.shape[1], 4 * ROWS * ptdf.shape[1]),
        name="first_flows",
    )(
        core,
        pltpu.with_memory_space_constraint(ptdf, pltpu.HBM),
        load,
        kept,
        unit_rows,
    )


def columns_kernel(group, ptdf_ref, unit_ref, *refs):
    high_ref, low_ref, pick_ref = refs[-3:]
    step = pl.program_id(0)
    units, span = pick_ref.shape
    peers = unit_ref.shape[0] // 2
    local = units // peers

    @pl.when(step == 0)
    def _():
        for peer in range(peers):
            spots = column(unit_ref[exchange_place(group * peers + peer)][0:1, :local]).astype(jnp.int32)
            index = lax.broadcasted_iota(jnp.int32, (local, span), 1) + group * span
            pick = jnp.where(index == spots, 1.0, 0.0).astype(BF16)
            pick_ref[peer * local : (peer + 1) * local, :] = pick

    inside = row_index((BLOCK, span), step * BLOCK) < LINES_DEV
    ptdf = jnp.where(inside, ptdf_ref[...], 0.0)
    both = dot(jnp.concatenate(halves(ptdf), axis=0), pick_ref[...], ((1,), (1,)))
    rows = row_index((BLOCK, units), step * BLOCK)
    high_ref[...] = jnp.where(rows == LINES_DEV, 1.0, both[:BLOCK]).astype(BF16)
    low_ref[...] = both[BLOCK:].astype(BF16)


def unit_columns(ptdf, unit_rows, units, *begun):
    span = ptdf.shape[1] // 2
    group = 1 if begun else 0
    by_row = pl.BlockSpec((BLOCK, units // 2), lambda i: (i, group))
    return pl.pallas_call(
        functools.partial(columns_kernel, group),
        grid=(ROWS // BLOCK,),
        in_specs=[
            pl.BlockSpec((BLOCK, span), lambda i: (i, group)),
            pl.BlockSpec(unit_rows.shape, lambda i: (0, 0, 0)),
        ]
        + [pl.BlockSpec(memory_space=pl.ANY)] * len(begun),
        out_specs=[by_row, by_row],
        out_shape=[jax.ShapeDtypeStruct((ROWS, units), BF16)] * 2,
        scratch_shapes=[pltpu.VMEM((units // 2, span), BF16)],
        input_output_aliases={2: 0, 3: 1} if begun else {},
        compiler_params=params(40),
        cost_estimate=cost_of(2 * ROWS * span * units, 4 * ROWS * span),
        name="unit_columns",
    )(pltpu.with_memory_space_constraint(ptdf, pltpu.HBM), unit_rows, *begun)


def flow_kernel(place_ref, high_ref, low_ref, extrap_ref, flow_ref):
    blocks = [extrap_ref[exchange_place(line)] for line in range(extrap_ref.shape[0])]
    high, low = halves(jnp.concatenate(blocks, axis=0))
    pair = jnp.concatenate([high, low], axis=1)
    rows = pl.ds(pl.multiple_of(place_ref[0] * HALF, 16), HALF)
    both = dot(high_ref[rows, :], pair)
    flow_ref[...] = both[:, :128] + both[:, 128:] + dot(low_ref[rows, :], high)


def unit_flows(place, high, low, extrap):
    return pl.pallas_call(
        flow_kernel,
        in_specs=[SMEM] + [VMEM] * 3,
        out_specs=VMEM,
        out_shape=jax.ShapeDtypeStruct((HALF, 128), F32),
        compiler_params=params(8),
        cost_estimate=cost_of(3 * 2 * HALF * 512 * 128, 4 * HALF * 512),
        name="unit_flows",
    )(place, high, low, extrap)


def dual_kernel(*refs):
    count = len(CHUNKS)
    lefts, rights = refs[:count], refs[count : 2 * count]
    flow_ref, dual_ref, step_ref, limit_ref, dual_out, *flow_out = refs[2 * count :]
    for chunk, ends in enumerate(CHUNKS):
        rows = slice(*ends)
        flow = flow_ref[rows, :] + (lefts[chunk][...] + rights[chunk][...])
        for ref in flow_out:
            ref[rows, :] = flow
        moved = dual_ref[rows, :] + step_ref[rows, :] * flow
        limit = limit_ref[rows, :]
        dual_out[rows, :] = moved - jnp.clip(moved, -limit, limit)


def dual_step(lefts, rights, flow, dual, steps, limits, outputs):
    half = jax.ShapeDtypeStruct((HALF, 128), F32)
    return pl.pallas_call(
        dual_kernel,
        in_specs=[VMEM] * (4 + 2 * len(lefts)),
        out_specs=[VMEM] * outputs,
        out_shape=[half] * outputs,
        compiler_params=params(8),
        name="dual_step",
    )(*lefts, *rights, flow, dual, steps, limits)


def price_kernel(place_ref, dual_ref, high_ref, low_ref, *refs):
    rows = pl.ds(pl.multiple_of(place_ref[0] * HALF, 16), HALF)
    high, low = halves(dual_ref[...].T)
    both = dot(jnp.concatenate([high, low], axis=0), high_ref[rows, :])
    price = both[:128] + both[128:] + dot(high, low_ref[rows, :])
    if len(refs) == 2:
        price = (refs[0][...] + price).T
        count, local, _ = refs[1].shape
        for line in range(count):
            refs[1][exchange_place(line)] = price[line * local : (line + 1) * local]
    else:
        refs[0][...] = price


def unit_prices(place, dual, high, low, *part):
    units = high.shape[1]
    return pl.pallas_call(
        price_kernel,
        in_specs=[SMEM] + [VMEM] * (3 + len(part)),
        out_specs=VMEM,
        out_shape=jax.ShapeDtypeStruct((16, units // 16, 128) if part else (128, units), F32),
        compiler_params=params(8),
        cost_estimate=cost_of(3 * 2 * HALF * 512 * 128, 4 * HALF * 512),
        name="unit_prices",
    )(place, dual, high, low, *part)


def placed_kernel(place_ref, half_ref, *refs):
    out_ref, arrived = refs[-2:]
    for place, count in enumerate((HALF, LINES_DEV - HALF)):

        @pl.when(place_ref[0] == place)
        def _(place=place, count=count):
            rows = out_ref.at[pl.ds(place * HALF, count), :]
            copy = pltpu.make_async_copy(half_ref.at[pl.ds(0, count), :], rows, arrived)
            copy.start()
            copy.wait()


def placed(place, half, *begun):
    anywhere = pl.BlockSpec(memory_space=pl.ANY)
    return pl.pallas_call(
        placed_kernel,
        in_specs=[SMEM, VMEM] + [anywhere] * len(begun),
        out_specs=anywhere,
        out_shape=jax.ShapeDtypeStruct((LINES_DEV, 128), F32),
        scratch_shapes=[pltpu.SemaphoreType.DMA(())],
        input_output_aliases={2: 0} if begun else {},
        compiler_params=params(8),
        cost_estimate=cost_of(0, 8 * HALF * 128),
        name="placed",
    )(place, half, *begun)


def unit_kernel(price_ref, gen_ref, old_ref, state_ref, table_ref, extrap_ref, copies_ref, *gen_out):
    cost = table_ref[:, 0:1]
    lower = table_ref[:, 1:2]
    upper = table_ref[:, 2:3]
    gen = gen_ref[...]
    gradient = cost + jnp.sum(price_ref[...], axis=0) + state_ref[...]
    updated = jnp.clip(gen - PRIMAL_STEP * gradient, lower, upper)
    extrap = 2.0 * updated - gen
    for ref in gen_out:
        ref[...] = updated
    extrap_ref[...] = extrap
    copies_ref[...] = jnp.broadcast_to((extrap - old_ref[...])[None], copies_ref.shape)


def unit_step(prices, gen, old, state, table, last):
    one = jax.ShapeDtypeStruct(gen.shape, F32)
    shapes = [one, jax.ShapeDtypeStruct(prices.shape, F32)] + ([] if last else [one])
    return pl.pallas_call(
        unit_kernel,
        in_specs=[VMEM] * 5,
        out_specs=[VMEM] * len(shapes),
        out_shape=shapes,
        compiler_params=params(8),
        name="unit_step",
    )(prices, gen, old, state, table)


def state_kernel(place_ref, own_ref, far_ref, ramp_ref, store_ref, table_ref, state_ref, *kept):
    ramp_limit = DUAL_STEP * table_ref[:, 3:4]
    storage = table_ref[:, 4:5]
    store_limit = DUAL_STEP * table_ref[:, 5:6]
    first = place_ref[0] == 0
    own, far = own_ref[...], far_ref[...]
    extrap = jnp.concatenate([jnp.where(first, own, far), jnp.where(first, far, own)], axis=1)
    hour = lax.broadcasted_iota(jnp.int32, extrap.shape, 1)
    hours = extrap.shape[1]
    previous = pltpu.roll(extrap, 1, 1)
    moved = ramp_ref[...] + jnp.where(hour >= 1, DUAL_STEP * (extrap - previous), 0.0)
    ramp = moved - jnp.clip(moved, -ramp_limit, ramp_limit)
    early = lax.broadcasted_iota(jnp.int32, (hours, hours), 0)
    late = lax.broadcasted_iota(jnp.int32, (hours, hours), 1)
    forward = jnp.where(early <= late, 1.0, 0.0)
    backward = jnp.where(early >= late, 1.0, 0.0)
    running = jnp.dot(extrap, forward, precision=lax.Precision.HIGHEST, preferred_element_type=F32)
    moved = store_ref[...] + DUAL_STEP * storage * running
    store = moved - jnp.clip(moved, -store_limit, store_limit)
    for ref, value in zip(kept, (ramp, store)):
        ref[...] = value
    suffix = jnp.dot(store, backward, precision=lax.Precision.HIGHEST, preferred_element_type=F32)
    after = jnp.where(hour < hours - 1, pltpu.roll(ramp, hours - 1, 1), 0.0)
    state = ramp - after + storage * suffix
    state_ref[...] = jnp.where(first, state[:, :128], state[:, 128:])


def state_step(place, own, far, ramp, store, table, last):
    wide = jax.ShapeDtypeStruct(ramp.shape, F32)
    shapes = [jax.ShapeDtypeStruct(own.shape, F32)] + ([] if last else [wide, wide])
    return pl.pallas_call(
        state_kernel,
        in_specs=[SMEM] + [VMEM] * 5,
        out_specs=[VMEM] * len(shapes),
        out_shape=shapes,
        compiler_params=params(8),
        cost_estimate=cost_of(12 * 2 * 32 * 256 * 256, 1 << 18),
        name="state_step",
    )(place, own, far, ramp, store, table)


SWAP = ((0, 1), (1, 0))
NEAR = ((0, 1), (1, 0), (2, 3), (3, 2))
FAR = ((1, 2), (2, 1), (3, 0), (0, 3))


def along_y(value, by_core):
    pairs = [(2 * i + core, 2 * j + core) for core in range(2) for i, j in by_core[core]]
    return lax.ppermute(value, BUS, pairs)


def on_device(ptdf, bus_load, unit_bus, unit_type, unit_limit, unit_cost, line_rating):
    line_count = lax.axis_size(LINE)
    hour_dev = bus_load.shape[1]
    local = unit_bus.shape[0]
    core = lax.axis_index("c").astype(jnp.int32)
    place = lax.axis_index("t").astype(jnp.int32)[None]
    block = (lax.axis_index(BUS) * ptdf.shape[1]).astype(jnp.int32)
    table, gen, copies = unit_tables(
        block[None], unit_bus, unit_type, unit_limit, unit_cost, line_count
    )
    unit_rows = lax.all_to_all(copies, EXCHANGE, 0, 0, tiled=True)
    load, kept = load_flows(ptdf, bus_load)
    mine, other = first_flows(core[None], ptdf, kept, unit_rows, load)
    extrap = far = 2.0 * gen

    pad = jnp.zeros((2 * HALF - LINES_DEV,), F32)
    limits = jnp.concatenate([DUAL_STEP * (line_rating.astype(F32) / 100.0), pad])
    index = core * HALF + jnp.arange(HALF, dtype=jnp.int32)
    weight = 1.0 / (UNITS * 16)
    steps = jnp.where(index < LINES_DEV, DUAL_STEP, jnp.where(index == LINES_DEV, weight, 0.0))
    steps = steps.astype(F32)[:, None]
    limits = lax.dynamic_slice_in_dim(limits, core * HALF, HALF, 0)[:, None]
    core, partner = core[None], 1 - core[None]
    flow = dual = jnp.zeros((HALF, hour_dev), F32)
    ramp = store = jnp.zeros((local, 2 * hour_dev), F32)
    high = low = None
    for iteration in range(ITERS):
        last = iteration == ITERS - 1
        got = lax.ppermute(other, "c", SWAP)
        if iteration == 0:
            state, ramp, store = state_step(place, extrap, far, ramp, store, table, False)
            total, tied, rows, state = lax.optimization_barrier(
                (mine + got, ptdf, unit_rows, state)
            )
            lefts = [total[start:stop] for start, stop in CHUNKS]
            high, low = unit_columns(tied, rows, line_count * local)
        elif last:
            total = mine + got
            lefts = [total[start:stop] for start, stop in CHUNKS]
        else:
            lefts = [mine[start:stop] + got[start:stop] for start, stop in CHUNKS]
        if 0 < iteration < ITERS - 1:
            lefts[0], tied = lax.optimization_barrier((lefts[0], extrap))
            far = lax.ppermute(tied, "t", SWAP)
        lefts = [left + along_y(left, (NEAR, FAR)) for left in lefts]
        if iteration == 0:
            lefts[0], high, low = lax.optimization_barrier((lefts[0], high, low))
            high, low = unit_columns(tied, rows, line_count * local, high, low)
        elif not last:
            lefts[0], far = lax.optimization_barrier((lefts[0], far))
        if 0 < iteration < ITERS - 1:
            state, *kept = state_step(place, extrap, far, ramp, store, table, iteration == ITERS - 2)
            ramp, store = kept if kept else (None, None)
        rights = [along_y(left, (FAR, NEAR)) for left in lefts]
        if iteration == 0:
            rights[-1], high, low = lax.optimization_barrier((rights[-1], high, low))
        if last:
            rights[-1], gen = lax.optimization_barrier((rights[-1], 0.5 * (extrap + before)))
            (dual,) = dual_step(lefts, rights, flow, dual, steps, limits, 1)
            result = placed(core, dual)
            return gen, placed(partner, lax.ppermute(dual, "c", SWAP), result)
        rights[-1], state, ramp, store = lax.optimization_barrier((rights[-1], state, ramp, store))
        dual, flow = dual_step(lefts, rights, flow, dual, steps, limits, 2)
        prices = unit_prices(core, dual, high, low)
        prices = unit_prices(partner, lax.ppermute(dual, "c", SWAP), high, low, prices)
        prices = lax.all_to_all(prices, EXCHANGE, 0, 0, tiled=True)
        before = gen
        extrap, copies, *updated = unit_step(
            prices, gen, extrap, state, table, iteration == ITERS - 2
        )
        gen = updated[0] if updated else None
        changes = lax.all_to_all(copies, EXCHANGE, 0, 0, tiled=True)
        other = unit_flows(partner, high, low, changes)
        mine = unit_flows(core, high, low, changes)


def solution(mesh):
    finer = Mesh(
        mesh.devices.reshape(8, 2, 4, 2, mesh.shape["tm"]),
        ("z", "xl", "y", "c", "t"),
    )
    return jax.shard_map(
        on_device,
        mesh=finer,
        in_specs=(
            P(LINE, BUS),
            P(BUS, "t"),
            P(LINE_BUS),
            P(LINE_BUS),
            P(LINE_BUS),
            P(LINE_BUS),
            P(LINE),
        ),
        out_specs=(P(LINE_BUS, "t"), P(LINE, "t")),
        check_vma=False,
    )
```

```python
import functools

import jax
import jax.numpy as jnp
from jax import lax
from jax.experimental import pallas as pl
from jax.experimental.pallas import tpu as pltpu
from jax.sharding import Mesh
from jax.sharding import PartitionSpec as P

UNITS = 4096
ITERS = 4
LINE = ("z", "xl")
EXCHANGE = ("xl", "z")
BUS = ("y", "c")
LINE_BUS = ("z", "xl", "y", "c")

RAMP_RATES = (0.1, 0.2, 0.4, 0.5)
COST_FACTORS = (1.0, 1.5, 3.0, 0.05)
PRIMAL_STEP = 0.5
DUAL_STEP = 0.5

LINES_DEV = 960
ROWS = 1024
HALF = 496
BLOCK = 512
KEPT = 320
CHUNKS = ((0, 240), (240, HALF))
BF16 = jnp.bfloat16
F32 = jnp.float32
VMEM = pl.BlockSpec(memory_space=pltpu.VMEM)
SMEM = pl.BlockSpec(memory_space=pltpu.SMEM)


def params(mib):
    return pltpu.CompilerParams(vmem_limit_bytes=mib << 20)


def cost_of(flops, size):
    return pl.CostEstimate(flops=flops, bytes_accessed=size, transcendentals=0)


def halves(value):
    high = value.astype(BF16)
    return high, (value - high.astype(F32)).astype(BF16)


def dot(left, right, dims=((1,), (0,))):
    return lax.dot_general(left, right, (dims, ((), ())), preferred_element_type=F32)


def exchange_place(line):
    return line % 2 * 8 + line // 2


def row_index(shape, first):
    return first + lax.broadcasted_iota(jnp.int32, shape, 0)


def picked(kinds, values):
    total = 0.0
    for kind, value in enumerate(values):
        total = total + jnp.where(kinds == kind, value, 0.0)
    return total


def column(row):
    count = row.shape[1]
    same = lax.broadcasted_iota(jnp.int32, (count, count), 0) == lax.broadcasted_iota(
        jnp.int32, (count, count), 1
    )
    return jnp.sum(jnp.where(same, row, jnp.zeros_like(row)), axis=1, keepdims=True)


def table_kernel(
    place_ref, bus_in, type_in, limit_in, cost_in, table_ref, first_ref, copies_ref,
    bus_ref, type_ref, limit_ref, cost_ref, send_ref, rows_ref, arrived
):
    pairs = (
        (bus_in, bus_ref.at[0]),
        (type_in, type_ref.at[0]),
        (limit_in, limit_ref.at[0]),
        (cost_in, cost_ref.at[0]),
    )
    copies = [pltpu.make_async_copy(*pair, arrived.at[spot]) for spot, pair in enumerate(pairs)]
    for copy in copies:
        copy.start()
    for copy in copies:
        copy.wait()
    kinds = type_ref[...]
    capacity = limit_ref[...].astype(F32) / 100.0
    cost = cost_ref[...] * picked(kinds, COST_FACTORS)
    storage = jnp.where(kinds == 3, 1.0, 0.0)
    lower = -capacity * storage
    first = jnp.clip(-PRIMAL_STEP * cost, lower, capacity)
    ramp = picked(kinds, RAMP_RATES) * capacity
    units = kinds.shape[1]
    send_ref[...] = jnp.zeros(send_ref.shape, F32)
    send_ref[0:1, :units] = (bus_ref[...] - place_ref[0]).astype(F32)
    send_ref[1:2, :units] = 2.0 * first
    copies_ref[...] = jnp.broadcast_to(send_ref[...][None], copies_ref.shape)
    rows_ref[...] = jnp.zeros(rows_ref.shape, F32)
    for spot, part in enumerate((cost, lower, capacity, ramp, storage, 2.0 * capacity, first)):
        rows_ref[spot : spot + 1, :units] = part
    table = rows_ref[...].T[:units]
    table_ref[...] = table
    first_ref[...] = jnp.broadcast_to(table[:, 6:7], first_ref.shape)


def unit_tables(place, unit_bus, unit_type, unit_limit, unit_cost, line_count):
    units = unit_bus.shape[0]
    rows = (unit_bus, unit_type, unit_limit, unit_cost)
    one = jax.ShapeDtypeStruct((units, 128), F32)
    return pl.pallas_call(
        table_kernel,
        in_specs=[SMEM] + [pl.BlockSpec(memory_space=pltpu.HBM)] * 4,
        out_specs=[VMEM] * 3,
        out_shape=[
            one,
            one,
            jax.ShapeDtypeStruct((line_count, 8, 128), F32),
        ],
        scratch_shapes=[pltpu.VMEM((1, units), row.dtype) for row in rows]
        + [pltpu.VMEM((8, 128), F32), pltpu.VMEM((128, 128), F32), pltpu.SemaphoreType.DMA((4,))],
        compiler_params=params(16),
        name="unit_tables",
    )(place, *(pltpu.with_memory_space_constraint(x, pltpu.HBM) for x in rows))


def load_kernel(ptdf_ref, load_ref, flow_ref, kept_ref):
    step = pl.program_id(0)
    ptdf, load = ptdf_ref[...], load_ref[...]
    kept_ref[...] = ptdf[:KEPT]
    high, low = halves(load)
    ptdf_high, ptdf_low = halves(ptdf)
    both = dot(ptdf_high, jnp.concatenate([high, low], axis=1))
    flow = both[:, :128] + both[:, 128:] + dot(ptdf_low, high)
    total = jnp.sum(load, axis=0, keepdims=True)
    end = row_index((2 * HALF - LINES_DEV, 128), LINES_DEV) == LINES_DEV
    total = jnp.where(end, total, 0.0)

    @pl.when(step == 0)
    def _():
        flow_ref[:LINES_DEV, :] = flow
        flow_ref[LINES_DEV:, :] = total

    @pl.when(step > 0)
    def _():
        flow_ref[:LINES_DEV, :] += flow
        flow_ref[LINES_DEV:, :] += total


def load_flows(ptdf, load):
    lines, buses = ptdf.shape
    return pl.pallas_call(
        load_kernel,
        grid=(buses // BLOCK,),
        in_specs=[
            pl.BlockSpec((lines, BLOCK), lambda i: (0, i)),
            pl.BlockSpec((BLOCK, 128), lambda i: (i, 0)),
        ],
        out_specs=[
            pl.BlockSpec((2 * HALF, 128), lambda i: (0, 0)),
            pl.BlockSpec((KEPT, BLOCK), lambda i: (0, i)),
        ],
        out_shape=[
            jax.ShapeDtypeStruct((2 * HALF, 128), F32),
            jax.ShapeDtypeStruct((KEPT, buses), F32),
        ],
        compiler_params=params(40),
        cost_estimate=cost_of(3 * 2 * ROWS * buses * 128, 4 * ROWS * buses),
        name="load_flows",
    )(*(pltpu.with_memory_space_constraint(x, pltpu.HBM) for x in (ptdf, load)))


def first_kernel(
    core_ref, ptdf_in, load_ref, kept_ref, unit_ref, mine_ref, other_ref, rest_ref, flow_ref, arrived
):
    rest_rows = ptdf_in.at[pl.ds(KEPT, LINES_DEV - KEPT), :]
    copy = pltpu.make_async_copy(rest_rows, rest_ref, arrived)
    copy.start()
    peers, buses = unit_ref.shape[0], ptdf_in.shape[1]
    span, units = buses // peers, 32
    lane = lax.broadcasted_iota(jnp.int32, (units, 128), 1)
    tiles = [jnp.zeros((units, 128), F32)] * (buses // 128)
    for peer in range(peers):
        spots = column(unit_ref[exchange_place(peer)][0:1, :units]).astype(jnp.int32)
        extrap = column(unit_ref[exchange_place(peer)][1:2, :units])
        for tile in range(peer * span // 128, ((peer + 1) * span - 1) // 128 + 1):
            tiles[tile] += jnp.where(lane + tile * 128 == spots, extrap, 0.0)
    injection = jnp.concatenate(
        [jnp.sum(tile, axis=0, keepdims=True) for tile in tiles], axis=1
    )
    flow_ref[:KEPT, :] = jnp.sum(kept_ref[...] * injection, axis=1, keepdims=True) - load_ref[:KEPT, :]
    total = jnp.sum(injection, axis=1, keepdims=True)
    end = row_index((2 * HALF - LINES_DEV, 128), LINES_DEV)
    flow_ref[LINES_DEV:, :] = jnp.where(end == LINES_DEV, total, 0.0) - load_ref[LINES_DEV:, :]
    copy.wait()
    rest = jnp.sum(rest_ref[...] * injection, axis=1, keepdims=True)
    flow_ref[KEPT:LINES_DEV, :] = rest - load_ref[KEPT:LINES_DEV, :]
    core = core_ref[0]
    for ref, place in ((other_ref, 1 - core), (mine_ref, core)):
        ref[...] = flow_ref[pl.ds(pl.multiple_of(place * HALF, 8), HALF), :]


def first_flows(core, ptdf, kept, unit_rows, load):
    half = jax.ShapeDtypeStruct((HALF, 128), F32)
    return pl.pallas_call(
        first_kernel,
        in_specs=[SMEM, pl.BlockSpec(memory_space=pltpu.HBM)] + [VMEM] * 3,
        out_specs=[VMEM, VMEM],
        out_shape=[half, half],
        scratch_shapes=[
            pltpu.VMEM((LINES_DEV - KEPT, ptdf.shape[1]), F32),
            pltpu.VMEM((2 * HALF, 128), F32),
            pltpu.SemaphoreType.DMA(()),
        ],
        compiler_params=params(24),
        cost_estimate=cost_of(2 * ROWS * ptdf.shape[1], 4 * ROWS * ptdf.shape[1]),
        name="first_flows",
    )(
        core,
        pltpu.with_memory_space_constraint(ptdf, pltpu.HBM),
        load,
        kept,
        unit_rows,
    )


def columns_kernel(group, ptdf_ref, unit_ref, *refs):
    high_ref, low_ref, pick_ref = refs[-3:]
    step = pl.program_id(0)
    units, span = pick_ref.shape
    peers = unit_ref.shape[0] // 2
    local = units // peers

    @pl.when(step == 0)
    def _():
        for peer in range(peers):
            spots = column(unit_ref[exchange_place(group * peers + peer)][0:1, :local]).astype(jnp.int32)
            index = lax.broadcasted_iota(jnp.int32, (local, span), 1) + group * span
            pick = jnp.where(index == spots, 1.0, 0.0).astype(BF16)
            pick_ref[peer * local : (peer + 1) * local, :] = pick

    inside = row_index((BLOCK, span), step * BLOCK) < LINES_DEV
    ptdf = jnp.where(inside, ptdf_ref[...], 0.0)
    both = dot(jnp.concatenate(halves(ptdf), axis=0), pick_ref[...], ((1,), (1,)))
    rows = row_index((BLOCK, units), step * BLOCK)
    high_ref[...] = jnp.where(rows == LINES_DEV, 1.0, both[:BLOCK]).astype(BF16)
    low_ref[...] = both[BLOCK:].astype(BF16)


def unit_columns(ptdf, unit_rows, units, *begun):
    span = ptdf.shape[1] // 2
    group = 1 if begun else 0
    by_row = pl.BlockSpec((BLOCK, units // 2), lambda i: (i, group))
    return pl.pallas_call(
        functools.partial(columns_kernel, group),
        grid=(ROWS // BLOCK,),
        in_specs=[
            pl.BlockSpec((BLOCK, span), lambda i: (i, group)),
            pl.BlockSpec(unit_rows.shape, lambda i: (0, 0, 0)),
        ]
        + [pl.BlockSpec(memory_space=pl.ANY)] * len(begun),
        out_specs=[by_row, by_row],
        out_shape=[jax.ShapeDtypeStruct((ROWS, units), BF16)] * 2,
        scratch_shapes=[pltpu.VMEM((units // 2, span), BF16)],
        input_output_aliases={2: 0, 3: 1} if begun else {},
        compiler_params=params(40),
        cost_estimate=cost_of(2 * ROWS * span * units, 4 * ROWS * span),
        name="unit_columns",
    )(pltpu.with_memory_space_constraint(ptdf, pltpu.HBM), unit_rows, *begun)


def flow_kernel(place_ref, high_ref, low_ref, extrap_ref, flow_ref):
    blocks = [extrap_ref[exchange_place(line)] for line in range(extrap_ref.shape[0])]
    high, low = halves(jnp.concatenate(blocks, axis=0))
    pair = jnp.concatenate([high, low], axis=1)
    rows = pl.ds(pl.multiple_of(place_ref[0] * HALF, 16), HALF)
    both = dot(high_ref[rows, :], pair)
    flow_ref[...] = both[:, :128] + both[:, 128:] + dot(low_ref[rows, :], high)


def unit_flows(place, high, low, extrap):
    return pl.pallas_call(
        flow_kernel,
        in_specs=[SMEM] + [VMEM] * 3,
        out_specs=VMEM,
        out_shape=jax.ShapeDtypeStruct((HALF, 128), F32),
        compiler_params=params(8),
        cost_estimate=cost_of(3 * 2 * HALF * 512 * 128, 4 * HALF * 512),
        name="unit_flows",
    )(place, high, low, extrap)


def dual_kernel(*refs):
    count = len(CHUNKS)
    lefts, rights = refs[:count], refs[count : 2 * count]
    flow_ref, dual_ref, step_ref, limit_ref, dual_out, *flow_out = refs[2 * count :]
    for chunk, ends in enumerate(CHUNKS):
        rows = slice(*ends)
        flow = flow_ref[rows, :] + (lefts[chunk][...] + rights[chunk][...])
        for ref in flow_out:
            ref[rows, :] = flow
        moved = dual_ref[rows, :] + step_ref[rows, :] * flow
        limit = limit_ref[rows, :]
        dual_out[rows, :] = moved - jnp.clip(moved, -limit, limit)


def dual_step(lefts, rights, flow, dual, steps, limits, outputs):
    half = jax.ShapeDtypeStruct((HALF, 128), F32)
    return pl.pallas_call(
        dual_kernel,
        in_specs=[VMEM] * (4 + 2 * len(lefts)),
        out_specs=[VMEM] * outputs,
        out_shape=[half] * outputs,
        compiler_params=params(8),
        name="dual_step",
    )(*lefts, *rights, flow, dual, steps, limits)


def price_kernel(place_ref, dual_ref, high_ref, low_ref, *refs):
    rows = pl.ds(pl.multiple_of(place_ref[0] * HALF, 16), HALF)
    high, low = halves(dual_ref[...].T)
    both = dot(jnp.concatenate([high, low], axis=0), high_ref[rows, :])
    price = both[:128] + both[128:] + dot(high, low_ref[rows, :])
    if len(refs) == 2:
        price = (refs[0][...] + price).T
        count, local, _ = refs[1].shape
        for line in range(count):
            refs[1][exchange_place(line)] = price[line * local : (line + 1) * local]
    else:
        refs[0][...] = price


def unit_prices(place, dual, high, low, *part):
    units = high.shape[1]
    return pl.pallas_call(
        price_kernel,
        in_specs=[SMEM] + [VMEM] * (3 + len(part)),
        out_specs=VMEM,
        out_shape=jax.ShapeDtypeStruct((16, units // 16, 128) if part else (128, units), F32),
        compiler_params=params(8),
        cost_estimate=cost_of(3 * 2 * HALF * 512 * 128, 4 * HALF * 512),
        name="unit_prices",
    )(place, dual, high, low, *part)


def placed_kernel(place_ref, half_ref, *refs):
    out_ref, arrived = refs[-2:]
    for place, count in enumerate((HALF, LINES_DEV - HALF)):

        @pl.when(place_ref[0] == place)
        def _(place=place, count=count):
            rows = out_ref.at[pl.ds(place * HALF, count), :]
            copy = pltpu.make_async_copy(half_ref.at[pl.ds(0, count), :], rows, arrived)
            copy.start()
            copy.wait()


def placed(place, half, *begun):
    anywhere = pl.BlockSpec(memory_space=pl.ANY)
    return pl.pallas_call(
        placed_kernel,
        in_specs=[SMEM, VMEM] + [anywhere] * len(begun),
        out_specs=anywhere,
        out_shape=jax.ShapeDtypeStruct((LINES_DEV, 128), F32),
        scratch_shapes=[pltpu.SemaphoreType.DMA(())],
        input_output_aliases={2: 0} if begun else {},
        compiler_params=params(8),
        cost_estimate=cost_of(0, 8 * HALF * 128),
        name="placed",
    )(place, half, *begun)


def unit_kernel(price_ref, gen_ref, old_ref, state_ref, table_ref, extrap_ref, copies_ref, *gen_out):
    cost = table_ref[:, 0:1]
    lower = table_ref[:, 1:2]
    upper = table_ref[:, 2:3]
    gen = gen_ref[...]
    gradient = cost + jnp.sum(price_ref[...], axis=0) + state_ref[...]
    updated = jnp.clip(gen - PRIMAL_STEP * gradient, lower, upper)
    extrap = 2.0 * updated - gen
    for ref in gen_out:
        ref[...] = updated
    extrap_ref[...] = extrap
    copies_ref[...] = jnp.broadcast_to((extrap - old_ref[...])[None], copies_ref.shape)


def unit_step(prices, gen, old, state, table, last):
    one = jax.ShapeDtypeStruct(gen.shape, F32)
    shapes = [one, jax.ShapeDtypeStruct(prices.shape, F32)] + ([] if last else [one])
    return pl.pallas_call(
        unit_kernel,
        in_specs=[VMEM] * 5,
        out_specs=[VMEM] * len(shapes),
        out_shape=shapes,
        compiler_params=params(8),
        name="unit_step",
    )(prices, gen, old, state, table)


def state_kernel(place_ref, own_ref, far_ref, ramp_ref, store_ref, table_ref, state_ref, *kept):
    ramp_limit = DUAL_STEP * table_ref[:, 3:4]
    storage = table_ref[:, 4:5]
    store_limit = DUAL_STEP * table_ref[:, 5:6]
    first = place_ref[0] == 0
    own, far = own_ref[...], far_ref[...]
    extrap = jnp.concatenate([jnp.where(first, own, far), jnp.where(first, far, own)], axis=1)
    hour = lax.broadcasted_iota(jnp.int32, extrap.shape, 1)
    hours = extrap.shape[1]
    previous = pltpu.roll(extrap, 1, 1)
    moved = ramp_ref[...] + jnp.where(hour >= 1, DUAL_STEP * (extrap - previous), 0.0)
    ramp = moved - jnp.clip(moved, -ramp_limit, ramp_limit)
    early = lax.broadcasted_iota(jnp.int32, (hours, hours), 0)
    late = lax.broadcasted_iota(jnp.int32, (hours, hours), 1)
    forward = jnp.where(early <= late, 1.0, 0.0)
    backward = jnp.where(early >= late, 1.0, 0.0)
    running = jnp.dot(extrap, forward, precision=lax.Precision.HIGHEST, preferred_element_type=F32)
    moved = store_ref[...] + DUAL_STEP * storage * running
    store = moved - jnp.clip(moved, -store_limit, store_limit)
    for ref, value in zip(kept, (ramp, store)):
        ref[...] = value
    suffix = jnp.dot(store, backward, precision=lax.Precision.HIGHEST, preferred_element_type=F32)
    after = jnp.where(hour < hours - 1, pltpu.roll(ramp, hours - 1, 1), 0.0)
    state = ramp - after + storage * suffix
    state_ref[...] = jnp.where(first, state[:, :128], state[:, 128:])


def state_step(place, own, far, ramp, store, table, last):
    wide = jax.ShapeDtypeStruct(ramp.shape, F32)
    shapes = [jax.ShapeDtypeStruct(own.shape, F32)] + ([] if last else [wide, wide])
    return pl.pallas_call(
        state_kernel,
        in_specs=[SMEM] + [VMEM] * 5,
        out_specs=[VMEM] * len(shapes),
        out_shape=shapes,
        compiler_params=params(8),
        cost_estimate=cost_of(12 * 2 * 32 * 256 * 256, 1 << 18),
        name="state_step",
    )(place, own, far, ramp, store, table)


SWAP = ((0, 1), (1, 0))
NEAR = ((0, 1), (1, 0), (2, 3), (3, 2))
FAR = ((1, 2), (2, 1), (3, 0), (0, 3))


def along_y(value, by_core):
    pairs = [(2 * i + core, 2 * j + core) for core in range(2) for i, j in by_core[core]]
    return lax.ppermute(value, BUS, pairs)


def on_device(ptdf, bus_load, unit_bus, unit_type, unit_limit, unit_cost, line_rating):
    line_count = lax.axis_size(LINE)
    hour_dev = bus_load.shape[1]
    local = unit_bus.shape[0]
    core = lax.axis_index("c").astype(jnp.int32)
    place = lax.axis_index("t").astype(jnp.int32)[None]
    block = (lax.axis_index(BUS) * ptdf.shape[1]).astype(jnp.int32)
    table, gen, copies = unit_tables(
        block[None], unit_bus, unit_type, unit_limit, unit_cost, line_count
    )
    unit_rows = lax.all_to_all(copies, EXCHANGE, 0, 0, tiled=True)
    load, kept = load_flows(ptdf, bus_load)
    mine, other = first_flows(core[None], ptdf, kept, unit_rows, load)
    extrap = far = 2.0 * gen

    pad = jnp.zeros((2 * HALF - LINES_DEV,), F32)
    limits = jnp.concatenate([DUAL_STEP * (line_rating.astype(F32) / 100.0), pad])
    index = core * HALF + jnp.arange(HALF, dtype=jnp.int32)
    weight = 1.0 / (UNITS * 16)
    steps = jnp.where(index < LINES_DEV, DUAL_STEP, jnp.where(index == LINES_DEV, weight, 0.0))
    steps = steps.astype(F32)[:, None]
    limits = lax.dynamic_slice_in_dim(limits, core * HALF, HALF, 0)[:, None]
    core, partner = core[None], 1 - core[None]
    flow = dual = jnp.zeros((HALF, hour_dev), F32)
    ramp = store = jnp.zeros((local, 2 * hour_dev), F32)
    high = low = None
    for iteration in range(ITERS):
        last = iteration == ITERS - 1
        got = lax.ppermute(other, "c", SWAP)
        if iteration == 0:
            state, ramp, store = state_step(place, extrap, far, ramp, store, table, False)
            total, tied, rows, state = lax.optimization_barrier(
                (mine + got, ptdf, unit_rows, state)
            )
            lefts = [total[start:stop] for start, stop in CHUNKS]
            high, low = unit_columns(tied, rows, line_count * local)
        elif last:
            total = mine + got
            lefts = [total[start:stop] for start, stop in CHUNKS]
        else:
            lefts = [mine[start:stop] + got[start:stop] for start, stop in CHUNKS]
        if 0 < iteration < ITERS - 1:
            lefts[0], tied = lax.optimization_barrier((lefts[0], extrap))
            far = lax.ppermute(tied, "t", SWAP)
        lefts = [left + along_y(left, (NEAR, FAR)) for left in lefts]
        if iteration == 0:
            lefts[0], high, low = lax.optimization_barrier((lefts[0], high, low))
            high, low = unit_columns(tied, rows, line_count * local, high, low)
        elif not last:
            lefts[0], far = lax.optimization_barrier((lefts[0], far))
        if 0 < iteration < ITERS - 1:
            state, *kept = state_step(place, extrap, far, ramp, store, table, iteration == ITERS - 2)
            ramp, store = kept if kept else (None, None)
        rights = [along_y(left, (FAR, NEAR)) for left in lefts]
        if iteration == 0:
            rights[-1], high, low = lax.optimization_barrier((rights[-1], high, low))
        if last:
            rights[-1], gen = lax.optimization_barrier((rights[-1], 0.5 * (extrap + before)))
            (dual,) = dual_step(lefts, rights, flow, dual, steps, limits, 1)
            result = placed(core, dual)
            return gen, placed(partner, lax.ppermute(dual, "c", SWAP), result)
        rights[-1], state, ramp, store = lax.optimization_barrier((rights[-1], state, ramp, store))
        dual, flow = dual_step(lefts, rights, flow, dual, steps, limits, 2)
        prices = unit_prices(core, dual, high, low)
        prices = unit_prices(partner, lax.ppermute(dual, "c", SWAP), high, low, prices)
        prices = lax.all_to_all(prices, EXCHANGE, 0, 0, tiled=True)
        before = gen
        extrap, copies, *updated = unit_step(
            prices, gen, extrap, state, table, iteration == ITERS - 2
        )
        gen = updated[0] if updated else None
        changes = lax.all_to_all(copies, EXCHANGE, 0, 0, tiled=True)
        other = unit_flows(partner, high, low, changes)
        mine = unit_flows(core, high, low, changes)


def solution(mesh):
    finer = Mesh(
        mesh.devices.reshape(8, 2, 4, 2, mesh.shape["tm"]),
        ("z", "xl", "y", "c", "t"),
    )
    return jax.shard_map(
        on_device,
        mesh=finer,
        in_specs=(
            P(LINE, BUS),
            P(BUS, "t"),
            P(LINE_BUS),
            P(LINE_BUS),
            P(LINE_BUS),
            P(LINE_BUS),
            P(LINE),
        ),
        out_specs=(P(LINE_BUS, "t"), P(LINE, "t")),
        check_vma=False,
    )
```
